32 devices in a mesh: enc: 2 (over core), dp: 16 (over z, y, x).
Axes of the slice: x: 2, y: 2, z: 4, core: 2. Of those that a mesh axis runs over, the one named last changes fastest.
Arguments:
- text_in: bfloat16 [16384, 768], P(('enc', 'dp')), may hold values from -6 to 6
- text_lengths: int32 [32, 5], P(('enc', 'dp')), may hold values from 1 to 256, 512 in all within a row
- region_feats: bfloat16 [4096, 2048], P(('enc', 'dp')), may hold values from -6 to 6
- region_boxes: float32 [4, 4096], P(None, ('enc', 'dp')), may hold values from 0 to 1
- region_dest: int32 [4096, 1], P(('enc', 'dp')), may hold values from 0 to 15; in each aligned block of 128 rows (0 to 127, 128 to 255, ...) at most 16 rows name the same one
- region_seq: int32 [4096], P(('enc', 'dp')), may hold values from 0 to 4
- w_region: bfloat16 [2048, 768], replicated, may hold values from -0.125 to 0.125
- w_box: float32 [4, 768], replicated, may hold values from -3 to 3
- type_embed: float32 [768], replicated, may hold values from -3 to 3
- region_gain: float32 [768], replicated, may hold values from 0.5 to 1.5
- region_shift: float32 [768], replicated, may hold values from -1.2 to 1.2
- w_qkv: bfloat16 [768, 2304], replicated, may hold values from -0.21875 to 0.21875
- q_bias: float32 [768], replicated, may hold values from -3 to 3
- v_bias: float32 [768], replicated, may hold values from -1.8 to 1.8
- w_out: bfloat16 [768, 768], replicated, may hold values from -0.875 to 0.875
- out_bias: float32 [768], replicated, may hold values from -1.2 to 1.2
- attn_gain: float32 [768], replicated, may hold values from 0.5 to 1.5
- attn_shift: float32 [768], replicated, may hold values from -1.2 to 1.2
- w_up: bfloat16 [768, 3072], replicated, may hold values from -0.21875 to 0.21875
- up_bias: float32 [3072], replicated, may hold values from -1.8 to 1.8
- w_down: bfloat16 [3072, 768], replicated, may hold values from -0.109375 to 0.109375
- down_bias: float32 [768], replicated, may hold values from -1.2 to 1.2
- ffn_gain: float32 [768], replicated, may hold values from 0.5 to 1.5
- ffn_shift: float32 [768], replicated, may hold values from -1.2 to 1.2
- cot_text: bfloat16 [16384, 768], P(('enc', 'dp')), may hold values from -6 to 6
- cot_region: bfloat16 [4096, 768], P(('enc', 'dp')), may hold values from -6 to 6
Outputs:
- text_out: bfloat16 [16384, 768], P(('enc', 'dp'))
- region_out: bfloat16 [4096, 768], P(('enc', 'dp'))
- text_grad: bfloat16 [16384, 768], P(('enc', 'dp'))
- feats_grad: bfloat16 [4096, 2048], P(('enc', 'dp'))
- w_region_grad: float32 [2048, 768], P(None, ('enc', 'dp'))
- w_box_grad: float32 [4, 768], P(None, ('enc', 'dp'))
- type_grad: float32 [768], P(('enc', 'dp'))
- region_gain_grad: float32 [768], P(('enc', 'dp'))
- region_shift_grad: float32 [768], P(('enc', 'dp'))
- w_qkv_grad: float32 [768, 2304], P(('enc', 'dp'))
- q_bias_grad: float32 [768], P(('enc', 'dp'))
- v_bias_grad: float32 [768], P(('enc', 'dp'))
- w_out_grad: float32 [768, 768], P(('enc', 'dp'))
- out_bias_grad: float32 [768], P(('enc', 'dp'))
- attn_gain_grad: float32 [768], P(('enc', 'dp'))
- attn_shift_grad: float32 [768], P(('enc', 'dp'))
- w_up_grad: float32 [768, 3072], P(('enc', 'dp'))
- up_bias_grad: float32 [3072], P(('enc', 'dp'))
- w_down_grad: float32 [3072, 768], P(('enc', 'dp'))
- down_bias_grad: float32 [768], P(('enc', 'dp'))
- ffn_gain_grad: float32 [768], P(('enc', 'dp'))
- ffn_shift_grad: float32 [768], P(('enc', 'dp'))
The draws below stay inside these ranges and needn't reach their ends.
Inputs may be any that keep to these rules, and one draw needn't show every extreme that they name: `text_lengths`: each row lists the text lengths of one device's 5 sequences and sums to 512. `region_dest`: A destination in the source's own enc group; of the 128 rows of one device at most 16 name the same destination.
All inputs are finite; a program needn't handle non-finite values.
Results may differ from the reference program's by a relative error of at most 0.017.
Values may be sent and summed in bfloat16 or wider, within the bound.
No kernel may reach another device: no remote copies, remote signals or barrier semaphores. Data moves between devices by JAX's collectives and lax.ppermute only.
A program may use at most 256 MiB of HBM per device.

```python
import math
from functools import partial
import jax
import jax.numpy as jnp
import numpy as np
from jax import lax

D = 768
HEADS = 12
HDIM = 64
FF = 3072
FEAT = 2048
LONGEST = 256
TXT_DEV = 512
REG_SRC = 128
SEQ_DEV = 5
CAP = 16
TOKENS = 16384
REGIONS = 4096
N_DP = 16
DEVICES = 32


def place_ends(array, rng, least, largest):
    place = [jax.random.randint(jax.random.fold_in(rng, axis), (), 0, length) for axis, length in enumerate(array.shape)]
    longest = array.shape.index(max(array.shape))
    neighbour = place[:longest] + [(place[longest] + 1) % array.shape[longest]] + place[longest + 1:]
    return array.at[tuple(place)].set(least).at[tuple(neighbour)].set(largest)


def raised(values, stream_key, source, target, parts, factor):
    def block_of(dim):
        return (jnp.arange(values.shape[dim]) // (values.shape[dim] // parts)).reshape((-1,) + (1,) * (values.ndim - 1 - dim))

    first = jax.random.permutation(stream_key, parts)[block_of(target)]
    far = (block_of(target) + parts // 2) % parts
    return jnp.where((block_of(source) == first) | (block_of(source) == far), factor * values, values)


def steps_of(key, dims, cuts, low, top_value):
    def one(position, blocks):
        heights = jax.random.uniform(jax.random.fold_in(jax.random.fold_in(key, 6), position), (blocks,), jnp.float32, low / len(cuts), top_value / len(cuts))
        return jnp.repeat(jnp.exp(heights), dims[position] // blocks).reshape((-1,) + (1,) * (len(dims) - position - 1))

    loudness = one(*cuts[0])
    for cut in cuts[1:]:
        loudness = loudness * one(*cut)
    return loudness


def split_up(count, total, most, lean):
    portions = [(1 << 20) // math.isqrt(grade ** lean) + 1 for grade in range(2, count + 1)]
    spare, holding = total - most - (count - 1), [1] * (count - 1)
    while spare > 0:
        candidates = [i for i in range(count - 1) if holding[i] < most]
        whole, left = sum([portions[i] for i in candidates]), spare
        for i in candidates:
            addition = min(most - holding[i], max(1, left * portions[i] // whole), spare)
            holding[i] = holding[i] + addition
            spare = spare - addition
    return np.array([most] + holding)


def uneven_parts(own_key, number_of, total, reach, skew):
    if number_of == 2:
        one = jax.random.randint(own_key, (), max(1, total - reach), min(reach, total - 1) + 1)
        return jnp.stack([one, total - one])
    sizes = jnp.asarray(split_up(number_of, total, reach, skew), jnp.int32)
    pairs = (number_of - 1) // 2
    source_of, taker = sizes[1:1 + 2 * pairs:2], sizes[2:2 + 2 * pairs:2]
    room = jnp.minimum(source_of - 1, reach - taker)
    moved = jax.random.randint(jax.random.fold_in(own_key, 1), (pairs,), 0, 1 << 20) % (room + 1)
    sizes = sizes.at[1:1 + 2 * pairs:2].set(source_of - moved).at[2:2 + 2 * pairs:2].set(taker + moved)
    return sizes[jax.random.permutation(jax.random.fold_in(own_key, 2), number_of)]


def routed_block(rng, own, number, rows, number_of, top, reach, slope):
    order = jax.random.permutation(rng, number_of)
    packed, common = portions_of(number_of, rows * top, reach, slope, True), portions_of(number_of, rows * top, reach, slope, False)
    places = jnp.arange(number_of)

    def named(tallies, rotation):
        used = int((tallies > 0).sum())
        fixed = max(1, used // 4)
        moved = fixed + (places - fixed + rotation * (used - fixed)) % max(1, number_of - fixed)
        return jnp.zeros((number_of,), jnp.int32).at[order[jnp.where(places < fixed, places, moved)]].set(jnp.asarray(tallies, jnp.int32))

    tallies = jnp.where(number % 4 == 0, named(packed, number // 4), named(common, number - number // 4 - 1))
    mixed = jax.random.permutation(jax.random.fold_in(own, 3), number_of)
    source_of, taker = mixed[0:number_of // 2 * 2:2], mixed[1:number_of // 2 * 2:2]
    room = jnp.minimum(tallies[source_of] - 1, reach - tallies[taker]) // 2
    room = jnp.where((source_of == order[0]) | (taker == order[0]) | (tallies[taker] == 0), 0, jnp.maximum(room, 0))
    moved = jax.random.randint(jax.random.fold_in(own, 4), (number_of // 2,), 0, 1 << 20) % (room + 1)
    tallies = tallies.at[source_of].add(-moved).at[taker].add(moved)
    members = jnp.searchsorted(jnp.cumsum(tallies), jnp.arange(rows * top), side="right").astype(jnp.int32)
    table = members.reshape(top, rows).T
    table = table[jax.random.permutation(jax.random.fold_in(own, 1), rows)]
    rotation = jax.random.randint(jax.random.fold_in(own, 2), (rows, 1), 0, top)
    return jnp.take_along_axis(table, (jnp.arange(top)[None, :] + rotation) % top, axis=1)


def portions_of(number_of, total, reach, skew, full):
    weights = [(1 << 20) // math.isqrt(standing ** skew) + 1 for standing in range(1, number_of + 1)]
    largest = reach if full else min(reach, max(-(-total // number_of), total * weights[0] // sum(weights)))
    least = 1 if total - largest >= number_of - 1 else 0
    given, surplus = [largest] + [least] * (number_of - 1), total - largest - least * (number_of - 1)
    while surplus > 0:
        movable = [i for i in range(1, number_of) if given[i] < largest] or [i for i in range(1, number_of) if given[i] < reach]
        whole, left = sum([weights[i] for i in movable]), surplus
        for i in movable:
            extra = min(reach - given[i], max(1, left * weights[i] // whole), surplus)
            given[i] = given[i] + extra
            surplus = surplus - extra
    return np.array(given)


def noise(own_key, extent, deviation, limit, split=(), held_as=jnp.bfloat16):
    array = deviation * jax.random.normal(own_key, extent, jnp.float32)
    if split:
        array = array * steps_of(own_key, extent, split, -0.22, 0.18)
    return jnp.clip(array, -limit, limit).astype(held_as)


def gaussian_with(rng, dims, scale, bound, cuts, heavy, held_as=jnp.bfloat16):
    entries = scale * jax.random.normal(rng, dims, jnp.float32)
    if cuts:
        entries = entries * steps_of(rng, dims, cuts, -0.22, 0.18)
    return jnp.clip(raised(entries, jax.random.fold_in(rng, 3), *heavy), -bound, bound).astype(held_as)


def setup_inputs(seed: int = 0) -> dict:
    splits = jax.random.split(jax.random.key(seed), 27)
    text_in = noise(splits[0], (TOKENS, D), 1.0, 6.0, ((0, 32),))
    text_lengths = jax.vmap(lambda own: uneven_parts(own, SEQ_DEV, TXT_DEV, LONGEST, 2))(jax.random.split(splits[1], DEVICES)).reshape((DEVICES, SEQ_DEV)).astype(jnp.int32)
    region_feats = noise(splits[2], (REGIONS, FEAT), 1.0, 6.0, ((0, 32),))
    region_boxes = jnp.clip(1.0 * jax.random.uniform(splits[3], (4, REGIONS), jnp.float32) ** steps_of(splits[3], (4, REGIONS), ((1, 32),), -0.2, 0.2), 0.0, 1.0)
    region_dest_keys = jax.random.split(jax.random.fold_in(splits[4], 1), REGIONS // REG_SRC)
    region_dest_turns = jax.random.permutation(jax.random.fold_in(splits[4], 3), REGIONS // REG_SRC)
    region_dest = jax.vmap(lambda own, number: routed_block(jax.random.fold_in(splits[4], 2), own, number, REG_SRC, N_DP, 1, CAP, 2))(region_dest_keys, region_dest_turns).reshape((REGIONS, 1))
    region_seq = place_ends(jax.random.randint(splits[5], (REGIONS,), 0, SEQ_DEV), jax.random.fold_in(splits[5], 1), 0, SEQ_DEV - 1).astype(jnp.int32)
    w_region = noise(splits[6], (FEAT, D), FEAT ** -0.5, 0.125)
    w_box = noise(splits[7], (4, D), 0.5, 3.0, (), jnp.float32)
    type_embed = noise(splits[8], (D,), 0.5, 3.0, (), jnp.float32)
    region_gain = jnp.clip(1.0 + 0.1 * jax.random.normal(splits[9], (D,), jnp.float32), 0.5, 1.5)
    region_shift = noise(splits[10], (D,), 0.2, 1.2, (), jnp.float32)
    w_qkv = noise(splits[11], (D, 3 * D), D ** -0.5, 0.21875)
    q_bias = noise(splits[12], (D,), 0.5, 3.0, (), jnp.float32)
    v_bias = noise(splits[13], (D,), 0.3, 1.8, (), jnp.float32)
    w_out = noise(splits[14], (D, D), (D // 16) ** -0.5, 0.875)
    out_bias = noise(splits[15], (D,), 0.2, 1.2, (), jnp.float32)
    attn_gain = jnp.clip(1.0 + 0.1 * jax.random.normal(splits[16], (D,), jnp.float32), 0.5, 1.5)
    attn_shift = noise(splits[17], (D,), 0.2, 1.2, (), jnp.float32)
    w_up = noise(splits[18], (D, FF), D ** -0.5, 0.21875)
    up_bias = noise(splits[19], (FF,), 0.3, 1.8, (), jnp.float32)
    w_down = noise(splits[20], (FF, D), FF ** -0.5, 0.109375)
    down_bias = noise(splits[21], (D,), 0.2, 1.2, (), jnp.float32)
    ffn_gain = jnp.clip(1.0 + 0.1 * jax.random.normal(splits[22], (D,), jnp.float32), 0.5, 1.5)
    ffn_shift = noise(splits[23], (D,), 0.2, 1.2, (), jnp.float32)
    cot_text = gaussian_with(splits[24], (TOKENS, D), 1.0, 6.0, ((0, 32),), (0, 1, 32, 2.75))
    cot_region = gaussian_with(splits[25], (REGIONS, D), 1.0, 6.0, ((0, 32),), (0, 1, 32, 2.75))
    return dict(text_in=text_in, text_lengths=text_lengths, region_feats=region_feats, region_boxes=region_boxes, region_dest=region_dest, region_seq=region_seq, w_region=w_region, w_box=w_box, type_embed=type_embed, region_gain=region_gain, region_shift=region_shift, w_qkv=w_qkv, q_bias=q_bias, v_bias=v_bias, w_out=w_out, out_bias=out_bias, attn_gain=attn_gain, attn_shift=attn_shift, w_up=w_up, up_bias=up_bias, w_down=w_down, down_bias=down_bias, ffn_gain=ffn_gain, ffn_shift=ffn_shift, cot_text=cot_text, cot_region=cot_region)


highest = lax.Precision.HIGHEST
eps = 1e-05

@jax.custom_vjp
def low(v):
    return lax.optimization_barrier(v.astype(jnp.bfloat16)).astype(jnp.float32)

@jax.custom_vjp
def low_back(v):
    return v

def low_keep(v):
    return (low(v), None)

def low_pass(kept, grad):
    return (grad,)

def back_keep(v):
    return (v, None)

def back_low(kept, grad):
    return (low(grad),)
low.defvjp(low_keep, low_pass)
low_back.defvjp(back_keep, back_low)

def normalize(inputs, gain_vec, shift_vec):
    row_mean = lax.optimization_barrier(jnp.mean(inputs, axis=-1, keepdims=True))
    centred = inputs - row_mean
    spread = lax.optimization_barrier(jnp.mean(centred * centred, axis=-1, keepdims=True))
    return centred * lax.rsqrt(spread + eps) * gain_vec + shift_vec

def layer(params, all_rows, segment):
    row_count = all_rows.shape[0]
    projected = jnp.dot(all_rows, params[0], precision=highest)
    queries = low_back(low(projected[:, :D] + params[1]))
    key_rows = low_back(low(projected[:, D:2 * D]))
    values = low_back(low(projected[:, 2 * D:] + params[2]))
    q_heads = queries.reshape(row_count, HEADS, HDIM)
    k_heads = key_rows.reshape(row_count, HEADS, HDIM)
    v_heads = values.reshape(row_count, HEADS, HDIM)
    scores = low_back(jnp.einsum('qhd,khd->hqk', q_heads, k_heads, precision=highest) * HDIM ** (-0.5))
    same_seq = segment[:, None] == segment[None, :]
    chance = jax.nn.softmax(jnp.where(same_seq[None], scores, -1e+30), axis=-1)
    context = jnp.einsum('hqk,khd->qhd', low(chance), v_heads, precision=highest).reshape(row_count, D)
    context = low_back(low(context))
    attn_out = low_back(jnp.dot(context, params[3], precision=highest) + params[4])
    normed_one = normalize(all_rows + attn_out, params[5], params[6])
    up_sum = low_back(jnp.dot(low(normed_one), params[7], precision=highest) + params[8])
    hidden = low(jax.nn.gelu(up_sum, approximate=False))
    down_sum = low_back(jnp.dot(hidden, params[9], precision=highest) + params[10])
    return normalize(normed_one + down_sum, params[11], params[12])

def reference(text_in, text_lengths, region_feats, region_boxes, region_dest, region_seq, w_region, w_box, type_embed, region_gain, region_shift, w_qkv, q_bias, v_bias, w_out, out_bias, attn_gain, attn_shift, w_up, up_bias, w_down, down_bias, ffn_gain, ffn_shift, cot_text, cot_region):
    capacity = max(2, 2 * REG_SRC // N_DP)
    slot_count = capacity * N_DP
    dest_of = region_dest[:, 0].reshape(DEVICES, REG_SRC)
    onehot = (dest_of[:, :, None] == jnp.arange(N_DP, dtype=jnp.int32)[None, None, :]).astype(jnp.int32)
    before = jnp.cumsum(onehot, axis=1) - onehot
    rank_of = lax.optimization_barrier(jnp.sum(before * onehot, axis=2))
    device_of = jnp.arange(DEVICES, dtype=jnp.int32)
    target = (device_of // N_DP)[:, None] * N_DP + dest_of
    slot_of = (target * slot_count + (device_of % N_DP)[:, None] * capacity + rank_of).reshape(-1).astype(jnp.int32)
    seq_ends = jnp.cumsum(text_lengths, axis=1)
    positions = jnp.arange(TXT_DEV, dtype=jnp.int32)
    text_seg = lax.optimization_barrier(jnp.sum((positions[None, :, None] >= seq_ends[:, None, :]).astype(jnp.int32), axis=2))
    region_seg = jnp.full((DEVICES * slot_count,), SEQ_DEV, jnp.int32).at[slot_of].set(region_seq)
    segment = jnp.concatenate([text_seg.astype(jnp.int32), region_seg.reshape(DEVICES, slot_count)], axis=1)

    def forward(params, text_f, feats_f):
        projection = low_back(jnp.dot(feats_f, params[0], precision=highest))
        spatial = jnp.dot(region_boxes.T, params[1], precision=highest)
        region_rows = low_back(low(normalize(projection + spatial + params[2], params[3], params[4])))
        buffer = jnp.zeros((DEVICES * slot_count, D), jnp.float32).at[slot_of].set(region_rows)
        all_rows = jnp.concatenate([text_f.reshape(DEVICES, TXT_DEV, D), buffer.reshape(DEVICES, slot_count, D)], axis=1)
        device_layer = jax.checkpoint(partial(layer, params[5:]))
        result = lax.map(lambda device_pair: device_layer(device_pair[0], device_pair[1]), (all_rows, segment))
        text_out = result[:, :TXT_DEV].reshape(DEVICES * TXT_DEV, D)
        region_out = result[:, TXT_DEV:].reshape(DEVICES * slot_count, D)[slot_of]
        return (text_out, region_out)
    params = tuple((tensor.astype(jnp.float32) for tensor in (w_region, w_box, type_embed, region_gain, region_shift, w_qkv, q_bias, v_bias, w_out, out_bias, attn_gain, attn_shift, w_up, up_bias, w_down, down_bias, ffn_gain, ffn_shift)))
    outputs, pullback = jax.vjp(forward, params, text_in.astype(jnp.float32), region_feats.astype(jnp.float32))
    grads_w, text_grad, feats_grad = pullback((cot_text.astype(jnp.float32), cot_region.astype(jnp.float32)))
    return (outputs[0].astype(jnp.bfloat16), outputs[1].astype(jnp.bfloat16), text_grad.astype(jnp.bfloat16), feats_grad.astype(jnp.bfloat16), grads_w[0], grads_w[1], grads_w[2], grads_w[3], grads_w[4], grads_w[5], grads_w[6], grads_w[7], grads_w[8], grads_w[9], grads_w[10], grads_w[11], grads_w[12], grads_w[13], grads_w[14], grads_w[15], grads_w[16], grads_w[17])
```

```python
import functools

import jax
import jax.numpy as jnp
from jax import lax
from jax.experimental import pallas as pl
from jax.experimental.pallas import tpu as pltpu
from jax.sharding import PartitionSpec as P

D = 768
HEADS = 12
HDIM = 64
PAIR = 2 * HDIM
PAIRS = HEADS // 2
TAGS = 128
VECS = 128

F32 = jnp.float32
BF16 = jnp.bfloat16
eps = 1e-05
SCALE = HDIM ** (-0.5)

TAIL_RATE = 0.3275911 * 0.7071067811865476
TAIL = (0.254829592, -0.284496736, 1.421413741, -1.453152027, 1.061405429)


def dot_nn(left, right):
    return lax.dot_general(left, right, (((1,), (0,)), ((), ())), preferred_element_type=F32)


def dot_nt(left, right):
    return lax.dot_general(left, right, (((1,), (1,)), ((), ())), preferred_element_type=F32)


def dot_tn(left, right):
    return lax.dot_general(left, right, (((0,), (0,)), ((), ())), preferred_element_type=F32)


def standardize(inputs):
    row_mean = jnp.mean(inputs, axis=-1, keepdims=True)
    centred = inputs - row_mean
    spread = jnp.mean(centred * centred, axis=-1, keepdims=True)
    inv = lax.rsqrt(spread + eps)
    return centred * inv, inv


def standardize_back(grad, norm, inv):
    first = jnp.mean(grad, axis=-1, keepdims=True)
    second = jnp.mean(grad * norm, axis=-1, keepdims=True)
    return (grad - first - norm * second) * inv


def row_of(ref):
    return ref[...].reshape(1, D)


def column_sum(inputs):
    return jnp.sum(inputs, axis=0, keepdims=True)


def whole(shape):
    return pl.BlockSpec(shape, lambda *_: (0,) * len(shape), pipeline_mode=pl.Buffered(1))


def struct(shape, dtype):
    return jax.ShapeDtypeStruct(shape, dtype)


def cost(flops, moved, exps=0):
    return pl.CostEstimate(flops=int(flops), bytes_accessed=int(moved), transcendentals=int(exps))


def region_body(
    capacity,
    feats_ref,
    w_ref,
    boxes_ref,
    dest_ref,
    seq_ref,
    w_box_ref,
    type_ref,
    gain_ref,
    shift_ref,
    cot_ref,
    out_ref,
    cot_out_ref,
    hot_ref,
    norm_ref,
    inv_ref,
):
    rows = feats_ref.shape[0]
    slots = out_ref.shape[0]
    dest_row = jnp.broadcast_to(dest_ref[...].astype(F32), (rows, rows))
    dest_col = dest_row.T
    row_io = lax.broadcasted_iota(jnp.int32, (rows, rows), 0)
    col_io = lax.broadcasted_iota(jnp.int32, (rows, rows), 1)
    earlier = jnp.where((dest_col == dest_row) & (row_io < col_io), 1.0, 0.0)
    slot = dest_row[0:1, :] * capacity + column_sum(earlier)
    slot_io = lax.broadcasted_iota(jnp.int32, (slots, rows), 0).astype(F32)
    hot = jnp.where(slot_io == slot, 1.0, 0.0)
    hot_low = hot.astype(BF16)
    hot_ref[...] = hot_low
    cot_out_ref[...] = dot_nn(hot_low, cot_ref[...]).astype(BF16)
    tags = jnp.sum(hot * (seq_ref[...].astype(F32) + 1.0), axis=1, keepdims=True)
    projection = dot_nn(feats_ref[...], w_ref[...])
    boxes = jnp.concatenate([boxes_ref[...], jnp.zeros((4, rows), F32)], axis=0).T
    spatial = boxes[:, 0:1] * w_box_ref[0:1, :]
    for side in range(1, 4):
        spatial = spatial + boxes[:, side : side + 1] * w_box_ref[side : side + 1, :]
    norm, inv = standardize(projection + spatial + row_of(type_ref))
    norm_ref[...] = norm
    inv_ref[...] = inv
    low_rows = (norm * row_of(gain_ref) + row_of(shift_ref)).astype(BF16)
    out_ref[:, :D] = dot_nn(hot_low, low_rows).astype(BF16)
    out_ref[:, D:] = jnp.broadcast_to(tags, (slots, TAGS)).astype(BF16)


def region_forward(capacity, slots, feats, w_region, *others):
    rows, width = feats.shape
    return pl.pallas_call(
        functools.partial(region_body, capacity),
        out_shape=(
            struct((slots, D + TAGS), BF16),
            struct((slots, D), BF16),
            struct((slots, rows), BF16),
            struct((rows, D), F32),
            struct((rows, 1), F32),
        ),
        cost_estimate=cost(2 * rows * width * D, 2 * (rows + D) * width),
        name="region_forward",
    )(feats, w_region, *others)


def head_mask(head):
    lane = lax.broadcasted_iota(jnp.int32, (1, PAIR), 1)
    return (lane >= head * HDIM) & (lane < (head + 1) * HDIM)


def join(*refs):
    return jnp.concatenate([ref[...] for ref in refs], axis=0)


def thirds(rows):
    return [pl.BlockSpec((rows, PAIR), lambda p, *_, part=part: (0, part * PAIRS + p)) for part in range(3)]


def attend_body(
    lengths_ref,
    tag_ref,
    text_q_ref,
    text_k_ref,
    text_v_ref,
    region_q_ref,
    region_k_ref,
    region_v_ref,
    ctx_ref,
    chance_ref,
    inv_ref,
    bias_ref,
):
    text_count, slots = text_q_ref.shape[0], region_q_ref.shape[0]
    count = text_count + slots
    sequences = lengths_ref.shape[1]

    @pl.when(pl.program_id(0) == 0)
    def _():
        place = lax.broadcasted_iota(jnp.int32, (text_count, 1), 0)
        text_seg = jnp.zeros((text_count, 1), F32)
        end = jnp.int32(0)
        for index in range(sequences):
            end = end + lengths_ref[0, index]
            text_seg = text_seg + jnp.where(place >= end, 1.0, 0.0)
        region_seg = tag_ref[:, 0:1].astype(F32) - 1.0
        region_seg = jnp.where(region_seg < 0.0, float(sequences), region_seg)
        seg_col = jnp.concatenate([text_seg, region_seg], axis=0)
        seg_row = jnp.broadcast_to(seg_col, (count, 128)).T[0:1, :]
        bias_ref[...] = jnp.where(seg_col == seg_row, 0.0, -1e30)

    queries = join(text_q_ref, region_q_ref) * jnp.asarray(SCALE, BF16)
    key_rows = join(text_k_ref, region_k_ref)
    values = join(text_v_ref, region_v_ref)
    step = 256
    first = head_mask(0)
    for start in range(0, count, step):
        stop = start + step
        outs, invs = [], []
        for head in range(2):
            q_part = jnp.where(head_mask(head), queries[start:stop], jnp.zeros((), BF16))
            scores = dot_nt(q_part, key_rows) + bias_ref[start:stop, :]
            exp_terms = jnp.exp(scores - jnp.max(scores, axis=1, keepdims=True))
            inv = 1.0 / jnp.sum(exp_terms, axis=1, keepdims=True)
            low_terms = exp_terms.astype(BF16)
            chance_ref[head, start:stop, :] = low_terms
            outs.append(dot_nn(low_terms, values) * inv)
            invs.append(inv)
        ctx_ref[start:stop, :] = jnp.where(first, outs[0], outs[1]).astype(BF16)
        inv_ref[start:stop, :] = jnp.where(first, invs[0], invs[1])


def attend(lengths, arrived, qkv_text, qkv_region):
    text_count, slots = qkv_text.shape[0], qkv_region.shape[0]
    count = text_count + slots
    return pl.pallas_call(
        attend_body,
        grid_spec=pltpu.PrefetchScalarGridSpec(
            num_scalar_prefetch=1,
            grid=(PAIRS,),
            in_specs=[pl.BlockSpec((slots, TAGS), lambda p, *_: (0, D // TAGS))] + thirds(text_count) + thirds(slots),
            out_specs=[
                pl.BlockSpec((count, PAIR), lambda p, *_: (0, p)),
                pl.BlockSpec((2, count, count), lambda p, *_: (p, 0, 0)),
                pl.BlockSpec((count, PAIR), lambda p, *_: (0, p)),
            ],
            scratch_shapes=[pltpu.VMEM((count, count), F32)],
        ),
        out_shape=(
            struct((count, D), BF16),
            struct((HEADS, count, count), BF16),
            struct((count, D), F32),
        ),
        cost_estimate=cost(4 * count * count * D * 4, HEADS * count * count * 2, HEADS * count * count),
        name="attend",
    )(lengths, arrived, *(qkv_text,) * 3, *(qkv_region,) * 3)


def attend_back_body(
    text_q_ref,
    text_k_ref,
    text_v_ref,
    region_q_ref,
    region_k_ref,
    region_v_ref,
    w_q_ref,
    w_k_ref,
    w_v_ref,
    chance_ref,
    inv_ref,
    ctx_ref,
    dctx_ref,
    d_mid_ref,
    grad_ref,
    sum_ref,
    text_grad_ref,
    region_grad_ref,
    total_ref,
):
    count = ctx_ref.shape[0]
    text_count = text_q_ref.shape[0]
    queries = join(text_q_ref, region_q_ref) * jnp.asarray(SCALE, BF16)
    key_rows = join(text_k_ref, region_k_ref)
    values = join(text_v_ref, region_v_ref)
    scaled = dctx_ref[...].astype(F32) * inv_ref[...]
    product = scaled * ctx_ref[...].astype(F32)
    scaled_low = scaled.astype(BF16)
    scaled_turned = scaled.T.astype(BF16)
    q_turned = queries.astype(F32).T.astype(BF16)
    step = 256
    first = head_mask(0)
    keys_turned, values_turned = [None, None], [None, None]
    for start in range(0, count, step):
        stop = start + step
        ques = []
        for head in range(2):
            mask = head_mask(head)
            low, high = head * HDIM, (head + 1) * HDIM
            low_terms = chance_ref[head, start:stop, :]
            delta = jnp.sum(jnp.where(mask, product[start:stop], 0.0), axis=1, keepdims=True)
            d_part = jnp.where(mask, scaled_low[start:stop], jnp.zeros((), BF16))
            d_chance = dot_nt(d_part, values)
            d_scores = (low_terms.astype(F32) * (d_chance - delta)).astype(BF16)
            ques.append(dot_nn(d_scores, key_rows))
            v_add = dot_nn(scaled_turned[low:high, start:stop], low_terms)
            k_add = dot_nn(q_turned[low:high, start:stop], d_scores)
            values_turned[head] = v_add if start == 0 else values_turned[head] + v_add
            keys_turned[head] = k_add if start == 0 else keys_turned[head] + k_add
        d_ques = (jnp.where(first, ques[0], ques[1]) * SCALE).astype(BF16)
        grad_ref[start:stop, :PAIR] = d_ques
    grad_ref[:, PAIR : 2 * PAIR] = jnp.concatenate(keys_turned, axis=0).T.astype(BF16)
    d_values = jnp.concatenate(values_turned, axis=0).T.astype(BF16)
    grad_ref[:, 2 * PAIR :] = d_values
    sum_ref[...] = column_sum(grad_ref[...].astype(F32))

    @pl.when(pl.program_id(0) == 0)
    def _():
        total_ref[...] = d_mid_ref[...]

    w_part = jnp.concatenate([w_q_ref[...], w_k_ref[...], w_v_ref[...]], axis=1)
    total_ref[...] += dot_nt(grad_ref[...], w_part)

    @pl.when(pl.program_id(0) == pl.num_programs(0) - 1)
    def _():
        text_grad_ref[...] = total_ref[:text_count, :].astype(BF16)
        region_grad_ref[...] = total_ref[text_count:, :].astype(BF16)


def attend_back(qkv_text, qkv_region, w_qkv, chance, inv, ctx, d_ctx, d_mid):
    text_count, slots = qkv_text.shape[0], qkv_region.shape[0]
    count = text_count + slots
    return pl.pallas_call(
        attend_back_body,
        grid=(PAIRS,),
        in_specs=thirds(text_count)
        + thirds(slots)
        + thirds(D)
        + [
            pl.BlockSpec((2, count, count), lambda p: (p, 0, 0)),
            pl.BlockSpec((count, PAIR), lambda p: (0, p)),
            pl.BlockSpec((count, PAIR), lambda p: (0, p)),
            pl.BlockSpec((count, PAIR), lambda p: (0, p)),
            whole((count, D)),
        ],
        out_specs=[
            pl.BlockSpec((count, 3 * PAIR), lambda p: (0, p)),
            pl.BlockSpec((1, 3 * PAIR), lambda p: (0, p)),
            whole((text_count, D)),
            whole((slots, D)),
        ],
        out_shape=(
            struct((count, 3 * D), BF16),
            struct((1, 3 * D), F32),
            struct((text_count, D), BF16),
            struct((slots, D), BF16),
        ),
        scratch_shapes=[pltpu.VMEM((count, D), F32)],
        cost_estimate=cost(8 * count * count * D * 4 + 6 * count * D * D, HEADS * count * count * 2),
        name="attend_back",
    )(*(qkv_text,) * 3, *(qkv_region,) * 3, *(w_qkv,) * 3, chance, inv, ctx, d_ctx, d_mid)


def gelu_parts(inputs):
    weight = jnp.exp(inputs * inputs * (-0.5))
    place = 1.0 / (1.0 + jnp.abs(inputs) * TAIL_RATE)
    poly = TAIL[4]
    for factor in TAIL[3::-1]:
        poly = poly * place + factor
    tail = (0.5 * weight) * (poly * place)
    phi_sum = jnp.where(inputs >= 0.0, 1.0 - tail, tail)
    return inputs * phi_sum, phi_sum + inputs * (weight * 0.3989422804014327)


def feed_body(
    ctx_ref,
    w_out_ref,
    text_ref,
    region_ref,
    perm_ref,
    out_bias_ref,
    attn_gain_ref,
    attn_shift_ref,
    down_bias_ref,
    ffn_gain_ref,
    ffn_shift_ref,
    w_up_ref,
    up_bias_ref,
    w_down_ref,
    cot_text_ref,
    cot_region_ref,
    hidden_ref,
    slope_ref,
    norm_ref,
    inv_ref,
    rows_keep_ref,
    rows_send_ref,
    ctx_keep_ref,
    ctx_send_ref,
    low_keep_ref,
    low_send_ref,
    text_out_ref,
    region_out_ref,
    d_second_ref,
    d_down_ref,
    stats_ref,
    normed_ref,
    low_ref,
    total_ref,
):
    step = pl.program_id(0)
    text_count = text_ref.shape[0]
    count = ctx_ref.shape[0]
    half = rows_keep_ref.shape[0]
    parts = [(start, start + 256) for start in range(0, count, 256)]

    def pick(first_ref, second_ref, start, stop):
        if start < text_count:
            return first_ref[start:stop, :]
        return second_ref[start - text_count : stop - text_count, :]

    @pl.when(step == 0)
    def _():
        for start, stop in parts:
            rows = pick(text_ref, region_ref, start, stop)
            ctx = ctx_ref[start:stop, :]
            attn_out = dot_nn(ctx, w_out_ref[...]) + row_of(out_bias_ref)
            norm, inv = standardize(rows.astype(F32) + attn_out)
            normed = norm * row_of(attn_gain_ref) + row_of(attn_shift_ref)
            low = normed.astype(BF16)
            norm_ref[start:stop, :] = norm
            inv_ref[start:stop, :] = inv
            normed_ref[start:stop, :] = normed
            low_ref[start:stop, :] = low
            total_ref[start:stop, :] = normed + row_of(down_bias_ref)
            turned = dot_nt(perm_ref[...], rows).astype(BF16)
            rows_keep_ref[:, start:stop] = turned[:half]
            rows_send_ref[:, start:stop] = turned[half:]
            turned = dot_nt(perm_ref[...], ctx).astype(BF16)
            ctx_keep_ref[:, start:stop] = turned[:half]
            ctx_send_ref[:, start:stop] = turned[half:]
            turned = dot_nt(perm_ref[...], low).astype(BF16)
            low_keep_ref[:, start:stop] = turned[:half]
            low_send_ref[:, start:stop] = turned[half:]

    for start, stop in parts:
        up_sum = dot_nn(low_ref[start:stop, :], w_up_ref[...]) + up_bias_ref[...]
        value, slope = gelu_parts(up_sum)
        hidden = value.astype(BF16)
        hidden_ref[start:stop, :] = hidden
        slope_ref[start:stop, :] = slope.astype(BF16)
        total_ref[start:stop, :] += dot_nn(hidden, w_down_ref[...])

    @pl.when(step == pl.num_programs(0) - 1)
    def _():
        stats = [jnp.zeros((1, D), F32)] * 3
        for start, stop in parts:
            norm, inv = standardize(total_ref[start:stop, :])
            layer_out = (norm * row_of(ffn_gain_ref) + row_of(ffn_shift_ref)).astype(BF16)
            if start < text_count:
                text_out_ref[start:stop, :] = layer_out
            else:
                region_out_ref[start - text_count : stop - text_count, :] = layer_out
            upstream = pick(cot_text_ref, cot_region_ref, start, stop).astype(F32)
            d_second = standardize_back(upstream * row_of(ffn_gain_ref), norm, inv)
            d_down = d_second.astype(BF16)
            d_second_ref[start:stop, :] = d_second
            d_down_ref[start:stop, :] = d_down
            stats = [
                stats[0] + column_sum(upstream * norm),
                stats[1] + column_sum(upstream),
                stats[2] + column_sum(d_down.astype(F32)),
            ]
        stats_ref[...] = jnp.concatenate(stats + [jnp.zeros((5, D), F32)], axis=0)


def feed_forward(ctx, w_out, text, arrived, perm, vecs, w_up, up_bias, w_down, cot_text, cot_region):
    count, text_count = ctx.shape[0], text.shape[0]
    slots = count - text_count
    units = w_up.shape[1]
    chunk = 512
    half = D // 2
    return pl.pallas_call(
        feed_body,
        grid=(units // chunk,),
        in_specs=[
            whole((count, D)),
            whole((D, D)),
            whole((text_count, D)),
            whole((slots, D)),
            whole((D, D)),
        ]
        + [whole((D,))] * len(vecs)
        + [
            pl.BlockSpec((D, chunk), lambda j: (0, j)),
            pl.BlockSpec((1, chunk), lambda j: (0, j)),
            pl.BlockSpec((chunk, D), lambda j: (j, 0)),
            whole((text_count, D)),
            whole((slots, D)),
        ],
        out_specs=[
            pl.BlockSpec((count, chunk), lambda j: (0, j)),
            pl.BlockSpec((count, chunk), lambda j: (0, j)),
            whole((count, D)),
            whole((count, 1)),
            whole((half, count)),
            whole((half, count)),
            whole((half, count)),
            whole((half, count)),
            whole((half, count)),
            whole((half, count)),
            whole((text_count, D)),
            whole((slots, D)),
            whole((count, D)),
            whole((count, D)),
            whole((8, D)),
        ],
        out_shape=(
            struct((count, units), BF16),
            struct((count, units), BF16),
            struct((count, D), F32),
            struct((count, 1), F32),
            struct((half, count), BF16),
            struct((half, count), BF16),
            struct((half, count), BF16),
            struct((half, count), BF16),
            struct((half, count), BF16),
            struct((half, count), BF16),
            struct((text_count, D), BF16),
            struct((slots, D), BF16),
            struct((count, D), F32),
            struct((count, D), BF16),
            struct((8, D), F32),
        ),
        scratch_shapes=[
            pltpu.VMEM((count, D), F32),
            pltpu.VMEM((count, D), BF16),
            pltpu.VMEM((count, D), F32),
        ],
        cost_estimate=cost(4 * count * D * units + 8 * count * D * D, 4 * D * units + 4 * count * units, count * units),
        name="feed_forward",
    )(ctx, w_out, text, arrived, perm, *vecs, w_up, up_bias, w_down, cot_text, cot_region)


def feed_back_body(
    d_down_ref,
    slope_ref,
    w_down_ref,
    w_up_ref,
    d_second_ref,
    norm_ref,
    inv_ref,
    gain_ref,
    w_out_ref,
    d_up_ref,
    up_sum_ref,
    d_mid_ref,
    d_attn_ref,
    d_ctx_ref,
    stats_ref,
    total_ref,
):
    step = pl.program_id(0)
    count = d_down_ref.shape[0]
    parts = [(start, start + 256) for start in range(0, count, 256)]

    @pl.when(step == 0)
    def _():
        total_ref[...] = d_second_ref[...]

    up_total = jnp.zeros(up_sum_ref.shape, F32)
    for start, stop in parts:
        d_hidden = dot_nt(d_down_ref[start:stop, :], w_down_ref[...])
        d_up = (d_hidden * slope_ref[start:stop, :].astype(F32)).astype(BF16)
        d_up_ref[start:stop, :] = d_up
        up_total = up_total + column_sum(d_up.astype(F32))
        total_ref[start:stop, :] += dot_nt(d_up, w_up_ref[...])
    up_sum_ref[...] = up_total

    @pl.when(step == pl.num_programs(0) - 1)
    def _():
        stats = [jnp.zeros((1, D), F32)] * 3
        for start, stop in parts:
            d_first = total_ref[start:stop, :]
            norm = norm_ref[start:stop, :]
            d_mid = standardize_back(d_first * row_of(gain_ref), norm, inv_ref[start:stop, :])
            d_attn = d_mid.astype(BF16)
            d_mid_ref[start:stop, :] = d_mid
            d_attn_ref[start:stop, :] = d_attn
            d_ctx_ref[start:stop, :] = dot_nt(d_attn, w_out_ref[...]).astype(BF16)
            stats = [
                stats[0] + column_sum(d_first * norm),
                stats[1] + column_sum(d_first),
                stats[2] + column_sum(d_attn.astype(F32)),
            ]
        stats_ref[...] = jnp.concatenate(stats + [jnp.zeros((5, D), F32)], axis=0)


def feed_back(d_down, slope, w_down, w_up, d_second, norm, inv, gain, w_out):
    count, units = slope.shape
    chunk = 512
    return pl.pallas_call(
        feed_back_body,
        grid=(units // chunk,),
        in_specs=[
            whole((count, D)),
            pl.BlockSpec((count, chunk), lambda j: (0, j)),
            pl.BlockSpec((chunk, D), lambda j: (j, 0)),
            pl.BlockSpec((D, chunk), lambda j: (0, j)),
            whole((count, D)),
            whole((count, D)),
            whole((count, 1)),
            whole((D,)),
            whole((D, D)),
        ],
        out_specs=[
            pl.BlockSpec((count, chunk), lambda j: (0, j)),
            pl.BlockSpec((1, chunk), lambda j: (0, j)),
            whole((count, D)),
            whole((count, D)),
            whole((count, D)),
            whole((8, D)),
        ],
        out_shape=(
            struct((count, units), BF16),
            struct((1, units), F32),
            struct((count, D), F32),
            struct((count, D), BF16),
            struct((count, D), BF16),
            struct((8, D), F32),
        ),
        scratch_shapes=[pltpu.VMEM((count, D), F32)],
        cost_estimate=cost(4 * count * D * units + 2 * count * D * D, 4 * D * units + 4 * count * units),
        name="feed_back",
    )(d_down, slope, w_down, w_up, d_second, norm, inv, gain, w_out)


def region_back_body(
    back_ref,
    hot_ref,
    norm_ref,
    inv_ref,
    gain_ref,
    boxes_ref,
    qkv_ref,
    attn_ref,
    ffn_ref,
    up_ref,
    perm_ref,
    d_proj_ref,
    *piece_refs,
):
    rows = norm_ref.shape[0]
    d_region = dot_tn(hot_ref[...], back_ref[...])
    norm = norm_ref[...]
    d_pre = standardize_back(d_region * row_of(gain_ref), norm, inv_ref[...])
    d_proj = d_pre.astype(BF16)
    d_proj_ref[...] = d_proj
    boxes = jnp.concatenate([boxes_ref[...], jnp.zeros((4, rows), F32)], axis=0).T
    vectors = [column_sum(d_pre), column_sum(d_region * norm), column_sum(d_region)]
    vectors += [column_sum(boxes[:, side : side + 1] * d_pre) for side in range(4)]
    for part in (0, 2):
        starts = [(3 * pair + part) * PAIR for pair in range(PAIRS)]
        vectors.append(jnp.concatenate([qkv_ref[:, start : start + PAIR] for start in starts], axis=1))
    for ref in (attn_ref, ffn_ref):
        vectors += [ref[2:3, :], ref[0:2, :]]
    vectors.append(up_ref[...])
    filled = sum(vector.shape[0] for vector in vectors)
    vectors.append(jnp.zeros((VECS - filled, D), F32))
    low_vectors = jnp.concatenate(vectors, axis=0).astype(BF16)
    turned = dot_nt(perm_ref[...], jnp.concatenate([d_proj, low_vectors], axis=0)).astype(BF16)
    size = D // len(piece_refs)
    for index, piece_ref in enumerate(piece_refs):
        piece_ref[...] = turned[index * size : (index + 1) * size]


def region_back(back, hot, norm, *others):
    rows = norm.shape[0]
    return pl.pallas_call(
        region_back_body,
        out_shape=(struct((rows, D), BF16),) + (struct((D // 4, rows + VECS), BF16),) * 4,
        cost_estimate=cost(0, 0),
        name="region_back",
    )(back, hot, norm, *others)


def swap_cores(sent):
    return lax.ppermute(sent, "enc", [(0, 1), (1, 0)])


def swap_chips(sent, offset, peers):
    return lax.ppermute(sent, "dp", [(peer, peer ^ offset) for peer in range(peers)])


MASKS = (0, 1, 3, 2)


def reverse(value, width):
    result = value & 0
    for bit in range(width):
        result = result | (((value >> bit) & 1) << (width - 1 - bit))
    return result


def after(first, *others):
    if not others:
        return first
    return lax.optimization_barrier((first,) + others)[0]


def swap_cores(sent):
    return [lax.ppermute(array, "enc", [(0, 1), (1, 0)]) for array in sent]


def swap_chips(sent, mask, peers):
    return lax.ppermute(sent, "dp", [(peer, peer ^ mask) for peer in range(peers)])


def cut_rows(parts, start, stop):
    return [tuple(array[start:stop] for array in arrays) for arrays in parts]


def edges_of(arrays):
    edges = [0]
    for array in arrays:
        edges.append(edges[-1] + array.shape[-1])
    return edges


def columns_of(arrays, start, stop):
    for array, low, high in zip(arrays, edges_of(arrays), edges_of(arrays)[1:]):
        if low <= start and stop <= high:
            return array[..., start - low : stop - low]
    pieces = []
    for array, low, high in zip(arrays, edges_of(arrays), edges_of(arrays)[1:]):
        if max(start, low) < min(stop, high):
            pieces.append(array[..., max(start, low) - low : min(stop, high) - low])
    return jnp.concatenate(pieces, axis=-1)


def total(parts):
    edges = sorted(set(sum([edges_of(arrays) for arrays in parts], [])))
    sums = []
    for start, stop in zip(edges, edges[1:]):
        sums.append(functools.reduce(jnp.add, [columns_of(arrays, start, stop).astype(F32) for arrays in parts]))
    return sums[0] if len(sums) == 1 else jnp.concatenate(sums, axis=-1)


def total_low(parts):
    return total(parts).astype(BF16)


class Pair:
    def __init__(self, parts, middle, peers):
        self.sides, self.peers = zip(*[split_columns(arrays, middle) for arrays in parts]), peers
        self.first, self.second = [list(side) for side in self.sides]
        self.quarter = parts[0][0].shape[0] // 4

    def start(self):
        size = self.quarter
        self.sent = [
            total_low(cut_rows(self.first, size, 3 * size)),
            total_low(cut_rows(self.second, 2 * size, 4 * size)),
        ]
        return self.sent

    def ship(self):
        self.got = [swap_chips(sent, bit, self.peers) for sent, bit in zip(self.sent, (1, 2))]
        return self.got

    def hold(self, *behind):
        self.got = [after(array, *behind) for array in self.got]

    def turn(self):
        size = self.quarter
        one, two = self.got
        self.sent = [
            total_low(cut_rows(self.first, 3 * size, 4 * size) + [(one[size:],)]),
            total_low(cut_rows(self.second, size, 2 * size) + [(two[:size],)]),
        ]
        return self.sent

    def finish(self):
        size = self.quarter
        last = [swap_chips(sent, bit, self.peers) for sent, bit in zip(self.sent, (2, 1))]
        one, two = self.got
        parts = [left + right for left, right in zip(cut_rows(self.first, 0, size), cut_rows(self.second, 0, size))]
        return Scatter(parts + [(one[:size], two[size:]), tuple(last)], self.peers)


class Scatter:
    def __init__(self, parts, peers, bit=2):
        self.parts, self.peers, self.bit, self.fresh = parts, peers, bit, 1

    def cut(self, width, *behind):
        self.width = min(width, self.peers.bit_length() - 1 - self.bit)
        size = self.parts[0][0].shape[0] >> self.width
        self.sent = [
            after(total_low(cut_rows(self.parts, offset * size, (offset + 1) * size)), *behind)
            for offset in range(1, 1 << self.width)
        ]
        self.parts = cut_rows(self.parts, 0, size)
        return self.sent

    def ship(self):
        masks = [reverse(offset, self.width) << self.bit for offset in range(1, 1 << self.width)]
        got = [swap_chips(sent, mask, self.peers) for sent, mask in zip(self.sent, masks)]
        self.parts = self.parts + [(array,) for array in got]
        self.bit += self.width
        self.fresh = len(got)
        return got

    def hold(self, *behind):
        late = [tuple(after(array, *behind) for array in arrays) for arrays in self.parts[-self.fresh :]]
        self.parts = self.parts[: -self.fresh] + late

    def finish(self, width):
        while 1 << self.bit < self.peers:
            self.cut(width)
            self.ship()
        return self

    def result(self, start=0, stop=None):
        stop = edges_of(self.parts[0])[-1] if stop is None else stop
        return total([(columns_of(arrays, start, stop),) for arrays in self.parts])


def direct(parts, peers, bit, *behind):
    size = parts[0][0].shape[0] // 4
    sent = [total_low(cut_rows(parts, place * size, (place + 1) * size)) for place in range(1, 4)]
    sent = [after(array, *behind) for array in sent]
    got = [swap_chips(array, mask, peers) for array, mask in zip(sent, MASKS[1:])]
    parts = cut_rows(parts, 0, size) + [(array,) for array in got]
    return sent, got, Scatter(parts, peers, bit)


def split_columns(arrays, middle):
    first, second, start = [], [], 0
    for array in arrays:
        width = array.shape[-1]
        cut = min(max(middle - start, 0), width)
        if cut:
            first.append(array[:, :cut])
        if cut < width:
            second.append(array[:, cut:])
        start += width
    return tuple(first), tuple(second)


def swap_near(pieces, peers):
    return [swap_chips(piece, offset << 2, peers) for offset, piece in enumerate(pieces[1:], 1)]


def products(lefts, rights):
    return tuple(dot_nn(left, right).astype(BF16) for left, right in zip(lefts, rights))


def place_of(block, peers):
    rest = peers // 4
    top = block // rest
    return (top ^ (top >> 1)) + (reverse(block % rest, rest.bit_length() - 1) << 2)


def block_of(place, peers):
    low, rest = place & 3, peers // 4
    return (low ^ (low >> 1)) * rest + reverse(place >> 2, rest.bit_length() - 1)


class UnitsPair:
    def __init__(self, parts, middle, peers):
        self.peers = peers
        self.mine = [(lax.axis_index("dp") >> bit) & 1 for bit in range(2)]

        def blocks(array):
            return array.reshape(peers // 4, 2, 2, array.shape[0] // peers, array.shape[1])

        self.first = [blocks(array[:, :middle]) for array in parts]
        self.second = [blocks(array[:, middle:]) for array in parts]

    def pick(self, parts, axis, bit, offset):
        return [lax.dynamic_index_in_dim(array, self.mine[bit] ^ offset, axis, keepdims=False) for array in parts]

    def cut(self, axes):
        sides = [(self.first, axes[0], self.order[0]), (self.second, axes[1], self.order[1])]
        self.sent = [total([(array,) for array in self.pick(*side, 1)]).astype(BF16) for side in sides]
        self.first, self.second = [self.pick(*side, 0) for side in sides]
        return self.sent

    def start(self):
        self.order = (0, 1)
        return self.cut((2, 1))

    def turn(self):
        self.order = (1, 0)
        return self.cut((1, 1))

    def ship(self):
        got = [swap_chips(sent, 1 << bit, self.peers) for sent, bit in zip(self.sent, self.order)]
        self.first, self.second = self.first + got[:1], self.second + got[1:]
        return got

    def finish(self):
        def rows(array):
            return array.reshape(-1, array.shape[2])

        parts = [(rows(one), rows(two)) for one, two in zip(self.first, self.second)]
        return Units(parts, self.peers, self.peers.bit_length() - 3)


class Units:
    def __init__(self, parts, peers, left):
        self.parts, self.peers, self.left = parts, peers, left

    def cut(self, *behind):
        width = min(2, self.left)
        self.left -= width
        self.low = self.left + 2
        mine = (lax.axis_index("dp") >> self.low) & ((1 << width) - 1)
        size = self.parts[0][0].shape[0] >> width

        def block(array, offset):
            return lax.dynamic_slice_in_dim(array, (mine ^ offset) * size, size, axis=0)

        ranges = [[tuple(block(array, offset) for array in arrays) for arrays in self.parts] for offset in range(1 << width)]
        self.sent = [after(total_low(parts), *behind) for parts in ranges[1:]]
        self.parts = ranges[0]
        return self.sent

    def ship(self):
        got = [swap_chips(sent, offset << self.low, self.peers) for offset, sent in enumerate(self.sent, 1)]
        self.parts = self.parts + [(array,) for array in got]
        return got

    def hold(self, *behind):
        self.parts = self.parts[:-1] + [tuple(after(array, *behind) for array in self.parts[-1])]

    def finish(self):
        while self.left:
            self.cut()
            self.ship()
        return self

    def result(self):
        return total(self.parts)


def one_hot_rows(core, place, inner, peers):
    share = D // (2 * peers)
    core, place = core ^ lax.axis_index("enc"), place ^ lax.axis_index("dp")
    row = (core * peers + place) * share + inner
    return (lax.broadcasted_iota(jnp.int32, (D, D), 1) == row).astype(BF16)


def share_order(peers):
    share = D // (2 * peers)
    row = lax.broadcasted_iota(jnp.int32, (D, 1), 0)
    block = row // share
    return one_hot_rows(block // peers, place_of(block % peers, peers), row % share, peers)


def region_order(peers):
    share, rest = D // (2 * peers), peers // 16
    row = lax.broadcasted_iota(jnp.int32, (D, 1), 0)
    block = row // share
    top = (block // rest) % 4
    place = (top ^ (top >> 1)) + ((block // (8 * rest)) << 2) + (reverse(block % rest, rest.bit_length() - 1) << 4)
    return one_hot_rows((block // (4 * rest)) % 2, place, row % share, peers)


def from_pairs(tensor):
    lead = tensor.shape[0]
    return tensor.reshape(lead, PAIRS, 3, PAIR).transpose(0, 2, 1, 3).reshape(lead, 3 * D)


def exchange(array):
    return lax.all_to_all(array, "dp", split_axis=0, concat_axis=0, tiled=True)


def per_device(
    text_in,
    text_lengths,
    region_feats,
    region_boxes,
    region_dest,
    region_seq,
    w_region,
    w_box,
    type_embed,
    region_gain,
    region_shift,
    w_qkv,
    q_bias,
    v_bias,
    w_out,
    out_bias,
    attn_gain,
    attn_shift,
    w_up,
    up_bias,
    w_down,
    down_bias,
    ffn_gain,
    ffn_shift,
    cot_text,
    cot_region,
):
    peers = lax.axis_size("dp")
    source_rows = region_feats.shape[0]
    capacity = max(2, 2 * source_rows // peers)
    slots = peers * capacity
    text_count = text_in.shape[0]
    units = w_up.shape[1]

    def row(vector):
        return vector.reshape(1, -1)

    outgoing, cot_sent, hot, region_norm, region_inv = region_forward(
        capacity,
        slots,
        region_feats,
        w_region,
        region_boxes,
        row(region_dest),
        row(region_seq),
        w_box,
        type_embed,
        region_gain,
        region_shift,
        cot_region,
    )
    arrived = exchange(outgoing)
    arrived_cot = exchange(cot_sent)

    far_feats = swap_near([region_feats] + [after(region_feats, arrived)] * 3, peers)
    all_feats = jnp.concatenate([region_feats] + far_feats, axis=0)

    bias = jnp.concatenate([q_bias, jnp.zeros_like(q_bias), v_bias])[None]
    perm = share_order(peers)
    qkv_text = (dot_nn(text_in, w_qkv) + bias).astype(BF16)
    qkv_region = (dot_nn(arrived[:, :D], w_qkv) + bias).astype(BF16)
    context, chance, chance_inv = attend(text_lengths, arrived, qkv_text, qkv_region)
    vecs = (out_bias, attn_gain, attn_shift, down_bias, ffn_gain, ffn_shift)
    (
        hidden,
        slope,
        norm,
        inv,
        rows_keep,
        rows_send,
        ctx_keep,
        ctx_send,
        low_keep,
        low_send,
        text_out,
        region_sent,
        d_second,
        d_down,
        ffn_stats,
    ) = feed_forward(context, w_out, text_in, arrived, perm, vecs, w_up, row(up_bias), w_down, cot_text, arrived_cot)

    d_down = after(d_down, *far_feats)
    core = lax.axis_index("enc")
    half = units // 2

    def unit_product(which):
        side = lax.dynamic_slice_in_dim(hidden, which * half, half, axis=1)
        return dot_tn(side, d_down).astype(BF16)

    (got,) = swap_cores([unit_product(1 - core)])
    down = UnitsPair([unit_product(core), got], D // 2, peers)
    covered = after(d_down, *down.start())
    near = down.ship()
    d_up, up_grad, d_mid, d_attn, d_ctx, attn_stats = feed_back(
        covered, slope, w_down, w_up, d_second, norm, inv, attn_gain, w_out
    )
    d_up, d_attn = lax.optimization_barrier((d_up, d_attn, *near))[:2]
    down.turn()
    down.ship()
    down = down.finish()
    got = swap_cores(products([low_send, ctx_send], [d_up, d_attn]))
    up_out = Pair([products([low_keep, ctx_keep], [d_up, d_attn]), tuple(got)], (units + D) // 2, peers)
    sent = up_out.start()
    covered = after(d_ctx, *down.cut(*sent))
    near = up_out.ship()
    far = down.ship()
    d_qkv, qkv_sums, text_grad, d_rows_region = attend_back(
        qkv_text, qkv_region, w_qkv, chance, chance_inv, context, covered, d_mid
    )
    d_qkv = after(d_qkv, *near, *far)
    got = swap_cores(products([rows_send], [d_qkv]))
    qkv_kept = products([rows_keep], [d_qkv])
    qkv = Pair([qkv_kept, tuple(got)], 3 * D // 2, peers)
    sent = qkv.start()
    qkv_got = qkv.ship()
    sent_back = exchange(after(d_rows_region, *sent))
    up_out.hold(*sent)
    up_out.turn()
    up_out = up_out.finish()
    sent_back = after(sent_back, *qkv_got, *qkv.turn())
    qkv = qkv.finish()

    share = D // (2 * peers)
    quarter = units // D
    up_rows = after(up_grad, *qkv_kept).reshape(2 * peers, quarter, share).transpose(1, 0, 2).reshape(quarter, D)
    d_proj, *pieces = region_back(
        sent_back,
        hot,
        region_norm,
        region_inv,
        region_gain,
        region_boxes,
        qkv_sums,
        attn_stats,
        ffn_stats,
        up_rows,
        region_order(peers),
    )
    feats_width = region_feats.shape[1]
    up_out.hold(*pieces)
    qkv.hold(*pieces)
    region_got = swap_near(pieces, peers)
    returned = exchange(after(region_sent, *pieces))
    sent = up_out.cut(1) + qkv.cut(2)
    up_out.ship()
    qkv.ship()
    region_got = [after(array, *sent) for array in region_got]
    pieces = pieces[:1] + region_got
    turned = jnp.concatenate([piece[:, :source_rows] for piece in pieces], axis=1)
    vectors = total([(piece[:, source_rows:],) for piece in pieces]).astype(BF16)
    product = jnp.concatenate([dot_nn(turned, all_feats).astype(BF16), vectors], axis=1)
    middle = product.shape[0] // 2
    last_sent = product[middle:]
    (got,) = swap_cores([last_sent])
    up_out.hold(last_sent)
    up_out.finish(1)
    last_sent, last_got, last = direct([(product[:middle],), (got,)], peers, 4)
    d_proj, returned = lax.optimization_barrier((d_proj, returned, *last_sent))[:2]
    region_out = dot_tn(hot, returned).astype(BF16)
    feats_grad = dot_nt(d_proj, w_region).astype(BF16)
    down.hold(*last_sent)
    down.finish()
    qkv.finish(2)
    turned = last.finish(2).result().T
    vectors = turned[feats_width:]
    return (
        text_out,
        region_out,
        text_grad,
        feats_grad,
        turned[:feats_width],
        vectors[3:7],
        vectors[0],
        vectors[1],
        vectors[2],
        from_pairs(qkv.result()),
        vectors[7],
        vectors[8],
        up_out.result(units),
        vectors[9],
        vectors[10],
        vectors[11],
        up_out.result(0, units),
        vectors[15 : 15 + quarter].reshape(-1),
        down.result(),
        vectors[12],
        vectors[13],
        vectors[14],
    )


def solution(mesh):
    both = ("enc", "dp")
    rows, flat, none = P(both, None), P(both), P()
    in_specs = (rows, rows, rows, P(None, both), rows, flat) + (none,) * 18 + (rows, rows)
    out_specs = (
        (rows,) * 4
        + (P(None, both), P(None, both), flat, flat, flat, rows, flat, flat, rows)
        + (flat, flat, flat, rows, flat, rows, flat, flat, flat)
    )
    return jax.shard_map(per_device, mesh=mesh, in_specs=in_specs, out_specs=out_specs, check_vma=False)
```

```python
import functools
import math

import jax
import jax.numpy as jnp
from jax import lax
from jax.experimental import pallas as pl
from jax.experimental.pallas import tpu as pltpu
from jax.sharding import PartitionSpec as P

D = 768
HEADS = 12
HDIM = 64
PAIR = 2 * HDIM
PAIRS = HEADS // 2
TAGS = 128
VECS = 128

F32 = jnp.float32
BF16 = jnp.bfloat16
eps = 1e-05
SCALE = HDIM ** (-0.5)

TAIL_RATE = 0.3275911 * 0.7071067811865476
TAIL = (0.254829592, -0.284496736, 1.421413741, -1.453152027, 1.061405429)


def dot_nn(left, right):
    return lax.dot_general(left, right, (((1,), (0,)), ((), ())), preferred_element_type=F32)


def dot_nt(left, right):
    return lax.dot_general(left, right, (((1,), (1,)), ((), ())), preferred_element_type=F32)


def dot_tn(left, right):
    return lax.dot_general(left, right, (((0,), (0,)), ((), ())), preferred_element_type=F32)


def standardize(inputs):
    row_mean = jnp.mean(inputs, axis=-1, keepdims=True)
    centred = inputs - row_mean
    spread = jnp.mean(centred * centred, axis=-1, keepdims=True)
    inv = lax.rsqrt(spread + eps)
    return centred * inv, inv


def standardize_back(grad, norm, inv):
    first = jnp.mean(grad, axis=-1, keepdims=True)
    second = jnp.mean(grad * norm, axis=-1, keepdims=True)
    return (grad - first - norm * second) * inv


def row_of(ref):
    return ref[...].reshape(1, D)


def column_sum(inputs):
    return jnp.sum(inputs, axis=0, keepdims=True)


def whole(shape):
    return pl.BlockSpec(shape, lambda *_: (0,) * len(shape), pipeline_mode=pl.Buffered(1))


def struct(shape, dtype):
    return jax.ShapeDtypeStruct(shape, dtype)


def cost(flops, moved, exps=0):
    return pl.CostEstimate(flops=int(flops), bytes_accessed=int(moved), transcendentals=int(exps))


def region_body(
    capacity,
    feats_ref,
    w_ref,
    boxes_ref,
    dest_ref,
    seq_ref,
    w_box_ref,
    type_ref,
    gain_ref,
    shift_ref,
    cot_ref,
    out_ref,
    cot_out_ref,
    hot_ref,
    norm_ref,
    inv_ref,
):
    rows = feats_ref.shape[0]
    slots = out_ref.shape[0]
    dest_row = jnp.broadcast_to(dest_ref[...].astype(F32), (rows, rows))
    dest_col = dest_row.T
    row_io = lax.broadcasted_iota(jnp.int32, (rows, rows), 0)
    col_io = lax.broadcasted_iota(jnp.int32, (rows, rows), 1)
    earlier = jnp.where((dest_col == dest_row) & (row_io < col_io), 1.0, 0.0)
    slot = dest_row[0:1, :] * capacity + column_sum(earlier)
    slot_io = lax.broadcasted_iota(jnp.int32, (slots, rows), 0).astype(F32)
    hot = jnp.where(slot_io == slot, 1.0, 0.0)
    hot_low = hot.astype(BF16)
    hot_ref[...] = hot_low
    cot_out_ref[...] = dot_nn(hot_low, cot_ref[...]).astype(BF16)
    tags = jnp.sum(hot * (seq_ref[...].astype(F32) + 1.0), axis=1, keepdims=True)
    projection = dot_nn(feats_ref[...], w_ref[...])
    boxes = jnp.concatenate([boxes_ref[...], jnp.zeros((4, rows), F32)], axis=0).T
    spatial = boxes[:, 0:1] * w_box_ref[0:1, :]
    for side in range(1, 4):
        spatial = spatial + boxes[:, side : side + 1] * w_box_ref[side : side + 1, :]
    norm, inv = standardize(projection + spatial + row_of(type_ref))
    norm_ref[...] = norm
    inv_ref[...] = inv
    low_rows = (norm * row_of(gain_ref) + row_of(shift_ref)).astype(BF16)
    out_ref[:, :D] = dot_nn(hot_low, low_rows).astype(BF16)
    out_ref[:, D:] = jnp.broadcast_to(tags, (slots, TAGS)).astype(BF16)


def region_forward(capacity, slots, feats, w_region, *others):
    rows, width = feats.shape
    return pl.pallas_call(
        functools.partial(region_body, capacity),
        out_shape=(
            struct((slots, D + TAGS), BF16),
            struct((slots, D), BF16),
            struct((slots, rows), BF16),
            struct((rows, D), F32),
            struct((rows, 1), F32),
        ),
        cost_estimate=cost(2 * rows * width * D, 2 * (rows + D) * width),
        name="region_forward",
    )(feats, w_region, *others)


def head_mask(head):
    lane = lax.broadcasted_iota(jnp.int32, (1, PAIR), 1)
    return (lane >= head * HDIM) & (lane < (head + 1) * HDIM)


def join(*refs):
    return jnp.concatenate([ref[...] for ref in refs], axis=0)


def thirds(rows):
    return [pl.BlockSpec((rows, PAIR), lambda p, *_, part=part: (0, part * PAIRS + p)) for part in range(3)]


def attend_body(
    lengths_ref,
    tag_ref,
    text_q_ref,
    text_k_ref,
    text_v_ref,
    region_q_ref,
    region_k_ref,
    region_v_ref,
    ctx_ref,
    chance_ref,
    inv_ref,
    bias_ref,
):
    text_count, slots = text_q_ref.shape[0], region_q_ref.shape[0]
    count = text_count + slots
    sequences = lengths_ref.shape[1]

    @pl.when(pl.program_id(0) == 0)
    def _():
        place = lax.broadcasted_iota(jnp.int32, (text_count, 1), 0)
        text_seg = jnp.zeros((text_count, 1), F32)
        end = jnp.int32(0)
        for index in range(sequences):
            end = end + lengths_ref[0, index]
            text_seg = text_seg + jnp.where(place >= end, 1.0, 0.0)
        region_seg = tag_ref[:, 0:1].astype(F32) - 1.0
        region_seg = jnp.where(region_seg < 0.0, float(sequences), region_seg)
        seg_col = jnp.concatenate([text_seg, region_seg], axis=0)
        seg_row = jnp.broadcast_to(seg_col, (count, 128)).T[0:1, :]
        bias_ref[...] = jnp.where(seg_col == seg_row, 0.0, -1e30)

    queries = join(text_q_ref, region_q_ref) * jnp.asarray(SCALE, BF16)
    key_rows = join(text_k_ref, region_k_ref)
    values = join(text_v_ref, region_v_ref)
    step = 256
    first = head_mask(0)
    for start in range(0, count, step):
        stop = start + step
        outs, invs = [], []
        for head in range(2):
            q_part = jnp.where(head_mask(head), queries[start:stop], jnp.zeros((), BF16))
            scores = dot_nt(q_part, key_rows) + bias_ref[start:stop, :]
            exp_terms = jnp.exp(scores - jnp.max(scores, axis=1, keepdims=True))
            inv = 1.0 / jnp.sum(exp_terms, axis=1, keepdims=True)
            low_terms = exp_terms.astype(BF16)
            chance_ref[head, start:stop, :] = low_terms
            outs.append(dot_nn(low_terms, values) * inv)
            invs.append(inv)
        ctx_ref[start:stop, :] = jnp.where(first, outs[0], outs[1]).astype(BF16)
        inv_ref[start:stop, :] = jnp.where(first, invs[0], invs[1])


def attend(lengths, arrived, qkv_text, qkv_region):
    text_count, slots = qkv_text.shape[0], qkv_region.shape[0]
    count = text_count + slots
    return pl.pallas_call(
        attend_body,
        grid_spec=pltpu.PrefetchScalarGridSpec(
            num_scalar_prefetch=1,
            grid=(PAIRS,),
            in_specs=[pl.BlockSpec((slots, TAGS), lambda p, *_: (0, D // TAGS))] + thirds(text_count) + thirds(slots),
            out_specs=[
                pl.BlockSpec((count, PAIR), lambda p, *_: (0, p)),
                pl.BlockSpec((2, count, count), lambda p, *_: (p, 0, 0)),
                pl.BlockSpec((count, PAIR), lambda p, *_: (0, p)),
            ],
            scratch_shapes=[pltpu.VMEM((count, count), F32)],
        ),
        out_shape=(
            struct((count, D), BF16),
            struct((HEADS, count, count), BF16),
            struct((count, D), F32),
        ),
        cost_estimate=cost(4 * count * count * D * 4, HEADS * count * count * 2, HEADS * count * count),
        name="attend",
    )(lengths, arrived, *(qkv_text,) * 3, *(qkv_region,) * 3)


def attend_back_body(
    text_q_ref,
    text_k_ref,
    text_v_ref,
    region_q_ref,
    region_k_ref,
    region_v_ref,
    w_q_ref,
    w_k_ref,
    w_v_ref,
    chance_ref,
    inv_ref,
    ctx_ref,
    dctx_ref,
    d_mid_ref,
    rows_turned_ref,
    keep_ref,
    send_ref,
    sum_ref,
    text_grad_ref,
    region_grad_ref,
    total_ref,
    grad_ref,
):
    count = ctx_ref.shape[0]
    text_count = text_q_ref.shape[0]
    queries = join(text_q_ref, region_q_ref) * jnp.asarray(SCALE, BF16)
    key_rows = join(text_k_ref, region_k_ref)
    values = join(text_v_ref, region_v_ref)
    scaled = dctx_ref[...].astype(F32) * inv_ref[...]
    product = scaled * ctx_ref[...].astype(F32)
    scaled_low = scaled.astype(BF16)
    scaled_turned = scaled.T.astype(BF16)
    q_turned = queries.astype(F32).T.astype(BF16)
    step = 256
    first = head_mask(0)
    keys_turned, values_turned = [None, None], [None, None]
    for start in range(0, count, step):
        stop = start + step
        ques = []
        for head in range(2):
            mask = head_mask(head)
            low, high = head * HDIM, (head + 1) * HDIM
            low_terms = chance_ref[head, start:stop, :]
            delta = jnp.sum(jnp.where(mask, product[start:stop], 0.0), axis=1, keepdims=True)
            d_part = jnp.where(mask, scaled_low[start:stop], jnp.zeros((), BF16))
            d_chance = dot_nt(d_part, values)
            d_scores = (low_terms.astype(F32) * (d_chance - delta)).astype(BF16)
            ques.append(dot_nn(d_scores, key_rows))
            v_add = dot_nn(scaled_turned[low:high, start:stop], low_terms)
            k_add = dot_nn(q_turned[low:high, start:stop], d_scores)
            values_turned[head] = v_add if start == 0 else values_turned[head] + v_add
            keys_turned[head] = k_add if start == 0 else keys_turned[head] + k_add
        d_ques = (jnp.where(first, ques[0], ques[1]) * SCALE).astype(BF16)
        grad_ref[start:stop, :PAIR] = d_ques
    grad_ref[:, PAIR : 2 * PAIR] = jnp.concatenate(keys_turned, axis=0).T.astype(BF16)
    d_values = jnp.concatenate(values_turned, axis=0).T.astype(BF16)
    grad_ref[:, 2 * PAIR :] = d_values
    sum_ref[...] = column_sum(grad_ref[...].astype(F32))

    @pl.when(pl.program_id(0) == 0)
    def _():
        total_ref[...] = d_mid_ref[...]

    w_part = jnp.concatenate([w_q_ref[...], w_k_ref[...], w_v_ref[...]], axis=1)
    total_ref[...] += dot_nt(grad_ref[...], w_part)
    half = keep_ref.shape[0]
    keep_ref[...] = dot_nn(rows_turned_ref[:half, :], grad_ref[...]).astype(BF16)
    send_ref[...] = dot_nn(rows_turned_ref[half:, :], grad_ref[...]).astype(BF16)

    @pl.when(pl.program_id(0) == pl.num_programs(0) - 1)
    def _():
        text_grad_ref[...] = total_ref[:text_count, :].astype(BF16)
        region_grad_ref[...] = total_ref[text_count:, :].astype(BF16)


def attend_back(qkv_text, qkv_region, w_qkv, chance, inv, ctx, d_ctx, d_mid, rows_turned):
    text_count, slots = qkv_text.shape[0], qkv_region.shape[0]
    count = text_count + slots
    return pl.pallas_call(
        attend_back_body,
        grid=(PAIRS,),
        in_specs=thirds(text_count)
        + thirds(slots)
        + thirds(D)
        + [
            pl.BlockSpec((2, count, count), lambda p: (p, 0, 0)),
            pl.BlockSpec((count, PAIR), lambda p: (0, p)),
            pl.BlockSpec((count, PAIR), lambda p: (0, p)),
            pl.BlockSpec((count, PAIR), lambda p: (0, p)),
            whole((count, D)),
            whole((D, count)),
        ],
        out_specs=[
            pl.BlockSpec((D // 2, 3 * PAIR), lambda p: (0, p)),
            pl.BlockSpec((D // 2, 3 * PAIR), lambda p: (0, p)),
            pl.BlockSpec((1, 3 * PAIR), lambda p: (0, p)),
            whole((text_count, D)),
            whole((slots, D)),
        ],
        out_shape=(
            struct((D // 2, 3 * D), BF16),
            struct((D // 2, 3 * D), BF16),
            struct((1, 3 * D), F32),
            struct((text_count, D), BF16),
            struct((slots, D), BF16),
        ),
        scratch_shapes=[pltpu.VMEM((count, D), F32), pltpu.VMEM((count, 3 * PAIR), BF16)],
        cost_estimate=cost(8 * count * count * D * 4 + 12 * count * D * D, HEADS * count * count * 2),
        name="attend_back",
    )(*(qkv_text,) * 3, *(qkv_region,) * 3, *(w_qkv,) * 3, chance, inv, ctx, d_ctx, d_mid, rows_turned)


def gelu_parts(inputs):
    weight = jnp.exp(inputs * inputs * (-0.5))
    place = 1.0 / (1.0 + jnp.abs(inputs) * TAIL_RATE)
    poly = TAIL[4]
    for factor in TAIL[3::-1]:
        poly = poly * place + factor
    tail = (0.5 * weight) * (poly * place)
    phi_sum = jnp.where(inputs >= 0.0, 1.0 - tail, tail)
    return inputs * phi_sum, phi_sum + inputs * (weight * 0.3989422804014327)


def feed_body(
    ctx_ref,
    w_out_ref,
    text_ref,
    region_ref,
    perm_ref,
    out_bias_ref,
    attn_gain_ref,
    attn_shift_ref,
    down_bias_ref,
    ffn_gain_ref,
    ffn_shift_ref,
    w_up_ref,
    up_bias_ref,
    w_down_ref,
    cot_text_ref,
    cot_region_ref,
    hidden_ref,
    slope_ref,
    norm_ref,
    inv_ref,
    rows_turned_ref,
    ctx_turned_ref,
    low_turned_ref,
    text_out_ref,
    region_out_ref,
    d_second_ref,
    d_down_ref,
    stats_ref,
    normed_ref,
    low_ref,
    total_ref,
):
    step = pl.program_id(0)
    text_count = text_ref.shape[0]
    count = ctx_ref.shape[0]
    parts = [(start, start + 256) for start in range(0, count, 256)]

    def each(body):
        @pl.loop(0, text_count // 256)
        def _(part):
            rows = pl.ds(pl.multiple_of(part * 256, 256), 256)
            body(rows, 0, rows)

        for start in range(text_count, count, 256):
            body(pl.ds(start, 256), 1, pl.ds(start - text_count, 256))

    @pl.when(step == 0)
    def _():
        def first(rows, side, own):
            inputs = (text_ref, region_ref)[side][own, :]
            ctx = ctx_ref[rows, :]
            attn_out = dot_nn(ctx, w_out_ref[...]) + row_of(out_bias_ref)
            norm, inv = standardize(inputs.astype(F32) + attn_out)
            normed = norm * row_of(attn_gain_ref) + row_of(attn_shift_ref)
            low = normed.astype(BF16)
            norm_ref[rows, :] = norm
            inv_ref[rows, :] = inv
            normed_ref[rows, :] = normed
            low_ref[rows, :] = low
            total_ref[rows, :] = normed + row_of(down_bias_ref)
            rows_turned_ref[:, rows] = dot_nt(perm_ref[...], inputs).astype(BF16)
            ctx_turned_ref[:, rows] = dot_nt(perm_ref[...], ctx).astype(BF16)
            low_turned_ref[:, rows] = dot_nt(perm_ref[...], low).astype(BF16)

        each(first)

    for start, stop in parts:
        up_sum = dot_nn(low_ref[start:stop, :], w_up_ref[...]) + up_bias_ref[...]
        value, slope = gelu_parts(up_sum)
        hidden = value.astype(BF16)
        hidden_ref[start:stop, :] = hidden
        slope_ref[start:stop, :] = slope.astype(BF16)
        total_ref[start:stop, :] += dot_nn(hidden, w_down_ref[...])

    @pl.when(step == pl.num_programs(0) - 1)
    def _():
        stats_ref[...] = jnp.zeros(stats_ref.shape, F32)

        def last(rows, side, own):
            norm, inv = standardize(total_ref[rows, :])
            out_ref = (text_out_ref, region_out_ref)[side]
            out_ref[own, :] = (norm * row_of(ffn_gain_ref) + row_of(ffn_shift_ref)).astype(BF16)
            upstream = (cot_text_ref, cot_region_ref)[side][own, :].astype(F32)
            d_second = standardize_back(upstream * row_of(ffn_gain_ref), norm, inv)
            d_down = d_second.astype(BF16)
            d_second_ref[rows, :] = d_second
            d_down_ref[rows, :] = d_down
            stats_ref[0:1, :] += column_sum(upstream * norm)
            stats_ref[1:2, :] += column_sum(upstream)
            stats_ref[2:3, :] += column_sum(d_down.astype(F32))

        each(last)


def feed_forward(ctx, w_out, text, arrived, perm, vecs, w_up, up_bias, w_down, cot_text, cot_region):
    count, text_count = ctx.shape[0], text.shape[0]
    slots = count - text_count
    units = w_up.shape[1]
    chunk = 512
    half = D // 2
    return pl.pallas_call(
        feed_body,
        grid=(units // chunk,),
        in_specs=[
            whole((count, D)),
            whole((D, D)),
            whole((text_count, D)),
            whole((slots, D)),
            whole((D, D)),
        ]
        + [whole((D,))] * len(vecs)
        + [
            pl.BlockSpec((D, chunk), lambda j: (0, j)),
            pl.BlockSpec((1, chunk), lambda j: (0, j)),
            pl.BlockSpec((chunk, D), lambda j: (j, 0)),
            whole((text_count, D)),
            whole((slots, D)),
        ],
        out_specs=[
            pl.BlockSpec((count, chunk), lambda j: (0, j)),
            pl.BlockSpec((count, chunk), lambda j: (0, j)),
            whole((count, D)),
            whole((count, 1)),
            whole((D, count)),
            whole((D, count)),
            whole((D, count)),
            whole((text_count, D)),
            whole((slots, D)),
            whole((count, D)),
            whole((count, D)),
            whole((8, D)),
        ],
        out_shape=(
            struct((count, units), BF16),
            struct((count, units), BF16),
            struct((count, D), F32),
            struct((count, 1), F32),
            struct((D, count), BF16),
            struct((D, count), BF16),
            struct((D, count), BF16),
            struct((text_count, D), BF16),
            struct((slots, D), BF16),
            struct((count, D), F32),
            struct((count, D), BF16),
            struct((8, D), F32),
        ),
        scratch_shapes=[
            pltpu.VMEM((count, D), F32),
            pltpu.VMEM((count, D), BF16),
            pltpu.VMEM((count, D), F32),
        ],
        cost_estimate=cost(4 * count * D * units + 8 * count * D * D, 4 * D * units + 4 * count * units, count * units),
        name="feed_forward",
    )(ctx, w_out, text, arrived, perm, *vecs, w_up, up_bias, w_down, cot_text, cot_region)


def feed_back_body(
    d_down_ref,
    slope_ref,
    w_down_ref,
    w_up_ref,
    d_second_ref,
    norm_ref,
    inv_ref,
    gain_ref,
    w_out_ref,
    low_turned_ref,
    ctx_turned_ref,
    up_keep_ref,
    up_send_ref,
    out_keep_ref,
    out_send_ref,
    up_sum_ref,
    d_mid_ref,
    d_ctx_ref,
    stats_ref,
    total_ref,
    d_up_ref,
    d_attn_ref,
):
    step = pl.program_id(0)
    count = d_down_ref.shape[0]
    parts = [(start, start + 256) for start in range(0, count, 256)]

    @pl.when(step == 0)
    def _():
        total_ref[...] = d_second_ref[...]

    up_total = jnp.zeros(up_sum_ref.shape, F32)
    for start, stop in parts:
        d_hidden = dot_nt(d_down_ref[start:stop, :], w_down_ref[...])
        d_up = (d_hidden * slope_ref[start:stop, :].astype(F32)).astype(BF16)
        d_up_ref[start:stop, :] = d_up
        up_total = up_total + column_sum(d_up.astype(F32))
        total_ref[start:stop, :] += dot_nt(d_up, w_up_ref[...])
    up_sum_ref[...] = up_total
    half = up_keep_ref.shape[0]
    up_keep_ref[...] = dot_nn(low_turned_ref[:half, :], d_up_ref[...]).astype(BF16)
    up_send_ref[...] = dot_nn(low_turned_ref[half:, :], d_up_ref[...]).astype(BF16)

    @pl.when(step == pl.num_programs(0) - 1)
    def _():
        stats_ref[...] = jnp.zeros(stats_ref.shape, F32)

        @pl.loop(0, len(parts))
        def _(part):
            rows = pl.ds(pl.multiple_of(part * 256, 256), 256)
            d_first = total_ref[rows, :]
            norm = norm_ref[rows, :]
            d_mid = standardize_back(d_first * row_of(gain_ref), norm, inv_ref[rows, :])
            d_attn = d_mid.astype(BF16)
            d_mid_ref[rows, :] = d_mid
            d_attn_ref[rows, :] = d_attn
            d_ctx_ref[rows, :] = dot_nt(d_attn, w_out_ref[...]).astype(BF16)
            stats_ref[0:1, :] += column_sum(d_first * norm)
            stats_ref[1:2, :] += column_sum(d_first)
            stats_ref[2:3, :] += column_sum(d_attn.astype(F32))

        out_keep_ref[...] = dot_nn(ctx_turned_ref[:half, :], d_attn_ref[...]).astype(BF16)
        out_send_ref[...] = dot_nn(ctx_turned_ref[half:, :], d_attn_ref[...]).astype(BF16)


def feed_back(d_down, slope, w_down, w_up, d_second, norm, inv, gain, w_out, low_turned, ctx_turned):
    count, units = slope.shape
    chunk = 512
    return pl.pallas_call(
        feed_back_body,
        grid=(units // chunk,),
        in_specs=[
            whole((count, D)),
            pl.BlockSpec((count, chunk), lambda j: (0, j)),
            pl.BlockSpec((chunk, D), lambda j: (j, 0)),
            pl.BlockSpec((D, chunk), lambda j: (0, j)),
            whole((count, D)),
            whole((count, D)),
            whole((count, 1)),
            whole((D,)),
            whole((D, D)),
            whole((D, count)),
            whole((D, count)),
        ],
        out_specs=[
            pl.BlockSpec((D // 2, chunk), lambda j: (0, j)),
            pl.BlockSpec((D // 2, chunk), lambda j: (0, j)),
            whole((D // 2, D)),
            whole((D // 2, D)),
            pl.BlockSpec((1, chunk), lambda j: (0, j)),
            whole((count, D)),
            whole((count, D)),
            whole((8, D)),
        ],
        out_shape=(
            struct((D // 2, units), BF16),
            struct((D // 2, units), BF16),
            struct((D // 2, D), BF16),
            struct((D // 2, D), BF16),
            struct((1, units), F32),
            struct((count, D), F32),
            struct((count, D), BF16),
            struct((8, D), F32),
        ),
        scratch_shapes=[
            pltpu.VMEM((count, D), F32),
            pltpu.VMEM((count, chunk), BF16),
            pltpu.VMEM((count, D), BF16),
        ],
        cost_estimate=cost(6 * count * D * units + 4 * count * D * D, 4 * D * units + 4 * count * units),
        name="feed_back",
    )(d_down, slope, w_down, w_up, d_second, norm, inv, gain, w_out, low_turned, ctx_turned)


def region_back_body(
    back_ref,
    hot_ref,
    norm_ref,
    inv_ref,
    gain_ref,
    boxes_ref,
    qkv_ref,
    attn_ref,
    ffn_ref,
    up_ref,
    perm_ref,
    d_proj_ref,
    *piece_refs,
):
    rows = norm_ref.shape[0]
    d_region = dot_tn(hot_ref[...], back_ref[...])
    norm = norm_ref[...]
    d_pre = standardize_back(d_region * row_of(gain_ref), norm, inv_ref[...])
    d_proj = d_pre.astype(BF16)
    d_proj_ref[...] = d_proj
    boxes = jnp.concatenate([boxes_ref[...], jnp.zeros((4, rows), F32)], axis=0).T
    vectors = [column_sum(d_pre), column_sum(d_region * norm), column_sum(d_region)]
    vectors += [column_sum(boxes[:, side : side + 1] * d_pre) for side in range(4)]
    for part in (0, 2):
        starts = [(3 * pair + part) * PAIR for pair in range(PAIRS)]
        vectors.append(jnp.concatenate([qkv_ref[:, start : start + PAIR] for start in starts], axis=1))
    for ref in (attn_ref, ffn_ref):
        vectors += [ref[2:3, :], ref[0:2, :]]
    vectors.append(up_ref[...])
    filled = sum(vector.shape[0] for vector in vectors)
    vectors.append(jnp.zeros((VECS - filled, D), F32))
    low_vectors = jnp.concatenate(vectors, axis=0).astype(BF16)
    turned = dot_nt(perm_ref[...], jnp.concatenate([d_proj, low_vectors], axis=0)).astype(BF16)
    size = D // len(piece_refs)
    for index, piece_ref in enumerate(piece_refs):
        piece_ref[...] = turned[index * size : (index + 1) * size]


def region_back(back, hot, norm, *others):
    rows = norm.shape[0]
    return pl.pallas_call(
        region_back_body,
        out_shape=(struct((rows, D), BF16),) + (struct((D // 4, rows + VECS), BF16),) * 4,
        cost_estimate=cost(0, 0),
        name="region_back",
    )(back, hot, norm, *others)


def swap_cores(sent):
    return lax.ppermute(sent, "enc", [(0, 1), (1, 0)])


def swap_chips(sent, offset, peers):
    return lax.ppermute(sent, "dp", [(peer, peer ^ offset) for peer in range(peers)])


MASKS = (0, 1, 3, 2)


def reverse(value, width):
    result = value & 0
    for bit in range(width):
        result = result | (((value >> bit) & 1) << (width - 1 - bit))
    return result


def after(first, *others):
    if not others:
        return first
    return lax.optimization_barrier((first,) + others)[0]


def swap_cores(sent):
    return [lax.ppermute(array, "enc", [(0, 1), (1, 0)]) for array in sent]


def swap_chips(sent, mask, peers):
    return lax.ppermute(sent, "dp", [(peer, peer ^ mask) for peer in range(peers)])


def combine_body(plans, counts, *refs):
    refs, out_refs = refs[:counts], refs[counts:]
    for out_ref, (unit, segments) in zip(out_refs, plans):

        def add(start, size, segments=segments, out_ref=out_ref):
            for place, at, terms in segments:
                sums = [refs[index][pl.ds(start, size), left:right].astype(F32) for index, left, right in terms]
                value = functools.reduce(jnp.add, sums).astype(out_ref.dtype)
                out_ref[pl.ds(place + start, size), at : at + value.shape[1]] = value

        if unit % 32 or unit < 64:
            add(0, unit)
        else:

            @pl.loop(0, unit // 32)
            def _(step, add=add):
                add(pl.multiple_of(step * 32, 32), 32)


def segments_of(terms, columns):
    edges = set()
    for array, _, first in terms:
        edges |= {first, first + array.shape[1]}
    for left, right in columns:
        inside = sorted({left, right} | {edge for edge in edges if left < edge < right})
        yield from zip(inside, inside[1:])


def combine_plain(terms, start, stop, columns, dtype):
    sums = []
    for left, right in segments_of(terms, columns):
        blocks = [
            array[row + start : row + stop, left - first : right - first].astype(F32)
            for array, row, first in terms
            if first <= left and right <= first + array.shape[1]
        ]
        sums.append(functools.reduce(jnp.add, blocks))
    return jnp.concatenate(sums, axis=1).astype(dtype)


def combine(wanted, name):
    plans, operands, specs, shapes, known = [], [], [], [], {}
    for terms, start, stop, columns, dtype in wanted:
        unit = functools.reduce(math.gcd, [value for _, row, _ in terms for value in (row + start, row + stop)])
        if unit % 8:
            return [combine_plain(*each) for each in wanted]
        segments = []
        for place in range(0, stop - start, unit):
            at = 0
            for left, right in segments_of(terms, columns):
                sources = []
                for array, row, first in terms:
                    if first <= left and right <= first + array.shape[1]:
                        block = (row + start + place) // unit
                        key = (id(array), unit, block)
                        if key not in known:
                            known[key] = len(operands)
                            operands.append(array)
                            specs.append(pl.BlockSpec((unit, array.shape[1]), lambda j, block=block: (block, 0)))
                        sources.append((known[key], left - first, right - first))
                segments.append((place, at, sources))
                at += right - left
        plans.append((unit, segments))
        shapes.append(struct((stop - start, at), dtype))
    return pl.pallas_call(
        functools.partial(combine_body, plans, len(operands)),
        grid=(1,),
        in_specs=specs,
        out_specs=[pl.BlockSpec(shape.shape, lambda j: (0, 0)) for shape in shapes],
        out_shape=tuple(shapes),
        cost_estimate=cost(0, 0),
        name=name,
    )(*operands)


def side_by_side(*arrays):
    terms, first = [], 0
    for array in arrays:
        terms.append((array, 0, first))
        first += array.shape[1]
    return terms


class Pair:
    def __init__(self, terms, rows, middle, width, peers):
        self.terms, self.size, self.middle, self.width, self.peers = terms, rows // 4, middle, width, peers
        self.sides = [(0, middle)], [(middle, width)]

    def start(self):
        size, (first, second) = self.size, self.sides
        wanted = [(self.terms, size, 3 * size, first, BF16), (self.terms, 2 * size, 4 * size, second, BF16)]
        self.sent = list(combine(wanted, "pair_start"))
        return self.sent

    def ship(self):
        self.got = [swap_chips(sent, bit, self.peers) for sent, bit in zip(self.sent, (1, 2))]
        return self.got

    def hold(self, *behind):
        self.got = [after(array, *behind) for array in self.got]

    def turn(self):
        size, (first, second), (one, two) = self.size, self.sides, self.got
        wanted = [
            (self.terms + [(one, -2 * size, 0)], 3 * size, 4 * size, first, BF16),
            (self.terms + [(two, -size, self.middle)], size, 2 * size, second, BF16),
        ]
        self.sent = list(combine(wanted, "pair_turn"))
        return self.sent

    def finish(self):
        last = [swap_chips(sent, bit, self.peers) for sent, bit in zip(self.sent, (2, 1))]
        (one, two), middle = self.got, self.middle
        arrived = [(one, 0, 0), (two, self.size, middle), (last[0], 0, 0), (last[1], 0, middle)]
        return Scatter(self.terms + arrived, self.size, self.width, self.peers, 2, 2)


class Scatter:
    def __init__(self, terms, rows, width, peers, bit, fresh):
        self.terms, self.rows, self.width, self.peers, self.bit, self.fresh = terms, rows, width, peers, bit, fresh

    def cut(self, bits, *behind):
        self.bits = min(bits, self.peers.bit_length() - 1 - self.bit)
        self.rows >>= self.bits
        wanted = [
            (self.terms, offset * self.rows, (offset + 1) * self.rows, [(0, self.width)], BF16)
            for offset in range(1, 1 << self.bits)
        ]
        self.sent = [after(array, *behind) for array in combine(wanted, "cut")]
        return self.sent

    def ship(self):
        masks = [reverse(offset, self.bits) << self.bit for offset in range(1, 1 << self.bits)]
        got = [swap_chips(sent, mask, self.peers) for sent, mask in zip(self.sent, masks)]
        self.terms = self.terms + side_by_side_rows(got)
        self.bit += self.bits
        self.fresh = len(got)
        return got

    def hold(self, *behind):
        late = [(after(array, *behind), row, first) for array, row, first in self.terms[-self.fresh :]]
        self.terms = self.terms[: -self.fresh] + late

    def finish(self, bits):
        while 1 << self.bit < self.peers:
            self.cut(bits)
            self.ship()
        return self

    def shares(self, *ranges):
        return [(self.terms, 0, self.rows, columns, F32) for columns in ranges]


def side_by_side_rows(arrays):
    return [(array, 0, 0) for array in arrays]


def direct(terms, rows, width, peers, bit):
    size = rows // 4
    wanted = [(terms, place * size, (place + 1) * size, [(0, width)], BF16) for place in range(1, 4)]
    sent = combine(wanted, "direct")
    got = [swap_chips(array, mask, peers) for array, mask in zip(sent, MASKS[1:])]
    return sent, Scatter(terms + side_by_side_rows(got), size, width, peers, bit, 3)


def swap_near(pieces, peers):
    return [swap_chips(piece, offset << 2, peers) for offset, piece in enumerate(pieces[1:], 1)]


def place_of(block, peers):
    rest = peers // 4
    top = block // rest
    return (top ^ (top >> 1)) + (reverse(block % rest, rest.bit_length() - 1) << 2)


def units_body(order_ref, *refs):
    kept, got = refs[:-3:2], refs[1:-3:2]
    near_ref, far_ref, keep_ref = refs[-3:]
    step, half = pl.program_id(0), near_ref.shape[1]
    rows = [(one[...].astype(F32) + two[...].astype(F32)).astype(BF16) for one, two in zip(kept, got)]
    rows = jnp.concatenate(rows, axis=0)
    keep_ref[...] = rows

    @pl.when((step == 1) | (step == 2))
    def _():
        near_ref[...] = rows[:, :half]

    @pl.when(step >= 2)
    def _():
        far_ref[...] = rows[:, half:]


def cut_units(kept, got, order, peers):
    count, width = kept.shape
    size, half, rest = count // peers, width // 2, peers // 4
    if size % 16:
        rows = (kept.astype(F32) + got.astype(F32)).reshape(peers, size, width)
        rows = jnp.take(rows, order, axis=0).reshape(count, width).astype(BF16)
        return rows[count // 4 : 3 * count // 4, :half], rows[count // 2 :, half:], rows
    specs = []
    for index in range(rest):
        specs += [pl.BlockSpec((size, width), lambda j, order, index=index: (order[j * rest + index], 0))] * 2
    return pl.pallas_call(
        units_body,
        grid_spec=pltpu.PrefetchScalarGridSpec(
            num_scalar_prefetch=1,
            grid=(4,),
            in_specs=specs,
            out_specs=[
                pl.BlockSpec((count // 4, half), lambda j, order: (jnp.clip(j - 1, 0, 1), 0)),
                pl.BlockSpec((count // 4, half), lambda j, order: (jnp.clip(j - 2, 0, 1), 0)),
                pl.BlockSpec((count // 4, width), lambda j, order: (j, 0)),
            ],
        ),
        out_shape=(struct((count // 2, half), BF16), struct((count // 2, half), BF16), struct((count, width), BF16)),
        cost_estimate=cost(count * width, 8 * count * width),
        name="cut_units",
    )(order, *(kept, got) * rest)


def region_product_body(*refs):
    *refs, keep_ref, send_ref = refs
    pieces, feats = refs[: len(refs) // 2], refs[len(refs) // 2 :]
    rows, width = feats[0].shape
    half = keep_ref.shape[0]
    turned = jnp.concatenate([piece[:, :rows] for piece in pieces], axis=1)
    vectors = functools.reduce(jnp.add, [piece[:, rows:].astype(F32) for piece in pieces])
    product = dot_nn(turned, jnp.concatenate([ref[...] for ref in feats], axis=0)).astype(BF16)
    for ref, start in ((keep_ref, 0), (send_ref, half)):
        ref[:, :width] = product[start : start + half]
        ref[:, width:] = vectors[start : start + half].astype(BF16)


def region_product(pieces, feats):
    half, width = pieces[0].shape[0] // 2, feats[0].shape[1] + VECS
    return pl.pallas_call(
        region_product_body,
        out_shape=(struct((half, width), BF16), struct((half, width), BF16)),
        cost_estimate=cost(0, 0),
        name="region_product",
    )(*pieces, *feats)


def one_hot_rows(core, place, inner, peers):
    share = D // (2 * peers)
    core, place = core ^ lax.axis_index("enc"), place ^ lax.axis_index("dp")
    row = (core * peers + place) * share + inner
    return (lax.broadcasted_iota(jnp.int32, (D, D), 1) == row).astype(BF16)


def share_order(peers):
    share = D // (2 * peers)
    row = lax.broadcasted_iota(jnp.int32, (D, 1), 0)
    block = row // share
    return one_hot_rows(block // peers, place_of(block % peers, peers), row % share, peers)


def region_order(peers):
    share, rest = D // (2 * peers), peers // 16
    row = lax.broadcasted_iota(jnp.int32, (D, 1), 0)
    block = row // share
    top = (block // rest) % 4
    place = (top ^ (top >> 1)) + ((block // (8 * rest)) << 2) + (reverse(block % rest, rest.bit_length() - 1) << 4)
    return one_hot_rows((block // (4 * rest)) % 2, place, row % share, peers)


def exchange(array):
    return lax.all_to_all(array, "dp", split_axis=0, concat_axis=0, tiled=True)


def per_device(
    text_in,
    text_lengths,
    region_feats,
    region_boxes,
    region_dest,
    region_seq,
    w_region,
    w_box,
    type_embed,
    region_gain,
    region_shift,
    w_qkv,
    q_bias,
    v_bias,
    w_out,
    out_bias,
    attn_gain,
    attn_shift,
    w_up,
    up_bias,
    w_down,
    down_bias,
    ffn_gain,
    ffn_shift,
    cot_text,
    cot_region,
):
    peers = lax.axis_size("dp")
    source_rows = region_feats.shape[0]
    capacity = max(2, 2 * source_rows // peers)
    slots = peers * capacity
    text_count = text_in.shape[0]
    units = w_up.shape[1]

    def row(vector):
        return vector.reshape(1, -1)

    outgoing, cot_sent, hot, region_norm, region_inv = region_forward(
        capacity,
        slots,
        region_feats,
        w_region,
        region_boxes,
        row(region_dest),
        row(region_seq),
        w_box,
        type_embed,
        region_gain,
        region_shift,
        cot_region,
    )
    arrived = exchange(outgoing)
    arrived_cot = exchange(cot_sent)

    far_feats = swap_near([region_feats] + [after(region_feats, arrived)] * 3, peers)

    bias = jnp.concatenate([q_bias, jnp.zeros_like(q_bias), v_bias])[None]
    perm, region_perm = lax.optimization_barrier((share_order(peers), region_order(peers)))
    order = place_of(jnp.arange(peers, dtype=jnp.int32), peers) ^ lax.axis_index("dp")
    qkv_text = (dot_nn(text_in, w_qkv) + bias).astype(BF16)
    qkv_region = (dot_nn(arrived[:, :D], w_qkv) + bias).astype(BF16)
    context, chance, chance_inv = attend(text_lengths, arrived, qkv_text, qkv_region)
    vecs = (out_bias, attn_gain, attn_shift, down_bias, ffn_gain, ffn_shift)
    (
        hidden,
        slope,
        norm,
        inv,
        rows_turned,
        ctx_turned,
        low_turned,
        text_out,
        region_sent,
        d_second,
        d_down,
        ffn_stats,
    ) = feed_forward(context, w_out, text_in, arrived, perm, vecs, w_up, row(up_bias), w_down, cot_text, arrived_cot)

    d_down = after(d_down, *far_feats)
    core = lax.axis_index("enc")
    half = units // 2

    def unit_product(which):
        side = lax.dynamic_slice_in_dim(hidden, which * half, half, axis=1)
        return dot_tn(side, d_down).astype(BF16)

    (got,) = swap_cores([unit_product(1 - core)])
    *sent, kept = cut_units(unit_product(core), got, order, peers)
    down = Pair([(kept, 0, 0)], half, D // 2, D, peers)
    down.sent = sent
    covered = after(d_down, *sent)
    near = down.ship()
    up_keep, up_send, out_keep, out_send, up_grad, d_mid, d_ctx, attn_stats = feed_back(
        covered, slope, w_down, w_up, d_second, norm, inv, attn_gain, w_out, low_turned, ctx_turned
    )
    up_send, out_send = lax.optimization_barrier((up_send, out_send, *near))[:2]
    got = swap_cores([up_send, out_send])
    down_sent = down.turn()
    down = down.finish()
    down_got = [array for array, _, _ in down.terms[-down.fresh :]]
    up_out = Pair(
        side_by_side(up_keep, out_keep) + side_by_side(*got), D // 2, (units + D) // 2, units + D, peers
    )
    returned = exchange(after(region_sent, *down_sent))
    covered = after(d_ctx, returned, *up_out.start())
    near = up_out.ship()
    qkv_keep, qkv_send, qkv_sums, text_grad, d_rows_region = attend_back(
        qkv_text, qkv_region, w_qkv, chance, chance_inv, context, covered, d_mid, rows_turned
    )
    qkv_send = after(qkv_send, *near, *down_got)
    (got,) = swap_cores([qkv_send])
    sent_back = exchange(after(d_rows_region, qkv_send))
    qkv = Pair([(qkv_keep, 0, 0), (got, 0, 0)], D // 2, 3 * D // 2, 3 * D, peers)
    sent = qkv.start()
    qkv_got = qkv.ship()
    up_out.hold(*sent)
    sent = up_out.turn()
    up_out = up_out.finish()
    down.hold(*sent)
    sent_back = after(sent_back, *qkv_got, *down.cut(1))
    down.ship()
    qkv.hold(sent_back)
    qkv_sent = qkv.turn()
    qkv = qkv.finish()

    share = D // (2 * peers)
    quarter = units // D
    up_rows = after(up_grad, *sent).reshape(2 * peers, quarter, share).transpose(1, 0, 2).reshape(quarter, D)
    d_proj, *pieces = region_back(
        sent_back,
        hot,
        region_norm,
        region_inv,
        region_gain,
        region_boxes,
        qkv_sums,
        attn_stats,
        ffn_stats,
        up_rows,
        region_perm,
    )
    feats_width = region_feats.shape[1]
    up_out.hold(*pieces)
    qkv.hold(*pieces)
    down.hold(*pieces)
    region_got = swap_near(pieces, peers)
    qkv_sent = qkv_sent + up_out.cut(1)
    up_out.ship()
    region_got = [after(array, *qkv_sent) for array in region_got]
    last_keep, last_send = region_product(pieces[:1] + region_got, [region_feats] + far_feats)
    (got,) = swap_cores([last_send])
    qkv.hold(last_send)
    down.hold(last_send)
    qkv.cut(1)
    qkv.ship()
    down.finish(1)
    last_sent, last = direct(
        [(last_keep, 0, 0), (got, 0, 0)], last_keep.shape[0], feats_width + VECS, peers, 4
    )
    qkv.hold(*last_sent)
    up_out.hold(*last_sent)
    down.hold(*last_sent)
    d_proj, returned = lax.optimization_barrier((d_proj, returned, *last_sent))[:2]
    region_out = dot_tn(hot, returned).astype(BF16)
    feats_grad = dot_nt(d_proj, w_region).astype(BF16)
    starts = [(3 * pair + part) * PAIR for part in range(3) for pair in range(PAIRS)]
    heads = [(start, start + PAIR) for start in starts]
    w_qkv_share, w_up_share, w_out_share, w_down_share = combine(
        qkv.finish(1).shares(heads)
        + up_out.finish(1).shares([(0, units)], [(units, units + D)])
        + down.finish(1).shares([(0, D)]),
        "shares",
    )
    w_region_share, vectors = combine(
        last.finish(2).shares([(0, feats_width)], [(feats_width, feats_width + VECS)]), "last_shares"
    )
    vectors = vectors.T
    return (
        text_out,
        region_out,
        text_grad,
        feats_grad,
        w_region_share.T,
        vectors[3:7],
        vectors[0],
        vectors[1],
        vectors[2],
        w_qkv_share,
        vectors[7],
        vectors[8],
        w_out_share,
        vectors[9],
        vectors[10],
        vectors[11],
        w_up_share,
        vectors[15 : 15 + quarter].reshape(-1),
        w_down_share,
        vectors[12],
        vectors[13],
        vectors[14],
    )


def solution(mesh):
    both = ("enc", "dp")
    rows, flat, none = P(both, None), P(both), P()
    in_specs = (rows, rows, rows, P(None, both), rows, flat) + (none,) * 18 + (rows, rows)
    out_specs = (
        (rows,) * 4
        + (P(None, both), P(None, both), flat, flat, flat, rows, flat, flat, rows)
        + (flat, flat, flat, rows, flat, rows, flat, flat, flat)
    )
    return jax.shard_map(per_device, mesh=mesh, in_specs=in_specs, out_specs=out_specs, check_vma=False)
```

```python
import functools
import math

import jax
import jax.numpy as jnp
from jax import lax
from jax.experimental import pallas as pl
from jax.experimental.pallas import tpu as pltpu
from jax.sharding import PartitionSpec as P

D = 768
HEADS = 12
HDIM = 64
PAIR = 2 * HDIM
PAIRS = HEADS // 2
TAGS = 128
VECS = 128

F32 = jnp.float32
BF16 = jnp.bfloat16
eps = 1e-05
SCALE = HDIM ** (-0.5)

TAIL_RATE = 0.3275911 * 0.7071067811865476
TAIL = (0.254829592, -0.284496736, 1.421413741, -1.453152027, 1.061405429)


def dot_nn(left, right):
    return lax.dot_general(left, right, (((1,), (0,)), ((), ())), preferred_element_type=F32)


def dot_nt(left, right):
    return lax.dot_general(left, right, (((1,), (1,)), ((), ())), preferred_element_type=F32)


def dot_tn(left, right):
    return lax.dot_general(left, right, (((0,), (0,)), ((), ())), preferred_element_type=F32)


def standardize(inputs):
    row_mean = jnp.mean(inputs, axis=-1, keepdims=True)
    centred = inputs - row_mean
    spread = jnp.mean(centred * centred, axis=-1, keepdims=True)
    inv = lax.rsqrt(spread + eps)
    return centred * inv, inv


def standardize_back(grad, norm, inv):
    first = jnp.mean(grad, axis=-1, keepdims=True)
    second = jnp.mean(grad * norm, axis=-1, keepdims=True)
    return (grad - first - norm * second) * inv


def row_of(ref):
    return ref[...].reshape(1, D)


def column_sum(inputs):
    return jnp.sum(inputs, axis=0, keepdims=True)


def whole(shape):
    return pl.BlockSpec(shape, lambda *_: (0,) * len(shape), pipeline_mode=pl.Buffered(1))


def struct(shape, dtype):
    return jax.ShapeDtypeStruct(shape, dtype)


def cost(flops, moved, exps=0):
    return pl.CostEstimate(flops=int(flops), bytes_accessed=int(moved), transcendentals=int(exps))


def region_body(
    capacity,
    feats_ref,
    w_ref,
    boxes_ref,
    dest_ref,
    seq_ref,
    w_box_ref,
    type_ref,
    gain_ref,
    shift_ref,
    cot_ref,
    out_ref,
    cot_out_ref,
    hot_ref,
    norm_ref,
    inv_ref,
):
    rows = feats_ref.shape[0]
    slots = out_ref.shape[0]
    dest_row = jnp.broadcast_to(dest_ref[...].astype(F32), (rows, rows))
    dest_col = dest_row.T
    row_io = lax.broadcasted_iota(jnp.int32, (rows, rows), 0)
    col_io = lax.broadcasted_iota(jnp.int32, (rows, rows), 1)
    earlier = jnp.where((dest_col == dest_row) & (row_io < col_io), 1.0, 0.0)
    slot = dest_row[0:1, :] * capacity + column_sum(earlier)
    slot_io = lax.broadcasted_iota(jnp.int32, (slots, rows), 0).astype(F32)
    hot = jnp.where(slot_io == slot, 1.0, 0.0)
    hot_low = hot.astype(BF16)
    hot_ref[...] = hot_low
    cot_out_ref[...] = dot_nn(hot_low, cot_ref[...]).astype(BF16)
    tags = jnp.sum(hot * (seq_ref[...].astype(F32) + 1.0), axis=1, keepdims=True)
    projection = dot_nn(feats_ref[...], w_ref[...])
    boxes = jnp.concatenate([boxes_ref[...], jnp.zeros((4, rows), F32)], axis=0).T
    spatial = boxes[:, 0:1] * w_box_ref[0:1, :]
    for side in range(1, 4):
        spatial = spatial + boxes[:, side : side + 1] * w_box_ref[side : side + 1, :]
    norm, inv = standardize(projection + spatial + row_of(type_ref))
    norm_ref[...] = norm
    inv_ref[...] = inv
    low_rows = (norm * row_of(gain_ref) + row_of(shift_ref)).astype(BF16)
    out_ref[:, :D] = dot_nn(hot_low, low_rows).astype(BF16)
    out_ref[:, D:] = jnp.broadcast_to(tags, (slots, TAGS)).astype(BF16)


def region_forward(capacity, slots, feats, w_region, *others):
    rows, width = feats.shape
    return pl.pallas_call(
        functools.partial(region_body, capacity),
        out_shape=(
            struct((slots, D + TAGS), BF16),
            struct((slots, D), BF16),
            struct((slots, rows), BF16),
            struct((rows, D), F32),
            struct((rows, 1), F32),
        ),
        cost_estimate=cost(2 * rows * width * D, 2 * (rows + D) * width),
        name="region_forward",
    )(feats, w_region, *others)


def head_mask(head):
    lane = lax.broadcasted_iota(jnp.int32, (1, PAIR), 1)
    return (lane >= head * HDIM) & (lane < (head + 1) * HDIM)


def join(*refs):
    return jnp.concatenate([ref[...] for ref in refs], axis=0)


def thirds(rows):
    return [pl.BlockSpec((rows, PAIR), lambda p, *_, part=part: (0, part * PAIRS + p)) for part in range(3)]


def attend_body(
    lengths_ref,
    tag_ref,
    text_q_ref,
    text_k_ref,
    text_v_ref,
    region_q_ref,
    region_k_ref,
    region_v_ref,
    ctx_ref,
    chance_ref,
    inv_ref,
    bias_ref,
):
    text_count, slots = text_q_ref.shape[0], region_q_ref.shape[0]
    count = text_count + slots
    sequences = lengths_ref.shape[1]

    @pl.when(pl.program_id(0) == 0)
    def _():
        place = lax.broadcasted_iota(jnp.int32, (text_count, 1), 0)
        text_seg = jnp.zeros((text_count, 1), F32)
        end = jnp.int32(0)
        for index in range(sequences):
            end = end + lengths_ref[0, index]
            text_seg = text_seg + jnp.where(place >= end, 1.0, 0.0)
        region_seg = tag_ref[:, 0:1].astype(F32) - 1.0
        region_seg = jnp.where(region_seg < 0.0, float(sequences), region_seg)
        seg_col = jnp.concatenate([text_seg, region_seg], axis=0)
        seg_row = jnp.broadcast_to(seg_col, (count, 128)).T[0:1, :]
        bias_ref[...] = jnp.where(seg_col == seg_row, 0.0, -1e30)

    queries = join(text_q_ref, region_q_ref) * jnp.asarray(SCALE, BF16)
    key_rows = join(text_k_ref, region_k_ref)
    values = join(text_v_ref, region_v_ref)
    step = 256
    first = head_mask(0)
    tasks = [(start, head) for start in range(0, count, step) for head in range(2)]

    def scores_of(start, head):
        q_part = jnp.where(head_mask(head), queries[start : start + step], jnp.zeros((), BF16))
        return dot_nt(q_part, key_rows)

    following, outs, invs = scores_of(*tasks[0]), [], []
    for index, (start, head) in enumerate(tasks):
        stop = start + step
        scores = following + bias_ref[start:stop, :]
        if index + 1 < len(tasks):
            following = scores_of(*tasks[index + 1])
        exp_terms = jnp.exp(scores - jnp.max(scores, axis=1, keepdims=True))
        inv = 1.0 / jnp.sum(exp_terms, axis=1, keepdims=True)
        low_terms = exp_terms.astype(BF16)
        chance_ref[head, start:stop, :] = low_terms
        outs.append(dot_nn(low_terms, values) * inv)
        invs.append(inv)
        if head == 1:
            ctx_ref[start:stop, :] = jnp.where(first, outs[0], outs[1]).astype(BF16)
            inv_ref[start:stop, :] = jnp.where(first, invs[0], invs[1])
            outs, invs = [], []


def attend(lengths, arrived, qkv_text, qkv_region):
    text_count, slots = qkv_text.shape[0], qkv_region.shape[0]
    count = text_count + slots
    return pl.pallas_call(
        attend_body,
        grid_spec=pltpu.PrefetchScalarGridSpec(
            num_scalar_prefetch=1,
            grid=(PAIRS,),
            in_specs=[pl.BlockSpec((slots, TAGS), lambda p, *_: (0, D // TAGS))] + thirds(text_count) + thirds(slots),
            out_specs=[
                pl.BlockSpec((count, PAIR), lambda p, *_: (0, p)),
                pl.BlockSpec((2, count, count), lambda p, *_: (p, 0, 0)),
                pl.BlockSpec((count, PAIR), lambda p, *_: (0, p)),
            ],
            scratch_shapes=[pltpu.VMEM((count, count), F32)],
        ),
        out_shape=(
            struct((count, D), BF16),
            struct((HEADS, count, count), BF16),
            struct((count, D), F32),
        ),
        cost_estimate=cost(4 * count * count * D * 4, HEADS * count * count * 2, HEADS * count * count),
        name="attend",
    )(lengths, arrived, *(qkv_text,) * 3, *(qkv_region,) * 3)


def attend_back_body(
    text_q_ref,
    text_k_ref,
    text_v_ref,
    region_q_ref,
    region_k_ref,
    region_v_ref,
    w_q_ref,
    w_k_ref,
    w_v_ref,
    chance_ref,
    inv_ref,
    ctx_ref,
    dctx_ref,
    d_mid_ref,
    rows_turned_ref,
    keep_ref,
    send_ref,
    sum_ref,
    text_grad_ref,
    region_grad_ref,
    total_ref,
    grad_ref,
):
    count = ctx_ref.shape[0]
    text_count = text_q_ref.shape[0]
    queries = join(text_q_ref, region_q_ref) * jnp.asarray(SCALE, BF16)
    key_rows = join(text_k_ref, region_k_ref)
    values = join(text_v_ref, region_v_ref)
    scaled = dctx_ref[...].astype(F32) * inv_ref[...]
    product = scaled * ctx_ref[...].astype(F32)
    scaled_low = scaled.astype(BF16)
    scaled_turned = scaled.T.astype(BF16)
    q_turned = queries.astype(F32).T.astype(BF16)
    step = 256
    first = head_mask(0)
    keys_turned, values_turned = [None, None], [None, None]
    tasks = [(start, head) for start in range(0, count, step) for head in range(2)]

    def d_chance_of(start, head):
        d_part = jnp.where(head_mask(head), scaled_low[start : start + step], jnp.zeros((), BF16))
        return dot_nt(d_part, values)

    following, ques = d_chance_of(*tasks[0]), []
    for index, (start, head) in enumerate(tasks):
        stop, low, high = start + step, head * HDIM, (head + 1) * HDIM
        d_chance = following
        if index + 1 < len(tasks):
            following = d_chance_of(*tasks[index + 1])
        low_terms = chance_ref[head, start:stop, :]
        delta = jnp.sum(jnp.where(head_mask(head), product[start:stop], 0.0), axis=1, keepdims=True)
        d_scores = (low_terms.astype(F32) * (d_chance - delta)).astype(BF16)
        ques.append(dot_nn(d_scores, key_rows))
        v_add = dot_nn(scaled_turned[low:high, start:stop], low_terms)
        k_add = dot_nn(q_turned[low:high, start:stop], d_scores)
        values_turned[head] = v_add if start == 0 else values_turned[head] + v_add
        keys_turned[head] = k_add if start == 0 else keys_turned[head] + k_add
        if head == 1:
            d_ques = (jnp.where(first, ques[0], ques[1]) * SCALE).astype(BF16)
            grad_ref[start:stop, :PAIR] = d_ques
            ques = []
    grad_ref[:, PAIR : 2 * PAIR] = jnp.concatenate(keys_turned, axis=0).T.astype(BF16)
    d_values = jnp.concatenate(values_turned, axis=0).T.astype(BF16)
    grad_ref[:, 2 * PAIR :] = d_values
    sum_ref[...] = column_sum(grad_ref[...].astype(F32))

    @pl.when(pl.program_id(0) == 0)
    def _():
        total_ref[...] = d_mid_ref[...]

    w_part = jnp.concatenate([w_q_ref[...], w_k_ref[...], w_v_ref[...]], axis=1)
    total_ref[...] += dot_nt(grad_ref[...], w_part)
    half = keep_ref.shape[0]
    keep_ref[...] = dot_nn(rows_turned_ref[:half, :], grad_ref[...]).astype(BF16)
    send_ref[...] = dot_nn(rows_turned_ref[half:, :], grad_ref[...]).astype(BF16)

    @pl.when(pl.program_id(0) == pl.num_programs(0) - 1)
    def _():
        text_grad_ref[...] = total_ref[:text_count, :].astype(BF16)
        region_grad_ref[...] = total_ref[text_count:, :].astype(BF16)


def attend_back(qkv_text, qkv_region, w_qkv, chance, inv, ctx, d_ctx, d_mid, rows_turned):
    text_count, slots = qkv_text.shape[0], qkv_region.shape[0]
    count = text_count + slots
    return pl.pallas_call(
        attend_back_body,
        grid=(PAIRS,),
        in_specs=thirds(text_count)
        + thirds(slots)
        + thirds(D)
        + [
            pl.BlockSpec((2, count, count), lambda p: (p, 0, 0)),
            pl.BlockSpec((count, PAIR), lambda p: (0, p)),
            pl.BlockSpec((count, PAIR), lambda p: (0, p)),
            pl.BlockSpec((count, PAIR), lambda p: (0, p)),
            whole((count, D)),
            whole((D, count)),
        ],
        out_specs=[
            pl.BlockSpec((D // 2, 3 * PAIR), lambda p: (0, p)),
            pl.BlockSpec((D // 2, 3 * PAIR), lambda p: (0, p)),
            pl.BlockSpec((1, 3 * PAIR), lambda p: (0, p)),
            whole((text_count, D)),
            whole((slots, D)),
        ],
        out_shape=(
            struct((D // 2, 3 * D), BF16),
            struct((D // 2, 3 * D), BF16),
            struct((1, 3 * D), F32),
            struct((text_count, D), BF16),
            struct((slots, D), BF16),
        ),
        scratch_shapes=[pltpu.VMEM((count, D), F32), pltpu.VMEM((count, 3 * PAIR), BF16)],
        cost_estimate=cost(8 * count * count * D * 4 + 12 * count * D * D, HEADS * count * count * 2),
        name="attend_back",
    )(*(qkv_text,) * 3, *(qkv_region,) * 3, *(w_qkv,) * 3, chance, inv, ctx, d_ctx, d_mid, rows_turned)


def gelu_parts(inputs):
    weight = jnp.exp2(inputs * inputs * (-0.5 * 1.4426950408889634))
    place = 1.0 / (1.0 + jnp.abs(inputs) * TAIL_RATE)
    poly = 0.5 * TAIL[4]
    for factor in TAIL[3::-1]:
        poly = poly * place + 0.5 * factor
    tail = weight * (poly * place)
    phi_sum = jnp.where(inputs >= 0.0, 1.0 - tail, tail)
    return inputs * phi_sum, phi_sum + inputs * weight * 0.3989422804014327


def feed_body(
    ctx_ref,
    w_out_ref,
    text_ref,
    region_ref,
    perm_ref,
    out_bias_ref,
    attn_gain_ref,
    attn_shift_ref,
    down_bias_ref,
    ffn_gain_ref,
    ffn_shift_ref,
    w_up_ref,
    up_bias_ref,
    w_down_ref,
    cot_text_ref,
    cot_region_ref,
    hidden_ref,
    slope_ref,
    norm_ref,
    inv_ref,
    rows_turned_ref,
    ctx_turned_ref,
    low_turned_ref,
    text_out_ref,
    region_out_ref,
    d_second_ref,
    d_down_ref,
    stats_ref,
    normed_ref,
    low_ref,
    total_ref,
):
    step = pl.program_id(0)
    text_count = text_ref.shape[0]
    count = ctx_ref.shape[0]
    parts = [(start, start + 256) for start in range(0, count, 256)]

    def each(body):
        @pl.loop(0, text_count // 256)
        def _(part):
            rows = pl.ds(pl.multiple_of(part * 256, 256), 256)
            body(rows, 0, rows)

        for start in range(text_count, count, 256):
            body(pl.ds(start, 256), 1, pl.ds(start - text_count, 256))

    @pl.when(step == 0)
    def _():
        def first(rows, side, own):
            inputs = (text_ref, region_ref)[side][own, :]
            ctx = ctx_ref[rows, :]
            attn_out = dot_nn(ctx, w_out_ref[...]) + row_of(out_bias_ref)
            norm, inv = standardize(inputs.astype(F32) + attn_out)
            normed = norm * row_of(attn_gain_ref) + row_of(attn_shift_ref)
            low = normed.astype(BF16)
            norm_ref[rows, :] = norm
            inv_ref[rows, :] = inv
            normed_ref[rows, :] = normed
            low_ref[rows, :] = low
            total_ref[rows, :] = normed + row_of(down_bias_ref)
            rows_turned_ref[:, rows] = dot_nt(perm_ref[...], inputs).astype(BF16)
            ctx_turned_ref[:, rows] = dot_nt(perm_ref[...], ctx).astype(BF16)
            low_turned_ref[:, rows] = dot_nt(perm_ref[...], low).astype(BF16)

        each(first)

    def up_of(start, stop):
        return dot_nn(low_ref[start:stop, :], w_up_ref[...]) + up_bias_ref[...]

    following = up_of(*parts[0])
    for index, (start, stop) in enumerate(parts):
        up_sum = following
        if index + 1 < len(parts):
            following = up_of(*parts[index + 1])
        value, slope = gelu_parts(up_sum)
        hidden = value.astype(BF16)
        hidden_ref[start:stop, :] = hidden
        slope_ref[start:stop, :] = slope.astype(BF16)
        total_ref[start:stop, :] += dot_nn(hidden, w_down_ref[...])

    @pl.when(step == pl.num_programs(0) - 1)
    def _():
        stats_ref[...] = jnp.zeros(stats_ref.shape, F32)

        def last(rows, side, own):
            norm, inv = standardize(total_ref[rows, :])
            out_ref = (text_out_ref, region_out_ref)[side]
            out_ref[own, :] = (norm * row_of(ffn_gain_ref) + row_of(ffn_shift_ref)).astype(BF16)
            upstream = (cot_text_ref, cot_region_ref)[side][own, :].astype(F32)
            d_second = standardize_back(upstream * row_of(ffn_gain_ref), norm, inv)
            d_down = d_second.astype(BF16)
            d_second_ref[rows, :] = d_second
            d_down_ref[rows, :] = d_down
            stats_ref[0:1, :] += column_sum(upstream * norm)
            stats_ref[1:2, :] += column_sum(upstream)
            stats_ref[2:3, :] += column_sum(d_down.astype(F32))

        each(last)


def feed_forward(ctx, w_out, text, arrived, perm, vecs, w_up, up_bias, w_down, cot_text, cot_region):
    count, text_count = ctx.shape[0], text.shape[0]
    slots = count - text_count
    units = w_up.shape[1]
    chunk = 512
    half = D // 2
    return pl.pallas_call(
        feed_body,
        grid=(units // chunk,),
        in_specs=[
            whole((count, D)),
            whole((D, D)),
            whole((text_count, D)),
            whole((slots, D)),
            whole((D, D)),
        ]
        + [whole((D,))] * len(vecs)
        + [
            pl.BlockSpec((D, chunk), lambda j: (0, j)),
            pl.BlockSpec((1, chunk), lambda j: (0, j)),
            pl.BlockSpec((chunk, D), lambda j: (j, 0)),
            whole((text_count, D)),
            whole((slots, D)),
        ],
        out_specs=[
            pl.BlockSpec((count, chunk), lambda j: (0, j)),
            pl.BlockSpec((count, chunk), lambda j: (0, j)),
            whole((count, D)),
            whole((count, 1)),
            whole((D, count)),
            whole((D, count)),
            whole((D, count)),
            whole((text_count, D)),
            whole((slots, D)),
            whole((count, D)),
            whole((count, D)),
            whole((8, D)),
        ],
        out_shape=(
            struct((count, units), BF16),
            struct((count, units), BF16),
            struct((count, D), F32),
            struct((count, 1), F32),
            struct((D, count), BF16),
            struct((D, count), BF16),
            struct((D, count), BF16),
            struct((text_count, D), BF16),
            struct((slots, D), BF16),
            struct((count, D), F32),
            struct((count, D), BF16),
            struct((8, D), F32),
        ),
        scratch_shapes=[
            pltpu.VMEM((count, D), F32),
            pltpu.VMEM((count, D), BF16),
            pltpu.VMEM((count, D), F32),
        ],
        cost_estimate=cost(4 * count * D * units + 8 * count * D * D, 4 * D * units + 4 * count * units, count * units),
        name="feed_forward",
    )(ctx, w_out, text, arrived, perm, *vecs, w_up, up_bias, w_down, cot_text, cot_region)


def feed_back_body(
    d_down_ref,
    slope_ref,
    w_down_ref,
    w_up_ref,
    d_second_ref,
    norm_ref,
    inv_ref,
    gain_ref,
    w_out_ref,
    low_turned_ref,
    ctx_turned_ref,
    up_keep_ref,
    up_send_ref,
    out_keep_ref,
    out_send_ref,
    up_sum_ref,
    d_mid_ref,
    d_ctx_ref,
    stats_ref,
    total_ref,
    d_up_ref,
    d_attn_ref,
):
    step = pl.program_id(0)
    count = d_down_ref.shape[0]
    parts = [(start, start + 256) for start in range(0, count, 256)]

    @pl.when(step == 0)
    def _():
        total_ref[...] = d_second_ref[...]

    up_total = jnp.zeros(up_sum_ref.shape, F32)
    def hidden_of(start, stop):
        return dot_nt(d_down_ref[start:stop, :], w_down_ref[...])

    following = hidden_of(*parts[0])
    for index, (start, stop) in enumerate(parts):
        d_hidden = following
        if index + 1 < len(parts):
            following = hidden_of(*parts[index + 1])
        d_up = (d_hidden * slope_ref[start:stop, :].astype(F32)).astype(BF16)
        d_up_ref[start:stop, :] = d_up
        up_total = up_total + column_sum(d_up.astype(F32))
        total_ref[start:stop, :] += dot_nt(d_up, w_up_ref[...])
    up_sum_ref[...] = up_total
    half = up_keep_ref.shape[0]
    up_keep_ref[...] = dot_nn(low_turned_ref[:half, :], d_up_ref[...]).astype(BF16)
    up_send_ref[...] = dot_nn(low_turned_ref[half:, :], d_up_ref[...]).astype(BF16)

    @pl.when(step == pl.num_programs(0) - 1)
    def _():
        stats_ref[...] = jnp.zeros(stats_ref.shape, F32)

        @pl.loop(0, len(parts))
        def _(part):
            rows = pl.ds(pl.multiple_of(part * 256, 256), 256)
            d_first = total_ref[rows, :]
            norm = norm_ref[rows, :]
            d_mid = standardize_back(d_first * row_of(gain_ref), norm, inv_ref[rows, :])
            d_attn = d_mid.astype(BF16)
            d_mid_ref[rows, :] = d_mid
            d_attn_ref[rows, :] = d_attn
            d_ctx_ref[rows, :] = dot_nt(d_attn, w_out_ref[...]).astype(BF16)
            stats_ref[0:1, :] += column_sum(d_first * norm)
            stats_ref[1:2, :] += column_sum(d_first)
            stats_ref[2:3, :] += column_sum(d_attn.astype(F32))

        out_keep_ref[...] = dot_nn(ctx_turned_ref[:half, :], d_attn_ref[...]).astype(BF16)
        out_send_ref[...] = dot_nn(ctx_turned_ref[half:, :], d_attn_ref[...]).astype(BF16)


def feed_back(d_down, slope, w_down, w_up, d_second, norm, inv, gain, w_out, low_turned, ctx_turned):
    count, units = slope.shape
    chunk = 512
    return pl.pallas_call(
        feed_back_body,
        grid=(units // chunk,),
        in_specs=[
            whole((count, D)),
            pl.BlockSpec((count, chunk), lambda j: (0, j)),
            pl.BlockSpec((chunk, D), lambda j: (j, 0)),
            pl.BlockSpec((D, chunk), lambda j: (0, j)),
            whole((count, D)),
            whole((count, D)),
            whole((count, 1)),
            whole((D,)),
            whole((D, D)),
            whole((D, count)),
            whole((D, count)),
        ],
        out_specs=[
            pl.BlockSpec((D // 2, chunk), lambda j: (0, j)),
            pl.BlockSpec((D // 2, chunk), lambda j: (0, j)),
            whole((D // 2, D)),
            whole((D // 2, D)),
            pl.BlockSpec((1, chunk), lambda j: (0, j)),
            whole((count, D)),
            whole((count, D)),
            whole((8, D)),
        ],
        out_shape=(
            struct((D // 2, units), BF16),
            struct((D // 2, units), BF16),
            struct((D // 2, D), BF16),
            struct((D // 2, D), BF16),
            struct((1, units), F32),
            struct((count, D), F32),
            struct((count, D), BF16),
            struct((8, D), F32),
        ),
        scratch_shapes=[
            pltpu.VMEM((count, D), F32),
            pltpu.VMEM((count, chunk), BF16),
            pltpu.VMEM((count, D), BF16),
        ],
        cost_estimate=cost(6 * count * D * units + 4 * count * D * D, 4 * D * units + 4 * count * units),
        name="feed_back",
    )(d_down, slope, w_down, w_up, d_second, norm, inv, gain, w_out, low_turned, ctx_turned)


def region_back_body(
    back_ref,
    hot_ref,
    norm_ref,
    inv_ref,
    gain_ref,
    boxes_ref,
    qkv_ref,
    attn_ref,
    ffn_ref,
    up_ref,
    perm_ref,
    d_proj_ref,
    *piece_refs,
):
    rows = norm_ref.shape[0]
    d_region = dot_tn(hot_ref[...], back_ref[...])
    norm = norm_ref[...]
    d_pre = standardize_back(d_region * row_of(gain_ref), norm, inv_ref[...])
    d_proj = d_pre.astype(BF16)
    d_proj_ref[...] = d_proj
    boxes = jnp.concatenate([boxes_ref[...], jnp.zeros((4, rows), F32)], axis=0).T
    vectors = [column_sum(d_pre), column_sum(d_region * norm), column_sum(d_region)]
    vectors += [column_sum(boxes[:, side : side + 1] * d_pre) for side in range(4)]
    for part in (0, 2):
        starts = [(3 * pair + part) * PAIR for pair in range(PAIRS)]
        vectors.append(jnp.concatenate([qkv_ref[:, start : start + PAIR] for start in starts], axis=1))
    for ref in (attn_ref, ffn_ref):
        vectors += [ref[2:3, :], ref[0:2, :]]
    vectors.append(up_ref[...])
    filled = sum(vector.shape[0] for vector in vectors)
    vectors.append(jnp.zeros((VECS - filled, D), F32))
    low_vectors = jnp.concatenate(vectors, axis=0).astype(BF16)
    turned = dot_nt(perm_ref[...], jnp.concatenate([d_proj, low_vectors], axis=0)).astype(BF16)
    size = D // len(piece_refs)
    for index, piece_ref in enumerate(piece_refs):
        piece_ref[...] = turned[index * size : (index + 1) * size]


def region_back(back, hot, norm, *others):
    rows = norm.shape[0]
    return pl.pallas_call(
        region_back_body,
        out_shape=(struct((rows, D), BF16),) + (struct((D // 4, rows + VECS), BF16),) * 4,
        cost_estimate=cost(0, 0),
        name="region_back",
    )(back, hot, norm, *others)


def swap_cores(sent):
    return lax.ppermute(sent, "enc", [(0, 1), (1, 0)])


def swap_chips(sent, offset, peers):
    return lax.ppermute(sent, "dp", [(peer, peer ^ offset) for peer in range(peers)])


MASKS = (0, 1, 3, 2)


def reverse(value, width):
    result = value & 0
    for bit in range(width):
        result = result | (((value >> bit) & 1) << (width - 1 - bit))
    return result


def after(first, *others):
    if not others:
        return first
    return lax.optimization_barrier((first,) + others)[0]


def swap_cores(sent):
    return [lax.ppermute(array, "enc", [(0, 1), (1, 0)]) for array in sent]


def swap_chips(sent, mask, peers):
    return lax.ppermute(sent, "dp", [(peer, peer ^ mask) for peer in range(peers)])


def combine_body(plans, counts, *refs):
    refs, out_refs = refs[:counts], refs[counts:]
    for out_ref, (unit, segments) in zip(out_refs, plans):

        def add(start, size, segments=segments, out_ref=out_ref):
            for place, at, terms in segments:
                sums = [refs[index][pl.ds(start, size), left:right].astype(F32) for index, left, right in terms]
                value = functools.reduce(jnp.add, sums).astype(out_ref.dtype)
                out_ref[pl.ds(place + start, size), at : at + value.shape[1]] = value

        if unit % 32 or unit < 64:
            add(0, unit)
        else:

            @pl.loop(0, unit // 32)
            def _(step, add=add):
                add(pl.multiple_of(step * 32, 32), 32)


def segments_of(terms, columns):
    edges = set()
    for array, _, first in terms:
        edges |= {first, first + array.shape[1]}
    for left, right in columns:
        inside = sorted({left, right} | {edge for edge in edges if left < edge < right})
        yield from zip(inside, inside[1:])


def combine_plain(terms, start, stop, columns, dtype):
    sums = []
    for left, right in segments_of(terms, columns):
        blocks = [
            array[row + start : row + stop, left - first : right - first].astype(F32)
            for array, row, first in terms
            if first <= left and right <= first + array.shape[1]
        ]
        sums.append(functools.reduce(jnp.add, blocks))
    return jnp.concatenate(sums, axis=1).astype(dtype)


def combine(wanted, name):
    plans, operands, specs, shapes, known = [], [], [], [], {}
    for terms, start, stop, columns, dtype in wanted:
        unit = functools.reduce(math.gcd, [value for _, row, _ in terms for value in (row + start, row + stop)])
        if unit % 8:
            return [combine_plain(*each) for each in wanted]
        segments = []
        for place in range(0, stop - start, unit):
            at = 0
            for left, right in segments_of(terms, columns):
                sources = []
                for array, row, first in terms:
                    if first <= left and right <= first + array.shape[1]:
                        block = (row + start + place) // unit
                        key = (id(array), unit, block)
                        if key not in known:
                            known[key] = len(operands)
                            operands.append(array)
                            specs.append(pl.BlockSpec((unit, array.shape[1]), lambda j, block=block: (block, 0)))
                        sources.append((known[key], left - first, right - first))
                segments.append((place, at, sources))
                at += right - left
        plans.append((unit, segments))
        shapes.append(struct((stop - start, at), dtype))
    return pl.pallas_call(
        functools.partial(combine_body, plans, len(operands)),
        grid=(1,),
        in_specs=specs,
        out_specs=[pl.BlockSpec(shape.shape, lambda j: (0, 0)) for shape in shapes],
        out_shape=tuple(shapes),
        cost_estimate=cost(0, 0),
        name=name,
    )(*operands)


def side_by_side(*arrays):
    terms, first = [], 0
    for array in arrays:
        terms.append((array, 0, first))
        first += array.shape[1]
    return terms


class Pair:
    def __init__(self, terms, rows, middle, width, peers):
        self.terms, self.size, self.middle, self.width, self.peers = terms, rows // 4, middle, width, peers
        self.sides = [(0, middle)], [(middle, width)]

    def start(self):
        size, (first, second) = self.size, self.sides
        wanted = [(self.terms, size, 3 * size, first, BF16), (self.terms, 2 * size, 4 * size, second, BF16)]
        self.sent = list(combine(wanted, "pair_start"))
        return self.sent

    def ship(self):
        self.got = [swap_chips(sent, bit, self.peers) for sent, bit in zip(self.sent, (1, 2))]
        return self.got

    def hold(self, *behind):
        self.got = [after(array, *behind) for array in self.got]

    def turn(self):
        size, (first, second), (one, two) = self.size, self.sides, self.got
        wanted = [
            (self.terms + [(one, -2 * size, 0)], 3 * size, 4 * size, first, BF16),
            (self.terms + [(two, -size, self.middle)], size, 2 * size, second, BF16),
        ]
        self.sent = list(combine(wanted, "pair_turn"))
        return self.sent

    def finish(self):
        last = [swap_chips(sent, bit, self.peers) for sent, bit in zip(self.sent, (2, 1))]
        (one, two), middle = self.got, self.middle
        arrived = [(one, 0, 0), (two, self.size, middle), (last[0], 0, 0), (last[1], 0, middle)]
        return Scatter(self.terms + arrived, self.size, self.width, self.peers, 2, 2)


class Scatter:
    def __init__(self, terms, rows, width, peers, bit, fresh):
        self.terms, self.rows, self.width, self.peers, self.bit, self.fresh = terms, rows, width, peers, bit, fresh

    def cut(self, bits, *behind):
        self.bits = min(bits, self.peers.bit_length() - 1 - self.bit)
        self.rows >>= self.bits
        wanted = [
            (self.terms, offset * self.rows, (offset + 1) * self.rows, [(0, self.width)], BF16)
            for offset in range(1, 1 << self.bits)
        ]
        self.sent = [after(array, *behind) for array in combine(wanted, "cut")]
        return self.sent

    def ship(self):
        masks = [reverse(offset, self.bits) << self.bit for offset in range(1, 1 << self.bits)]
        got = [swap_chips(sent, mask, self.peers) for sent, mask in zip(self.sent, masks)]
        self.terms = self.terms + side_by_side_rows(got)
        self.bit += self.bits
        self.fresh = len(got)
        return got

    def hold(self, *behind):
        late = [(after(array, *behind), row, first) for array, row, first in self.terms[-self.fresh :]]
        self.terms = self.terms[: -self.fresh] + late

    def finish(self, bits):
        while 1 << self.bit < self.peers:
            self.cut(bits)
            self.ship()
        return self

    def shares(self, *ranges):
        return [(self.terms, 0, self.rows, columns, F32) for columns in ranges]


def side_by_side_rows(arrays):
    return [(array, 0, 0) for array in arrays]


def direct(terms, rows, width, peers, bit):
    size = rows // 4
    wanted = [(terms, place * size, (place + 1) * size, [(0, width)], BF16) for place in range(1, 4)]
    sent = combine(wanted, "direct")
    got = [swap_chips(array, mask, peers) for array, mask in zip(sent, MASKS[1:])]
    return sent, Scatter(terms + side_by_side_rows(got), size, width, peers, bit, 3)


def swap_near(pieces, peers):
    return [swap_chips(piece, offset << 2, peers) for offset, piece in enumerate(pieces[1:], 1)]


def place_of(block, peers):
    rest = peers // 4
    top = block // rest
    return (top ^ (top >> 1)) + (reverse(block % rest, rest.bit_length() - 1) << 2)


def units_body(order_ref, *refs):
    kept, got = refs[:-3:2], refs[1:-3:2]
    near_ref, far_ref, keep_ref = refs[-3:]
    step, half = pl.program_id(0), near_ref.shape[1]
    rows = [(one[...].astype(F32) + two[...].astype(F32)).astype(BF16) for one, two in zip(kept, got)]
    rows = jnp.concatenate(rows, axis=0)
    keep_ref[...] = rows

    @pl.when((step == 1) | (step == 2))
    def _():
        near_ref[...] = rows[:, :half]

    @pl.when(step >= 2)
    def _():
        far_ref[...] = rows[:, half:]


def cut_units(kept, got, order, peers):
    count, width = kept.shape
    size, half, rest = count // peers, width // 2, peers // 4
    if size % 16:
        rows = (kept.astype(F32) + got.astype(F32)).reshape(peers, size, width)
        rows = jnp.take(rows, order, axis=0).reshape(count, width).astype(BF16)
        return rows[count // 4 : 3 * count // 4, :half], rows[count // 2 :, half:], rows
    specs = []
    for index in range(rest):
        specs += [pl.BlockSpec((size, width), lambda j, order, index=index: (order[j * rest + index], 0))] * 2
    return pl.pallas_call(
        units_body,
        grid_spec=pltpu.PrefetchScalarGridSpec(
            num_scalar_prefetch=1,
            grid=(4,),
            in_specs=specs,
            out_specs=[
                pl.BlockSpec((count // 4, half), lambda j, order: (jnp.clip(j - 1, 0, 1), 0)),
                pl.BlockSpec((count // 4, half), lambda j, order: (jnp.clip(j - 2, 0, 1), 0)),
                pl.BlockSpec((count // 4, width), lambda j, order: (j, 0)),
            ],
        ),
        out_shape=(struct((count // 2, half), BF16), struct((count // 2, half), BF16), struct((count, width), BF16)),
        cost_estimate=cost(count * width, 8 * count * width),
        name="cut_units",
    )(order, *(kept, got) * rest)


def region_product_body(*refs):
    *refs, keep_ref, send_ref = refs
    pieces, feats = refs[: len(refs) // 2], refs[len(refs) // 2 :]
    rows, width = feats[0].shape
    half = keep_ref.shape[0]
    turned = jnp.concatenate([piece[:, :rows] for piece in pieces], axis=1)
    vectors = functools.reduce(jnp.add, [piece[:, rows:].astype(F32) for piece in pieces])
    product = dot_nn(turned, jnp.concatenate([ref[...] for ref in feats], axis=0)).astype(BF16)
    for ref, start in ((keep_ref, 0), (send_ref, half)):
        ref[:, :width] = product[start : start + half]
        ref[:, width:] = vectors[start : start + half].astype(BF16)


def region_product(pieces, feats):
    half, width = pieces[0].shape[0] // 2, feats[0].shape[1] + VECS
    return pl.pallas_call(
        region_product_body,
        out_shape=(struct((half, width), BF16), struct((half, width), BF16)),
        cost_estimate=cost(0, 0),
        name="region_product",
    )(*pieces, *feats)


def one_hot_rows(core, place, inner, peers):
    share = D // (2 * peers)
    core, place = core ^ lax.axis_index("enc"), place ^ lax.axis_index("dp")
    row = (core * peers + place) * share + inner
    return (lax.broadcasted_iota(jnp.int32, (D, D), 1) == row).astype(BF16)


def share_order(peers):
    share = D // (2 * peers)
    row = lax.broadcasted_iota(jnp.int32, (D, 1), 0)
    block = row // share
    return one_hot_rows(block // peers, place_of(block % peers, peers), row % share, peers)


def region_order(peers):
    share, rest = D // (2 * peers), peers // 16
    row = lax.broadcasted_iota(jnp.int32, (D, 1), 0)
    block = row // share
    top = (block // rest) % 4
    place = (top ^ (top >> 1)) + ((block // (8 * rest)) << 2) + (reverse(block % rest, rest.bit_length() - 1) << 4)
    return one_hot_rows((block // (4 * rest)) % 2, place, row % share, peers)


def exchange(array):
    return lax.all_to_all(array, "dp", split_axis=0, concat_axis=0, tiled=True)


def per_device(
    text_in,
    text_lengths,
    region_feats,
    region_boxes,
    region_dest,
    region_seq,
    w_region,
    w_box,
    type_embed,
    region_gain,
    region_shift,
    w_qkv,
    q_bias,
    v_bias,
    w_out,
    out_bias,
    attn_gain,
    attn_shift,
    w_up,
    up_bias,
    w_down,
    down_bias,
    ffn_gain,
    ffn_shift,
    cot_text,
    cot_region,
):
    peers = lax.axis_size("dp")
    source_rows = region_feats.shape[0]
    capacity = max(2, 2 * source_rows // peers)
    slots = peers * capacity
    text_count = text_in.shape[0]
    units = w_up.shape[1]

    def row(vector):
        return vector.reshape(1, -1)

    outgoing, cot_sent, hot, region_norm, region_inv = region_forward(
        capacity,
        slots,
        region_feats,
        w_region,
        region_boxes,
        row(region_dest),
        row(region_seq),
        w_box,
        type_embed,
        region_gain,
        region_shift,
        cot_region,
    )
    arrived = exchange(outgoing)
    arrived_cot = exchange(cot_sent)

    far_feats = swap_near([region_feats] + [after(region_feats, arrived)] * 3, peers)

    bias = jnp.concatenate([q_bias, jnp.zeros_like(q_bias), v_bias])[None]
    perm, region_perm = lax.optimization_barrier((share_order(peers), region_order(peers)))
    order = place_of(jnp.arange(peers, dtype=jnp.int32), peers) ^ lax.axis_index("dp")
    qkv_text = (dot_nn(text_in, w_qkv) + bias).astype(BF16)
    qkv_region = (dot_nn(arrived[:, :D], w_qkv) + bias).astype(BF16)
    context, chance, chance_inv = attend(text_lengths, arrived, qkv_text, qkv_region)
    vecs = (out_bias, attn_gain, attn_shift, down_bias, ffn_gain, ffn_shift)
    (
        hidden,
        slope,
        norm,
        inv,
        rows_turned,
        ctx_turned,
        low_turned,
        text_out,
        region_sent,
        d_second,
        d_down,
        ffn_stats,
    ) = feed_forward(context, w_out, text_in, arrived, perm, vecs, w_up, row(up_bias), w_down, cot_text, arrived_cot)

    d_down = after(d_down, *far_feats)
    core = lax.axis_index("enc")
    half = units // 2

    def unit_product(which):
        side = lax.dynamic_slice_in_dim(hidden, which * half, half, axis=1)
        return dot_tn(side, d_down).astype(BF16)

    (got,) = swap_cores([unit_product(1 - core)])
    *sent, kept = cut_units(unit_product(core), got, order, peers)
    down = Pair([(kept, 0, 0)], half, D // 2, D, peers)
    down.sent = sent
    covered = after(d_down, *sent)
    near = down.ship()
    up_keep, up_send, out_keep, out_send, up_grad, d_mid, d_ctx, attn_stats = feed_back(
        covered, slope, w_down, w_up, d_second, norm, inv, attn_gain, w_out, low_turned, ctx_turned
    )
    up_send, out_send = lax.optimization_barrier((up_send, out_send, *near))[:2]
    got = swap_cores([up_send, out_send])
    down.turn()
    down = down.finish()
    up_out = Pair(
        side_by_side(up_keep, out_keep) + side_by_side(*got), D // 2, (units + D) // 2, units + D, peers
    )
    sent = up_out.start()
    near = up_out.ship()
    returned = exchange(after(region_sent, *sent))
    down.hold(*sent)
    covered = after(d_ctx, *sent, *down.cut(2))
    far = down.ship()
    qkv_keep, qkv_send, qkv_sums, text_grad, d_rows_region = attend_back(
        qkv_text, qkv_region, w_qkv, chance, chance_inv, context, covered, d_mid, rows_turned
    )
    qkv_send = after(qkv_send, returned, *near, *far)
    (got,) = swap_cores([qkv_send])
    sent_back = exchange(after(d_rows_region, qkv_send))
    qkv = Pair([(qkv_keep, 0, 0), (got, 0, 0)], D // 2, 3 * D // 2, 3 * D, peers)
    sent = qkv.start()
    qkv_got = qkv.ship()
    up_out.hold(*sent)
    sent = up_out.turn()
    up_out = up_out.finish()
    sent_back = after(sent_back, *qkv_got)

    share = D // (2 * peers)
    quarter = units // D
    up_rows = after(up_grad, *sent).reshape(2 * peers, quarter, share).transpose(1, 0, 2).reshape(quarter, D)
    d_proj, *pieces = region_back(
        sent_back,
        hot,
        region_norm,
        region_inv,
        region_gain,
        region_boxes,
        qkv_sums,
        attn_stats,
        ffn_stats,
        up_rows,
        region_perm,
    )
    feats_width = region_feats.shape[1]
    up_out.hold(*pieces)
    qkv.hold(*pieces)
    region_got = swap_near(pieces, peers)
    qkv.turn()
    qkv = qkv.finish()
    qkv_got = [array for array, _, _ in qkv.terms[-qkv.fresh :]]
    sent = up_out.cut(1)
    up_out.ship()
    region_got = [after(array, *qkv_got, *sent) for array in region_got]
    last_keep, last_send = region_product(pieces[:1] + region_got, [region_feats] + far_feats)
    (got,) = swap_cores([last_send])
    qkv.hold(last_send)
    qkv.cut(1)
    qkv.ship()
    last_sent, last = direct(
        [(last_keep, 0, 0), (got, 0, 0)], last_keep.shape[0], feats_width + VECS, peers, 4
    )
    qkv.hold(*last_sent)
    up_out.hold(*last_sent)
    down.hold(*last_sent)
    sent = up_out.cut(1)
    up_out.ship()
    d_proj, returned = lax.optimization_barrier((d_proj, returned, *sent))[:2]
    region_out = dot_tn(hot, returned).astype(BF16)
    feats_grad = dot_nt(d_proj, w_region).astype(BF16)
    starts = [(3 * pair + part) * PAIR for part in range(3) for pair in range(PAIRS)]
    heads = [(start, start + PAIR) for start in starts]
    w_qkv_share, w_up_share, w_out_share, w_down_share = combine(
        qkv.finish(1).shares(heads)
        + up_out.finish(1).shares([(0, units)], [(units, units + D)])
        + down.finish(2).shares([(0, D)]),
        "shares",
    )
    w_region_share, vectors = combine(
        last.finish(2).shares([(0, feats_width)], [(feats_width, feats_width + VECS)]), "last_shares"
    )
    vectors = vectors.T
    return (
        text_out,
        region_out,
        text_grad,
        feats_grad,
        w_region_share.T,
        vectors[3:7],
        vectors[0],
        vectors[1],
        vectors[2],
        w_qkv_share,
        vectors[7],
        vectors[8],
        w_out_share,
        vectors[9],
        vectors[10],
        vectors[11],
        w_up_share,
        vectors[15 : 15 + quarter].reshape(-1),
        w_down_share,
        vectors[12],
        vectors[13],
        vectors[14],
    )


def solution(mesh):
    both = ("enc", "dp")
    rows, flat, none = P(both, None), P(both), P()
    in_specs = (rows, rows, rows, P(None, both), rows, flat) + (none,) * 18 + (rows, rows)
    out_specs = (
        (rows,) * 4
        + (P(None, both), P(None, both), flat, flat, flat, rows, flat, flat, rows)
        + (flat, flat, flat, rows, flat, rows, flat, flat, flat)
    )
    return jax.shard_map(per_device, mesh=mesh, in_specs=in_specs, out_specs=out_specs, check_vma=False)
```

```python
import functools
import math

import jax
import jax.numpy as jnp
from jax import lax
from jax.experimental import pallas as pl
from jax.experimental.pallas import tpu as pltpu
from jax.sharding import PartitionSpec as P

D = 768
HEADS = 12
HDIM = 64
PAIR = 2 * HDIM
PAIRS = HEADS // 2
TAGS = 128
VECS = 128

F32 = jnp.float32
BF16 = jnp.bfloat16
eps = 1e-05
SCALE = HDIM ** (-0.5)

TAIL_RATE = 0.3275911 * 0.7071067811865476
TAIL = (0.254829592, -0.284496736, 1.421413741, -1.453152027, 1.061405429)


def dot_nn(left, right):
    return lax.dot_general(left, right, (((1,), (0,)), ((), ())), preferred_element_type=F32)


def dot_nt(left, right):
    return lax.dot_general(left, right, (((1,), (1,)), ((), ())), preferred_element_type=F32)


def dot_tn(left, right):
    return lax.dot_general(left, right, (((0,), (0,)), ((), ())), preferred_element_type=F32)


def standardize(inputs):
    row_mean = jnp.mean(inputs, axis=-1, keepdims=True)
    centred = inputs - row_mean
    spread = jnp.mean(centred * centred, axis=-1, keepdims=True)
    inv = lax.rsqrt(spread + eps)
    return centred * inv, inv


def standardize_back(grad, norm, inv):
    first = jnp.mean(grad, axis=-1, keepdims=True)
    second = jnp.mean(grad * norm, axis=-1, keepdims=True)
    return (grad - first - norm * second) * inv


def row_of(ref):
    return ref[...].reshape(1, D)


def column_sum(inputs):
    return jnp.sum(inputs, axis=0, keepdims=True)


def whole(shape):
    return pl.BlockSpec(shape, lambda *_: (0,) * len(shape), pipeline_mode=pl.Buffered(1))


def struct(shape, dtype):
    return jax.ShapeDtypeStruct(shape, dtype)


def cost(flops, moved, exps=0):
    return pl.CostEstimate(flops=int(flops), bytes_accessed=int(moved), transcendentals=int(exps))


def region_body(
    capacity,
    feats_ref,
    w_ref,
    boxes_ref,
    dest_ref,
    seq_ref,
    w_box_ref,
    type_ref,
    gain_ref,
    shift_ref,
    cot_ref,
    out_ref,
    cot_out_ref,
    hot_ref,
    norm_ref,
    inv_ref,
):
    rows = feats_ref.shape[0]
    slots = out_ref.shape[0]
    dest_row = jnp.broadcast_to(dest_ref[...].astype(F32), (rows, rows))
    dest_col = dest_row.T
    row_io = lax.broadcasted_iota(jnp.int32, (rows, rows), 0)
    col_io = lax.broadcasted_iota(jnp.int32, (rows, rows), 1)
    earlier = jnp.where((dest_col == dest_row) & (row_io < col_io), 1.0, 0.0)
    slot = dest_row[0:1, :] * capacity + column_sum(earlier)
    slot_io = lax.broadcasted_iota(jnp.int32, (slots, rows), 0).astype(F32)
    hot = jnp.where(slot_io == slot, 1.0, 0.0)
    hot_low = hot.astype(BF16)
    hot_ref[...] = hot_low
    cot_out_ref[...] = dot_nn(hot_low, cot_ref[...]).astype(BF16)
    tags = jnp.sum(hot * (seq_ref[...].astype(F32) + 1.0), axis=1, keepdims=True)
    projection = dot_nn(feats_ref[...], w_ref[...])
    boxes = jnp.concatenate([boxes_ref[...], jnp.zeros((4, rows), F32)], axis=0).T
    spatial = boxes[:, 0:1] * w_box_ref[0:1, :]
    for side in range(1, 4):
        spatial = spatial + boxes[:, side : side + 1] * w_box_ref[side : side + 1, :]
    norm, inv = standardize(projection + spatial + row_of(type_ref))
    norm_ref[...] = norm
    inv_ref[...] = inv
    low_rows = (norm * row_of(gain_ref) + row_of(shift_ref)).astype(BF16)
    out_ref[:, :D] = dot_nn(hot_low, low_rows).astype(BF16)
    out_ref[:, D:] = jnp.broadcast_to(tags, (slots, TAGS)).astype(BF16)


def region_forward(capacity, slots, feats, w_region, *others):
    rows, width = feats.shape
    return pl.pallas_call(
        functools.partial(region_body, capacity),
        out_shape=(
            struct((slots, D + TAGS), BF16),
            struct((slots, D), BF16),
            struct((slots, rows), BF16),
            struct((rows, D), F32),
            struct((rows, 1), F32),
        ),
        cost_estimate=cost(2 * rows * width * D, 2 * (rows + D) * width),
        name="region_forward",
    )(feats, w_region, *others)


def head_mask(head):
    lane = lax.broadcasted_iota(jnp.int32, (1, PAIR), 1)
    return (lane >= head * HDIM) & (lane < (head + 1) * HDIM)


def join(*refs):
    return jnp.concatenate([ref[...] for ref in refs], axis=0)


def thirds(rows):
    return [pl.BlockSpec((rows, PAIR), lambda p, *_, part=part: (0, part * PAIRS + p)) for part in range(3)]


def attend_body(
    lengths_ref,
    tag_ref,
    text_q_ref,
    text_k_ref,
    text_v_ref,
    region_q_ref,
    region_k_ref,
    region_v_ref,
    ctx_ref,
    chance_ref,
    inv_ref,
    bias_ref,
):
    text_count, slots = text_q_ref.shape[0], region_q_ref.shape[0]
    count = text_count + slots
    sequences = lengths_ref.shape[1]

    @pl.when(pl.program_id(0) == 0)
    def _():
        place = lax.broadcasted_iota(jnp.int32, (text_count, 1), 0)
        text_seg = jnp.zeros((text_count, 1), F32)
        end = jnp.int32(0)
        for index in range(sequences):
            end = end + lengths_ref[0, index]
            text_seg = text_seg + jnp.where(place >= end, 1.0, 0.0)
        region_seg = tag_ref[:, 0:1].astype(F32) - 1.0
        region_seg = jnp.where(region_seg < 0.0, float(sequences), region_seg)
        seg_col = jnp.concatenate([text_seg, region_seg], axis=0)
        seg_row = jnp.broadcast_to(seg_col, (count, 128)).T[0:1, :]
        bias_ref[...] = jnp.where(seg_col == seg_row, 0.0, -1e30)

    queries = join(text_q_ref, region_q_ref) * jnp.asarray(SCALE, BF16)
    key_rows = join(text_k_ref, region_k_ref)
    values = jnp.concatenate([join(text_v_ref, region_v_ref), jnp.ones((count, PAIR), BF16)], axis=1)
    step = 256
    first = head_mask(0)
    tasks = [(start, head) for start in range(0, count, step) for head in range(2)]

    def scores_of(start, head):
        q_part = jnp.where(head_mask(head), queries[start : start + step], jnp.zeros((), BF16))
        return dot_nt(q_part, key_rows)

    following, outs, invs = scores_of(*tasks[0]), [], []
    for index, (start, head) in enumerate(tasks):
        stop = start + step
        scores = following + bias_ref[start:stop, :]
        if index + 1 < len(tasks):
            following = scores_of(*tasks[index + 1])
        exp_terms = jnp.exp(scores - jnp.max(scores, axis=1, keepdims=True))
        low_terms = exp_terms.astype(BF16)
        chance_ref[head, start:stop, :] = low_terms
        summed = dot_nn(low_terms, values)
        inv = 1.0 / summed[:, PAIR:]
        outs.append(summed[:, :PAIR] * inv)
        invs.append(inv)
        if head == 1:
            ctx_ref[start:stop, :] = jnp.where(first, outs[0], outs[1]).astype(BF16)
            inv_ref[start:stop, :] = jnp.where(first, invs[0], invs[1])
            outs, invs = [], []


def attend(lengths, arrived, qkv_text, qkv_region):
    text_count, slots = qkv_text.shape[0], qkv_region.shape[0]
    count = text_count + slots
    return pl.pallas_call(
        attend_body,
        grid_spec=pltpu.PrefetchScalarGridSpec(
            num_scalar_prefetch=1,
            grid=(PAIRS,),
            in_specs=[pl.BlockSpec((slots, TAGS), lambda p, *_: (0, D // TAGS))] + thirds(text_count) + thirds(slots),
            out_specs=[
                pl.BlockSpec((count, PAIR), lambda p, *_: (0, p)),
                pl.BlockSpec((2, count, count), lambda p, *_: (p, 0, 0)),
                pl.BlockSpec((count, PAIR), lambda p, *_: (0, p)),
            ],
            scratch_shapes=[pltpu.VMEM((count, count), F32)],
        ),
        out_shape=(
            struct((count, D), BF16),
            struct((HEADS, count, count), BF16),
            struct((count, D), F32),
        ),
        cost_estimate=cost(4 * count * count * D * 4, HEADS * count * count * 2, HEADS * count * count),
        name="attend",
    )(lengths, arrived, *(qkv_text,) * 3, *(qkv_region,) * 3)


def attend_back_body(
    text_q_ref,
    text_k_ref,
    text_v_ref,
    region_q_ref,
    region_k_ref,
    region_v_ref,
    w_q_ref,
    w_k_ref,
    w_v_ref,
    chance_ref,
    inv_ref,
    ctx_ref,
    dctx_ref,
    d_mid_ref,
    rows_turned_ref,
    keep_ref,
    send_ref,
    sum_ref,
    text_grad_ref,
    region_grad_ref,
    total_ref,
    grad_ref,
):
    count = ctx_ref.shape[0]
    text_count = text_q_ref.shape[0]
    queries = join(text_q_ref, region_q_ref) * jnp.asarray(SCALE, BF16)
    key_rows = join(text_k_ref, region_k_ref)
    values = join(text_v_ref, region_v_ref)
    scaled = dctx_ref[...].astype(F32) * inv_ref[...]
    product = scaled * ctx_ref[...].astype(F32)
    scaled_low = scaled.astype(BF16)
    scaled_turned = scaled.T.astype(BF16)
    q_turned = queries.astype(F32).T.astype(BF16)
    step = 256
    first = head_mask(0)
    keys_turned, values_turned = [None, None], [None, None]
    tasks = [(start, head) for start in range(0, count, step) for head in range(2)]

    def d_chance_of(start, head):
        d_part = jnp.where(head_mask(head), scaled_low[start : start + step], jnp.zeros((), BF16))
        return dot_nt(d_part, values)

    following, ques = d_chance_of(*tasks[0]), []
    for index, (start, head) in enumerate(tasks):
        stop, low, high = start + step, head * HDIM, (head + 1) * HDIM
        d_chance = following
        if index + 1 < len(tasks):
            following = d_chance_of(*tasks[index + 1])
        low_terms = chance_ref[head, start:stop, :]
        delta = jnp.sum(jnp.where(head_mask(head), product[start:stop], 0.0), axis=1, keepdims=True)
        d_scores = (low_terms.astype(F32) * (d_chance - delta)).astype(BF16)
        ques.append(dot_nn(d_scores, key_rows))
        v_add = dot_nn(scaled_turned[low:high, start:stop], low_terms)
        k_add = dot_nn(q_turned[low:high, start:stop], d_scores)
        values_turned[head] = v_add if start == 0 else values_turned[head] + v_add
        keys_turned[head] = k_add if start == 0 else keys_turned[head] + k_add
        if head == 1:
            d_ques = (jnp.where(first, ques[0], ques[1]) * SCALE).astype(BF16)
            grad_ref[start:stop, :PAIR] = d_ques
            ques = []
    grad_ref[:, PAIR : 2 * PAIR] = jnp.concatenate(keys_turned, axis=0).T.astype(BF16)
    d_values = jnp.concatenate(values_turned, axis=0).T.astype(BF16)
    grad_ref[:, 2 * PAIR :] = d_values
    sum_ref[...] = column_sum(grad_ref[...].astype(F32))

    @pl.when(pl.program_id(0) == 0)
    def _():
        total_ref[...] = d_mid_ref[...]

    w_part = jnp.concatenate([w_q_ref[...], w_k_ref[...], w_v_ref[...]], axis=1)
    total_ref[...] += dot_nt(grad_ref[...], w_part)
    half = keep_ref.shape[0]
    keep_ref[...] = dot_nn(rows_turned_ref[:half, :], grad_ref[...]).astype(BF16)
    send_ref[...] = dot_nn(rows_turned_ref[half:, :], grad_ref[...]).astype(BF16)

    @pl.when(pl.program_id(0) == pl.num_programs(0) - 1)
    def _():
        text_grad_ref[...] = total_ref[:text_count, :].astype(BF16)
        region_grad_ref[...] = total_ref[text_count:, :].astype(BF16)


def attend_back(qkv_text, qkv_region, w_qkv, chance, inv, ctx, d_ctx, d_mid, rows_turned):
    text_count, slots = qkv_text.shape[0], qkv_region.shape[0]
    count = text_count + slots
    return pl.pallas_call(
        attend_back_body,
        grid=(PAIRS,),
        in_specs=thirds(text_count)
        + thirds(slots)
        + thirds(D)
        + [
            pl.BlockSpec((2, count, count), lambda p: (p, 0, 0)),
            pl.BlockSpec((count, PAIR), lambda p: (0, p)),
            pl.BlockSpec((count, PAIR), lambda p: (0, p)),
            pl.BlockSpec((count, PAIR), lambda p: (0, p)),
            whole((count, D)),
            whole((D, count)),
        ],
        out_specs=[
            pl.BlockSpec((D // 2, 3 * PAIR), lambda p: (0, p)),
            pl.BlockSpec((D // 2, 3 * PAIR), lambda p: (0, p)),
            pl.BlockSpec((1, 3 * PAIR), lambda p: (0, p)),
            whole((text_count, D)),
            whole((slots, D)),
        ],
        out_shape=(
            struct((D // 2, 3 * D), BF16),
            struct((D // 2, 3 * D), BF16),
            struct((1, 3 * D), F32),
            struct((text_count, D), BF16),
            struct((slots, D), BF16),
        ),
        scratch_shapes=[pltpu.VMEM((count, D), F32), pltpu.VMEM((count, 3 * PAIR), BF16)],
        cost_estimate=cost(8 * count * count * D * 4 + 12 * count * D * D, HEADS * count * count * 2),
        name="attend_back",
    )(*(qkv_text,) * 3, *(qkv_region,) * 3, *(w_qkv,) * 3, chance, inv, ctx, d_ctx, d_mid, rows_turned)


def gelu_parts(inputs):
    weight = jnp.exp2(inputs * inputs * (-0.5 * 1.4426950408889634))
    place = 1.0 / (1.0 + jnp.abs(inputs) * TAIL_RATE)
    poly = 0.5 * TAIL[4]
    for factor in TAIL[3::-1]:
        poly = poly * place + 0.5 * factor
    tail = weight * (poly * place)
    phi_sum = jnp.where(inputs >= 0.0, 1.0 - tail, tail)
    return inputs * phi_sum, phi_sum + inputs * weight * 0.3989422804014327


def feed_body(
    ctx_ref,
    w_out_ref,
    text_ref,
    region_ref,
    perm_ref,
    out_bias_ref,
    attn_gain_ref,
    attn_shift_ref,
    down_bias_ref,
    ffn_gain_ref,
    ffn_shift_ref,
    w_up_ref,
    up_bias_ref,
    w_down_ref,
    cot_text_ref,
    cot_region_ref,
    hidden_ref,
    slope_ref,
    norm_ref,
    inv_ref,
    rows_turned_ref,
    ctx_turned_ref,
    low_turned_ref,
    text_out_ref,
    region_out_ref,
    d_second_ref,
    d_down_ref,
    stats_ref,
    normed_ref,
    low_ref,
    total_ref,
):
    step = pl.program_id(0)
    text_count = text_ref.shape[0]
    count = ctx_ref.shape[0]
    parts = [(start, start + 256) for start in range(0, count, 256)]

    def each(body):
        @pl.loop(0, text_count // 256)
        def _(part):
            rows = pl.ds(pl.multiple_of(part * 256, 256), 256)
            body(rows, 0, rows)

        for start in range(text_count, count, 256):
            body(pl.ds(start, 256), 1, pl.ds(start - text_count, 256))

    @pl.when(step == 0)
    def _():
        def first(rows, side, own):
            inputs = (text_ref, region_ref)[side][own, :]
            ctx = ctx_ref[rows, :]
            attn_out = dot_nn(ctx, w_out_ref[...]) + row_of(out_bias_ref)
            norm, inv = standardize(inputs.astype(F32) + attn_out)
            normed = norm * row_of(attn_gain_ref) + row_of(attn_shift_ref)
            low = normed.astype(BF16)
            norm_ref[rows, :] = norm
            inv_ref[rows, :] = inv
            normed_ref[rows, :] = normed
            low_ref[rows, :] = low
            total_ref[rows, :] = normed + row_of(down_bias_ref)
            rows_turned_ref[:, rows] = dot_nt(perm_ref[...], inputs).astype(BF16)
            ctx_turned_ref[:, rows] = dot_nt(perm_ref[...], ctx).astype(BF16)
            low_turned_ref[:, rows] = dot_nt(perm_ref[...], low).astype(BF16)

        each(first)

    def up_of(start, stop):
        return dot_nn(low_ref[start:stop, :], w_up_ref[...]) + up_bias_ref[...]

    following = up_of(*parts[0])
    for index, (start, stop) in enumerate(parts):
        up_sum = following
        if index + 1 < len(parts):
            following = up_of(*parts[index + 1])
        value, slope = gelu_parts(up_sum)
        hidden = value.astype(BF16)
        hidden_ref[start:stop, :] = hidden
        slope_ref[start:stop, :] = slope.astype(BF16)
        total_ref[start:stop, :] += dot_nn(hidden, w_down_ref[...])

    @pl.when(step == pl.num_programs(0) - 1)
    def _():
        stats_ref[...] = jnp.zeros(stats_ref.shape, F32)

        def last(rows, side, own):
            norm, inv = standardize(total_ref[rows, :])
            out_ref = (text_out_ref, region_out_ref)[side]
            out_ref[own, :] = (norm * row_of(ffn_gain_ref) + row_of(ffn_shift_ref)).astype(BF16)
            upstream = (cot_text_ref, cot_region_ref)[side][own, :].astype(F32)
            d_second = standardize_back(upstream * row_of(ffn_gain_ref), norm, inv)
            d_down = d_second.astype(BF16)
            d_second_ref[rows, :] = d_second
            d_down_ref[rows, :] = d_down
            stats_ref[0:1, :] += column_sum(upstream * norm)
            stats_ref[1:2, :] += column_sum(upstream)
            stats_ref[2:3, :] += column_sum(d_down.astype(F32))

        each(last)


def feed_forward(ctx, w_out, text, arrived, perm, vecs, w_up, up_bias, w_down, cot_text, cot_region):
    count, text_count = ctx.shape[0], text.shape[0]
    slots = count - text_count
    units = w_up.shape[1]
    chunk = 512
    half = D // 2
    return pl.pallas_call(
        feed_body,
        grid=(units // chunk,),
        in_specs=[
            whole((count, D)),
            whole((D, D)),
            whole((text_count, D)),
            whole((slots, D)),
            whole((D, D)),
        ]
        + [whole((D,))] * len(vecs)
        + [
            pl.BlockSpec((D, chunk), lambda j: (0, j)),
            pl.BlockSpec((1, chunk), lambda j: (0, j)),
            pl.BlockSpec((chunk, D), lambda j: (j, 0)),
            whole((text_count, D)),
            whole((slots, D)),
        ],
        out_specs=[
            pl.BlockSpec((count, chunk), lambda j: (0, j)),
            pl.BlockSpec((count, chunk), lambda j: (0, j)),
            whole((count, D)),
            whole((count, 1)),
            whole((D, count)),
            whole((D, count)),
            whole((D, count)),
            whole((text_count, D)),
            whole((slots, D)),
            whole((count, D)),
            whole((count, D)),
            whole((8, D)),
        ],
        out_shape=(
            struct((count, units), BF16),
            struct((count, units), BF16),
            struct((count, D), F32),
            struct((count, 1), F32),
            struct((D, count), BF16),
            struct((D, count), BF16),
            struct((D, count), BF16),
            struct((text_count, D), BF16),
            struct((slots, D), BF16),
            struct((count, D), F32),
            struct((count, D), BF16),
            struct((8, D), F32),
        ),
        scratch_shapes=[
            pltpu.VMEM((count, D), F32),
            pltpu.VMEM((count, D), BF16),
            pltpu.VMEM((count, D), F32),
        ],
        cost_estimate=cost(4 * count * D * units + 8 * count * D * D, 4 * D * units + 4 * count * units, count * units),
        name="feed_forward",
    )(ctx, w_out, text, arrived, perm, *vecs, w_up, up_bias, w_down, cot_text, cot_region)


def feed_back_body(
    d_down_ref,
    slope_ref,
    w_down_ref,
    w_up_ref,
    d_second_ref,
    norm_ref,
    inv_ref,
    gain_ref,
    w_out_ref,
    low_turned_ref,
    ctx_turned_ref,
    up_keep_ref,
    up_send_ref,
    out_keep_ref,
    out_send_ref,
    up_sum_ref,
    d_mid_ref,
    d_ctx_ref,
    stats_ref,
    total_ref,
    d_up_ref,
    d_attn_ref,
):
    step = pl.program_id(0)
    count = d_down_ref.shape[0]
    parts = [(start, start + 256) for start in range(0, count, 256)]

    @pl.when(step == 0)
    def _():
        total_ref[...] = d_second_ref[...]

    up_total = jnp.zeros(up_sum_ref.shape, F32)
    def hidden_of(start, stop):
        return dot_nt(d_down_ref[start:stop, :], w_down_ref[...])

    following = hidden_of(*parts[0])
    for index, (start, stop) in enumerate(parts):
        d_hidden = following
        if index + 1 < len(parts):
            following = hidden_of(*parts[index + 1])
        d_up = (d_hidden * slope_ref[start:stop, :].astype(F32)).astype(BF16)
        d_up_ref[start:stop, :] = d_up
        up_total = up_total + column_sum(d_up.astype(F32))
        total_ref[start:stop, :] += dot_nt(d_up, w_up_ref[...])
    up_sum_ref[...] = up_total
    half = up_keep_ref.shape[0]
    up_keep_ref[...] = dot_nn(low_turned_ref[:half, :], d_up_ref[...]).astype(BF16)
    up_send_ref[...] = dot_nn(low_turned_ref[half:, :], d_up_ref[...]).astype(BF16)

    @pl.when(step == pl.num_programs(0) - 1)
    def _():
        stats_ref[...] = jnp.zeros(stats_ref.shape, F32)

        @pl.loop(0, len(parts))
        def _(part):
            rows = pl.ds(pl.multiple_of(part * 256, 256), 256)
            d_first = total_ref[rows, :]
            norm = norm_ref[rows, :]
            d_mid = standardize_back(d_first * row_of(gain_ref), norm, inv_ref[rows, :])
            d_attn = d_mid.astype(BF16)
            d_mid_ref[rows, :] = d_mid
            d_attn_ref[rows, :] = d_attn
            d_ctx_ref[rows, :] = dot_nt(d_attn, w_out_ref[...]).astype(BF16)
            stats_ref[0:1, :] += column_sum(d_first * norm)
            stats_ref[1:2, :] += column_sum(d_first)
            stats_ref[2:3, :] += column_sum(d_attn.astype(F32))

        out_keep_ref[...] = dot_nn(ctx_turned_ref[:half, :], d_attn_ref[...]).astype(BF16)
        out_send_ref[...] = dot_nn(ctx_turned_ref[half:, :], d_attn_ref[...]).astype(BF16)


def feed_back(d_down, slope, w_down, w_up, d_second, norm, inv, gain, w_out, low_turned, ctx_turned):
    count, units = slope.shape
    chunk = 512
    return pl.pallas_call(
        feed_back_body,
        grid=(units // chunk,),
        in_specs=[
            whole((count, D)),
            pl.BlockSpec((count, chunk), lambda j: (0, j)),
            pl.BlockSpec((chunk, D), lambda j: (j, 0)),
            pl.BlockSpec((D, chunk), lambda j: (0, j)),
            whole((count, D)),
            whole((count, D)),
            whole((count, 1)),
            whole((D,)),
            whole((D, D)),
            whole((D, count)),
            whole((D, count)),
        ],
        out_specs=[
            pl.BlockSpec((D // 2, chunk), lambda j: (0, j)),
            pl.BlockSpec((D // 2, chunk), lambda j: (0, j)),
            whole((D // 2, D)),
            whole((D // 2, D)),
            pl.BlockSpec((1, chunk), lambda j: (0, j)),
            whole((count, D)),
            whole((count, D)),
            whole((8, D)),
        ],
        out_shape=(
            struct((D // 2, units), BF16),
            struct((D // 2, units), BF16),
            struct((D // 2, D), BF16),
            struct((D // 2, D), BF16),
            struct((1, units), F32),
            struct((count, D), F32),
            struct((count, D), BF16),
            struct((8, D), F32),
        ),
        scratch_shapes=[
            pltpu.VMEM((count, D), F32),
            pltpu.VMEM((count, chunk), BF16),
            pltpu.VMEM((count, D), BF16),
        ],
        cost_estimate=cost(6 * count * D * units + 4 * count * D * D, 4 * D * units + 4 * count * units),
        name="feed_back",
    )(d_down, slope, w_down, w_up, d_second, norm, inv, gain, w_out, low_turned, ctx_turned)


def region_back_body(
    back_ref,
    hot_ref,
    norm_ref,
    inv_ref,
    gain_ref,
    boxes_ref,
    qkv_ref,
    attn_ref,
    ffn_ref,
    up_ref,
    perm_ref,
    d_proj_ref,
    *piece_refs,
):
    rows = norm_ref.shape[0]
    d_region = dot_tn(hot_ref[...], back_ref[...])
    norm = norm_ref[...]
    d_pre = standardize_back(d_region * row_of(gain_ref), norm, inv_ref[...])
    d_proj = d_pre.astype(BF16)
    d_proj_ref[...] = d_proj
    boxes = jnp.concatenate([boxes_ref[...], jnp.zeros((4, rows), F32)], axis=0).T
    vectors = [column_sum(d_pre), column_sum(d_region * norm), column_sum(d_region)]
    vectors += [column_sum(boxes[:, side : side + 1] * d_pre) for side in range(4)]
    for part in (0, 2):
        starts = [(3 * pair + part) * PAIR for pair in range(PAIRS)]
        vectors.append(jnp.concatenate([qkv_ref[:, start : start + PAIR] for start in starts], axis=1))
    for ref in (attn_ref, ffn_ref):
        vectors += [ref[2:3, :], ref[0:2, :]]
    vectors.append(up_ref[...])
    filled = sum(vector.shape[0] for vector in vectors)
    vectors.append(jnp.zeros((VECS - filled, D), F32))
    low_vectors = jnp.concatenate(vectors, axis=0).astype(BF16)
    turned = dot_nt(perm_ref[...], jnp.concatenate([d_proj, low_vectors], axis=0)).astype(BF16)
    size = D // len(piece_refs)
    for index, piece_ref in enumerate(piece_refs):
        piece_ref[...] = turned[index * size : (index + 1) * size]


def region_back(back, hot, norm, *others):
    rows = norm.shape[0]
    return pl.pallas_call(
        region_back_body,
        out_shape=(struct((rows, D), BF16),) + (struct((D // 4, rows + VECS), BF16),) * 4,
        cost_estimate=cost(0, 0),
        name="region_back",
    )(back, hot, norm, *others)


def swap_cores(sent):
    return lax.ppermute(sent, "enc", [(0, 1), (1, 0)])


def swap_chips(sent, offset, peers):
    return lax.ppermute(sent, "dp", [(peer, peer ^ offset) for peer in range(peers)])


MASKS = (0, 1, 3, 2)


def reverse(value, width):
    result = value & 0
    for bit in range(width):
        result = result | (((value >> bit) & 1) << (width - 1 - bit))
    return result


def after(first, *others):
    if not others:
        return first
    return lax.optimization_barrier((first,) + others)[0]


def swap_cores(sent):
    return [lax.ppermute(array, "enc", [(0, 1), (1, 0)]) for array in sent]


def swap_chips(sent, mask, peers):
    return lax.ppermute(sent, "dp", [(peer, peer ^ mask) for peer in range(peers)])


def combine_body(plans, counts, *refs):
    refs, out_refs = refs[:counts], refs[counts:]
    for out_ref, (unit, segments) in zip(out_refs, plans):

        def add(start, size, segments=segments, out_ref=out_ref):
            for place, at, terms in segments:
                sums = [refs[index][pl.ds(start, size), left:right].astype(F32) for index, left, right in terms]
                value = functools.reduce(jnp.add, sums).astype(out_ref.dtype)
                out_ref[pl.ds(place + start, size), at : at + value.shape[1]] = value

        if unit % 32 or unit < 64:
            add(0, unit)
        else:

            @pl.loop(0, unit // 32)
            def _(step, add=add):
                add(pl.multiple_of(step * 32, 32), 32)


def segments_of(terms, columns):
    edges = set()
    for array, _, first in terms:
        edges |= {first, first + array.shape[1]}
    for left, right in columns:
        inside = sorted({left, right} | {edge for edge in edges if left < edge < right})
        yield from zip(inside, inside[1:])


def combine_plain(terms, start, stop, columns, dtype):
    sums = []
    for left, right in segments_of(terms, columns):
        blocks = [
            array[row + start : row + stop, left - first : right - first].astype(F32)
            for array, row, first in terms
            if first <= left and right <= first + array.shape[1]
        ]
        sums.append(functools.reduce(jnp.add, blocks))
    return jnp.concatenate(sums, axis=1).astype(dtype)


def combine(wanted, name):
    plans, operands, specs, shapes, known = [], [], [], [], {}
    for terms, start, stop, columns, dtype in wanted:
        unit = functools.reduce(math.gcd, [value for _, row, _ in terms for value in (row + start, row + stop)])
        if unit % 8:
            return [combine_plain(*each) for each in wanted]
        segments = []
        for place in range(0, stop - start, unit):
            at = 0
            for left, right in segments_of(terms, columns):
                sources = []
                for array, row, first in terms:
                    if first <= left and right <= first + array.shape[1]:
                        block = (row + start + place) // unit
                        key = (id(array), unit, block)
                        if key not in known:
                            known[key] = len(operands)
                            operands.append(array)
                            specs.append(pl.BlockSpec((unit, array.shape[1]), lambda j, block=block: (block, 0)))
                        sources.append((known[key], left - first, right - first))
                segments.append((place, at, sources))
                at += right - left
        plans.append((unit, segments))
        shapes.append(struct((stop - start, at), dtype))
    return pl.pallas_call(
        functools.partial(combine_body, plans, len(operands)),
        grid=(1,),
        in_specs=specs,
        out_specs=[pl.BlockSpec(shape.shape, lambda j: (0, 0)) for shape in shapes],
        out_shape=tuple(shapes),
        cost_estimate=cost(0, 0),
        name=name,
    )(*operands)


def side_by_side(*arrays):
    terms, first = [], 0
    for array in arrays:
        terms.append((array, 0, first))
        first += array.shape[1]
    return terms


class Pair:
    def __init__(self, terms, rows, middle, width, peers):
        self.terms, self.size, self.middle, self.width, self.peers = terms, rows // 4, middle, width, peers
        self.sides = [(0, middle)], [(middle, width)]

    def start(self):
        size, (first, second) = self.size, self.sides
        wanted = [(self.terms, size, 3 * size, first, BF16), (self.terms, 2 * size, 4 * size, second, BF16)]
        self.sent = list(combine(wanted, "pair_start"))
        return self.sent

    def ship(self):
        self.got = [swap_chips(sent, bit, self.peers) for sent, bit in zip(self.sent, (1, 2))]
        return self.got

    def hold(self, *behind):
        self.got = [after(array, *behind) for array in self.got]

    def turn(self):
        size, (first, second), (one, two) = self.size, self.sides, self.got
        wanted = [
            (self.terms + [(one, -2 * size, 0)], 3 * size, 4 * size, first, BF16),
            (self.terms + [(two, -size, self.middle)], size, 2 * size, second, BF16),
        ]
        self.sent = list(combine(wanted, "pair_turn"))
        return self.sent

    def finish(self):
        last = [swap_chips(sent, bit, self.peers) for sent, bit in zip(self.sent, (2, 1))]
        (one, two), middle = self.got, self.middle
        arrived = [(one, 0, 0), (two, self.size, middle), (last[0], 0, 0), (last[1], 0, middle)]
        return Scatter(self.terms + arrived, self.size, self.width, self.peers, 2, 2)


class Scatter:
    def __init__(self, terms, rows, width, peers, bit, fresh):
        self.terms, self.rows, self.width, self.peers, self.bit, self.fresh = terms, rows, width, peers, bit, fresh

    def cut(self, bits, *behind):
        self.bits = min(bits, self.peers.bit_length() - 1 - self.bit)
        self.rows >>= self.bits
        wanted = [
            (self.terms, offset * self.rows, (offset + 1) * self.rows, [(0, self.width)], BF16)
            for offset in range(1, 1 << self.bits)
        ]
        self.sent = [after(array, *behind) for array in combine(wanted, "cut")]
        return self.sent

    def ship(self):
        masks = [reverse(offset, self.bits) << self.bit for offset in range(1, 1 << self.bits)]
        got = [swap_chips(sent, mask, self.peers) for sent, mask in zip(self.sent, masks)]
        self.terms = self.terms + side_by_side_rows(got)
        self.bit += self.bits
        self.fresh = len(got)
        return got

    def hold(self, *behind):
        late = [(after(array, *behind), row, first) for array, row, first in self.terms[-self.fresh :]]
        self.terms = self.terms[: -self.fresh] + late

    def finish(self, bits):
        while 1 << self.bit < self.peers:
            self.cut(bits)
            self.ship()
        return self

    def shares(self, *ranges):
        return [(self.terms, 0, self.rows, columns, F32) for columns in ranges]


def side_by_side_rows(arrays):
    return [(array, 0, 0) for array in arrays]


def direct(terms, rows, width, peers, bit):
    size = rows // 4
    wanted = [(terms, place * size, (place + 1) * size, [(0, width)], BF16) for place in range(1, 4)]
    sent = combine(wanted, "direct")
    got = [swap_chips(array, mask, peers) for array, mask in zip(sent, MASKS[1:])]
    return sent, Scatter(terms + side_by_side_rows(got), size, width, peers, bit, 3)


def swap_near(pieces, peers):
    return [swap_chips(piece, offset << 2, peers) for offset, piece in enumerate(pieces[1:], 1)]


def place_of(block, peers):
    rest = peers // 4
    top = block // rest
    return (top ^ (top >> 1)) + (reverse(block % rest, rest.bit_length() - 1) << 2)


def units_body(order_ref, *refs):
    kept, got = refs[:-3:2], refs[1:-3:2]
    near_ref, far_ref, keep_ref = refs[-3:]
    step, half = pl.program_id(0), near_ref.shape[1]
    rows = [(one[...].astype(F32) + two[...].astype(F32)).astype(BF16) for one, two in zip(kept, got)]
    rows = jnp.concatenate(rows, axis=0)
    keep_ref[...] = rows

    @pl.when((step == 1) | (step == 2))
    def _():
        near_ref[...] = rows[:, :half]

    @pl.when(step >= 2)
    def _():
        far_ref[...] = rows[:, half:]


def cut_units(kept, got, order, peers):
    count, width = kept.shape
    size, half, rest = count // peers, width // 2, peers // 4
    if size % 16:
        rows = (kept.astype(F32) + got.astype(F32)).reshape(peers, size, width)
        rows = jnp.take(rows, order, axis=0).reshape(count, width).astype(BF16)
        return rows[count // 4 : 3 * count // 4, :half], rows[count // 2 :, half:], rows
    specs = []
    for index in range(rest):
        specs += [pl.BlockSpec((size, width), lambda j, order, index=index: (order[j * rest + index], 0))] * 2
    return pl.pallas_call(
        units_body,
        grid_spec=pltpu.PrefetchScalarGridSpec(
            num_scalar_prefetch=1,
            grid=(4,),
            in_specs=specs,
            out_specs=[
                pl.BlockSpec((count // 4, half), lambda j, order: (jnp.clip(j - 1, 0, 1), 0)),
                pl.BlockSpec((count // 4, half), lambda j, order: (jnp.clip(j - 2, 0, 1), 0)),
                pl.BlockSpec((count // 4, width), lambda j, order: (j, 0)),
            ],
        ),
        out_shape=(struct((count // 2, half), BF16), struct((count // 2, half), BF16), struct((count, width), BF16)),
        cost_estimate=cost(count * width, 8 * count * width),
        name="cut_units",
    )(order, *(kept, got) * rest)


def region_product_body(*refs):
    *refs, keep_ref, send_ref = refs
    pieces, feats = refs[: len(refs) // 2], refs[len(refs) // 2 :]
    rows, width = feats[0].shape
    half = keep_ref.shape[0]
    turned = jnp.concatenate([piece[:, :rows] for piece in pieces], axis=1)
    vectors = functools.reduce(jnp.add, [piece[:, rows:].astype(F32) for piece in pieces])
    product = dot_nn(turned, jnp.concatenate([ref[...] for ref in feats], axis=0)).astype(BF16)
    for ref, start in ((keep_ref, 0), (send_ref, half)):
        ref[:, :width] = product[start : start + half]
        ref[:, width:] = vectors[start : start + half].astype(BF16)


def region_product(pieces, feats):
    half, width = pieces[0].shape[0] // 2, feats[0].shape[1] + VECS
    return pl.pallas_call(
        region_product_body,
        out_shape=(struct((half, width), BF16), struct((half, width), BF16)),
        cost_estimate=cost(0, 0),
        name="region_product",
    )(*pieces, *feats)


def one_hot_rows(core, place, inner, peers):
    share = D // (2 * peers)
    core, place = core ^ lax.axis_index("enc"), place ^ lax.axis_index("dp")
    row = (core * peers + place) * share + inner
    return (lax.broadcasted_iota(jnp.int32, (D, D), 1) == row).astype(BF16)


def share_order(peers):
    share = D // (2 * peers)
    row = lax.broadcasted_iota(jnp.int32, (D, 1), 0)
    block = row // share
    return one_hot_rows(block // peers, place_of(block % peers, peers), row % share, peers)


def region_order(peers):
    share, rest = D // (2 * peers), peers // 16
    row = lax.broadcasted_iota(jnp.int32, (D, 1), 0)
    block = row // share
    top = (block // rest) % 4
    place = (top ^ (top >> 1)) + ((block // (8 * rest)) << 2) + (reverse(block % rest, rest.bit_length() - 1) << 4)
    return one_hot_rows((block // (4 * rest)) % 2, place, row % share, peers)


def exchange(array):
    return lax.all_to_all(array, "dp", split_axis=0, concat_axis=0, tiled=True)


def per_device(
    text_in,
    text_lengths,
    region_feats,
    region_boxes,
    region_dest,
    region_seq,
    w_region,
    w_box,
    type_embed,
    region_gain,
    region_shift,
    w_qkv,
    q_bias,
    v_bias,
    w_out,
    out_bias,
    attn_gain,
    attn_shift,
    w_up,
    up_bias,
    w_down,
    down_bias,
    ffn_gain,
    ffn_shift,
    cot_text,
    cot_region,
):
    peers = lax.axis_size("dp")
    source_rows = region_feats.shape[0]
    capacity = max(2, 2 * source_rows // peers)
    slots = peers * capacity
    text_count = text_in.shape[0]
    units = w_up.shape[1]

    def row(vector):
        return vector.reshape(1, -1)

    outgoing, cot_sent, hot, region_norm, region_inv = region_forward(
        capacity,
        slots,
        region_feats,
        w_region,
        region_boxes,
        row(region_dest),
        row(region_seq),
        w_box,
        type_embed,
        region_gain,
        region_shift,
        cot_region,
    )
    arrived = exchange(outgoing)
    arrived_cot = exchange(cot_sent)

    far_feats = swap_near([region_feats] + [after(region_feats, arrived)] * 3, peers)

    bias = jnp.concatenate([q_bias, jnp.zeros_like(q_bias), v_bias])[None]
    perm, region_perm = lax.optimization_barrier((share_order(peers), region_order(peers)))
    order = place_of(jnp.arange(peers, dtype=jnp.int32), peers) ^ lax.axis_index("dp")
    qkv_text = (dot_nn(text_in, w_qkv) + bias).astype(BF16)
    qkv_region = (dot_nn(arrived[:, :D], w_qkv) + bias).astype(BF16)
    context, chance, chance_inv = attend(text_lengths, arrived, qkv_text, qkv_region)
    vecs = (out_bias, attn_gain, attn_shift, down_bias, ffn_gain, ffn_shift)
    (
        hidden,
        slope,
        norm,
        inv,
        rows_turned,
        ctx_turned,
        low_turned,
        text_out,
        region_sent,
        d_second,
        d_down,
        ffn_stats,
    ) = feed_forward(context, w_out, text_in, arrived, perm, vecs, w_up, row(up_bias), w_down, cot_text, arrived_cot)

    d_down = after(d_down, *far_feats)
    core = lax.axis_index("enc")
    half = units // 2

    def unit_product(which):
        side = lax.dynamic_slice_in_dim(hidden, which * half, half, axis=1)
        return dot_tn(side, d_down).astype(BF16)

    (got,) = swap_cores([unit_product(1 - core)])
    *sent, kept = cut_units(unit_product(core), got, order, peers)
    down = Pair([(kept, 0, 0)], half, D // 2, D, peers)
    down.sent = sent
    covered = after(d_down, *sent)
    near = down.ship()
    up_keep, up_send, out_keep, out_send, up_grad, d_mid, d_ctx, attn_stats = feed_back(
        covered, slope, w_down, w_up, d_second, norm, inv, attn_gain, w_out, low_turned, ctx_turned
    )
    up_send, out_send = lax.optimization_barrier((up_send, out_send, *near))[:2]
    got = swap_cores([up_send, out_send])
    down.turn()
    down = down.finish()
    up_out = Pair(
        side_by_side(up_keep, out_keep) + side_by_side(*got), D // 2, (units + D) // 2, units + D, peers
    )
    sent = up_out.start()
    near = up_out.ship()
    returned = exchange(after(region_sent, *sent))
    down.hold(*sent)
    covered = after(d_ctx, *sent, *down.cut(2))
    far = down.ship()
    qkv_keep, qkv_send, qkv_sums, text_grad, d_rows_region = attend_back(
        qkv_text, qkv_region, w_qkv, chance, chance_inv, context, covered, d_mid, rows_turned
    )
    qkv_send = after(qkv_send, returned, *near, *far)
    (got,) = swap_cores([qkv_send])
    sent_back = exchange(after(d_rows_region, qkv_send))
    qkv = Pair([(qkv_keep, 0, 0), (got, 0, 0)], D // 2, 3 * D // 2, 3 * D, peers)
    sent = qkv.start()
    qkv_got = qkv.ship()
    up_out.hold(*sent)
    sent = up_out.turn()
    up_out = up_out.finish()
    sent_back = after(sent_back, *qkv_got)

    share = D // (2 * peers)
    quarter = units // D
    up_rows = after(up_grad, *sent).reshape(2 * peers, quarter, share).transpose(1, 0, 2).reshape(quarter, D)
    d_proj, *pieces = region_back(
        sent_back,
        hot,
        region_norm,
        region_inv,
        region_gain,
        region_boxes,
        qkv_sums,
        attn_stats,
        ffn_stats,
        up_rows,
        region_perm,
    )
    feats_width = region_feats.shape[1]
    up_out.hold(*pieces)
    qkv.hold(*pieces)
    region_got = swap_near(pieces, peers)
    qkv.turn()
    qkv = qkv.finish()
    qkv_got = [array for array, _, _ in qkv.terms[-qkv.fresh :]]
    sent = up_out.cut(1)
    up_out.ship()
    region_got = [after(array, *qkv_got, *sent) for array in region_got]
    last_keep, last_send = region_product(pieces[:1] + region_got, [region_feats] + far_feats)
    (got,) = swap_cores([last_send])
    qkv.hold(last_send)
    qkv.cut(1)
    qkv.ship()
    last_sent, last = direct(
        [(last_keep, 0, 0), (got, 0, 0)], last_keep.shape[0], feats_width + VECS, peers, 4
    )
    qkv.hold(*last_sent)
    up_out.hold(*last_sent)
    down.hold(*last_sent)
    sent = up_out.cut(1)
    up_out.ship()
    d_proj, returned = lax.optimization_barrier((d_proj, returned, *sent))[:2]
    region_out = dot_tn(hot, returned).astype(BF16)
    feats_grad = dot_nt(d_proj, w_region).astype(BF16)
    starts = [(3 * pair + part) * PAIR for part in range(3) for pair in range(PAIRS)]
    heads = [(start, start + PAIR) for start in starts]
    w_qkv_share, w_up_share, w_out_share, w_down_share = combine(
        qkv.finish(1).shares(heads)
        + up_out.finish(1).shares([(0, units)], [(units, units + D)])
        + down.finish(2).shares([(0, D)]),
        "shares",
    )
    w_region_share, vectors = combine(
        last.finish(2).shares([(0, feats_width)], [(feats_width, feats_width + VECS)]), "last_shares"
    )
    vectors = vectors.T
    return (
        text_out,
        region_out,
        text_grad,
        feats_grad,
        w_region_share.T,
        vectors[3:7],
        vectors[0],
        vectors[1],
        vectors[2],
        w_qkv_share,
        vectors[7],
        vectors[8],
        w_out_share,
        vectors[9],
        vectors[10],
        vectors[11],
        w_up_share,
        vectors[15 : 15 + quarter].reshape(-1),
        w_down_share,
        vectors[12],
        vectors[13],
        vectors[14],
    )


def solution(mesh):
    both = ("enc", "dp")
    rows, flat, none = P(both, None), P(both), P()
    in_specs = (rows, rows, rows, P(None, both), rows, flat) + (none,) * 18 + (rows, rows)
    out_specs = (
        (rows,) * 4
        + (P(None, both), P(None, both), flat, flat, flat, rows, flat, flat, rows)
        + (flat, flat, flat, rows, flat, rows, flat, flat, flat)
    )
    return jax.shard_map(per_device, mesh=mesh, in_specs=in_specs, out_specs=out_specs, check_vma=False)
```

```python
import functools
import math

import jax
import jax.numpy as jnp
from jax import lax
from jax.experimental import pallas as pl
from jax.experimental.pallas import tpu as pltpu
from jax.sharding import PartitionSpec as P

D = 768
HEADS = 12
HDIM = 64
PAIR = 2 * HDIM
PAIRS = HEADS // 2
TAGS = 128
VECS = 128

F32 = jnp.float32
BF16 = jnp.bfloat16
eps = 1e-05
SCALE = HDIM ** (-0.5)

TAIL_RATE = 0.3275911 * 0.7071067811865476
TAIL = (0.254829592, -0.284496736, 1.421413741, -1.453152027, 1.061405429)


def dot_nn(left, right):
    return lax.dot_general(left, right, (((1,), (0,)), ((), ())), preferred_element_type=F32)


def dot_nt(left, right):
    return lax.dot_general(left, right, (((1,), (1,)), ((), ())), preferred_element_type=F32)


def dot_tn(left, right):
    return lax.dot_general(left, right, (((0,), (0,)), ((), ())), preferred_element_type=F32)


def standardize(inputs):
    row_mean = jnp.mean(inputs, axis=-1, keepdims=True)
    centred = inputs - row_mean
    spread = jnp.mean(centred * centred, axis=-1, keepdims=True)
    inv = lax.rsqrt(spread + eps)
    return centred * inv, inv


def standardize_back(grad, norm, inv):
    first = jnp.mean(grad, axis=-1, keepdims=True)
    second = jnp.mean(grad * norm, axis=-1, keepdims=True)
    return (grad - first - norm * second) * inv


def row_of(ref):
    return ref[...].reshape(1, D)


def column_sum(inputs):
    return jnp.sum(inputs, axis=0, keepdims=True)


def whole(shape):
    return pl.BlockSpec(shape, lambda *_: (0,) * len(shape), pipeline_mode=pl.Buffered(1))


def struct(shape, dtype):
    return jax.ShapeDtypeStruct(shape, dtype)


def cost(flops, moved, exps=0):
    return pl.CostEstimate(flops=int(flops), bytes_accessed=int(moved), transcendentals=int(exps))


def region_body(
    capacity,
    feats_ref,
    w_ref,
    boxes_ref,
    dest_ref,
    seq_ref,
    w_box_ref,
    type_ref,
    gain_ref,
    shift_ref,
    cot_ref,
    out_ref,
    cot_out_ref,
    hot_ref,
    norm_ref,
    inv_ref,
):
    rows = feats_ref.shape[0]
    slots = out_ref.shape[0]
    dest_row = jnp.broadcast_to(dest_ref[...].astype(F32), (rows, rows))
    dest_col = dest_row.T
    row_io = lax.broadcasted_iota(jnp.int32, (rows, rows), 0)
    col_io = lax.broadcasted_iota(jnp.int32, (rows, rows), 1)
    earlier = jnp.where((dest_col == dest_row) & (row_io < col_io), 1.0, 0.0)
    slot = dest_row[0:1, :] * capacity + column_sum(earlier)
    slot_io = lax.broadcasted_iota(jnp.int32, (slots, rows), 0).astype(F32)
    hot = jnp.where(slot_io == slot, 1.0, 0.0)
    hot_low = hot.astype(BF16)
    hot_ref[...] = hot_low
    cot_out_ref[...] = dot_nn(hot_low, cot_ref[...]).astype(BF16)
    tags = jnp.sum(hot * (seq_ref[...].astype(F32) + 1.0), axis=1, keepdims=True)
    projection = dot_nn(feats_ref[...], w_ref[...])
    boxes = jnp.concatenate([boxes_ref[...], jnp.zeros((4, rows), F32)], axis=0).T
    spatial = boxes[:, 0:1] * w_box_ref[0:1, :]
    for side in range(1, 4):
        spatial = spatial + boxes[:, side : side + 1] * w_box_ref[side : side + 1, :]
    norm, inv = standardize(projection + spatial + row_of(type_ref))
    norm_ref[...] = norm
    inv_ref[...] = inv
    low_rows = (norm * row_of(gain_ref) + row_of(shift_ref)).astype(BF16)
    out_ref[:, :D] = dot_nn(hot_low, low_rows).astype(BF16)
    out_ref[:, D:] = jnp.broadcast_to(tags, (slots, TAGS)).astype(BF16)


def region_forward(capacity, slots, feats, w_region, *others):
    rows, width = feats.shape
    return pl.pallas_call(
        functools.partial(region_body, capacity),
        out_shape=(
            struct((slots, D + TAGS), BF16),
            struct((slots, D), BF16),
            struct((slots, rows), BF16),
            struct((rows, D), F32),
            struct((rows, 1), F32),
        ),
        cost_estimate=cost(2 * rows * width * D, 2 * (rows + D) * width),
        name="region_forward",
    )(feats, w_region, *others)


def head_mask(head):
    lane = lax.broadcasted_iota(jnp.int32, (1, PAIR), 1)
    return (lane >= head * HDIM) & (lane < (head + 1) * HDIM)


def join(*refs):
    return jnp.concatenate([ref[...] for ref in refs], axis=0)


def thirds(rows):
    return [pl.BlockSpec((rows, PAIR), lambda p, *_, part=part: (0, part * PAIRS + p)) for part in range(3)]


def attend_body(
    lengths_ref,
    tag_ref,
    text_q_ref,
    text_k_ref,
    text_v_ref,
    region_q_ref,
    region_k_ref,
    region_v_ref,
    ctx_ref,
    chance_ref,
    inv_ref,
    bias_ref,
):
    text_count, slots = text_q_ref.shape[0], region_q_ref.shape[0]
    count = text_count + slots
    sequences = lengths_ref.shape[1]

    @pl.when(pl.program_id(0) == 0)
    def _():
        place = lax.broadcasted_iota(jnp.int32, (text_count, 1), 0)
        text_seg = jnp.zeros((text_count, 1), F32)
        end = jnp.int32(0)
        for index in range(sequences):
            end = end + lengths_ref[0, index]
            text_seg = text_seg + jnp.where(place >= end, 1.0, 0.0)
        region_seg = tag_ref[:, 0:1].astype(F32) - 1.0
        region_seg = jnp.where(region_seg < 0.0, float(sequences), region_seg)
        seg_col = jnp.concatenate([text_seg, region_seg], axis=0)
        seg_row = jnp.broadcast_to(seg_col, (count, 128)).T[0:1, :]
        bias_ref[...] = jnp.where(seg_col == seg_row, 0.0, -1e30)

    queries = join(text_q_ref, region_q_ref) * jnp.asarray(SCALE, BF16)
    key_rows = join(text_k_ref, region_k_ref)
    values = jnp.concatenate([join(text_v_ref, region_v_ref), jnp.ones((count, PAIR), BF16)], axis=1)
    step = 256
    first = head_mask(0)
    tasks = [(start, head) for start in range(0, count, step) for head in range(2)]

    def scores_of(start, head):
        q_part = jnp.where(head_mask(head), queries[start : start + step], jnp.zeros((), BF16))
        return dot_nt(q_part, key_rows)

    following, outs, invs = scores_of(*tasks[0]), [], []
    for index, (start, head) in enumerate(tasks):
        stop = start + step
        scores = following + bias_ref[start:stop, :]
        if index + 1 < len(tasks):
            following = scores_of(*tasks[index + 1])
        exp_terms = jnp.exp(scores - jnp.max(scores, axis=1, keepdims=True))
        low_terms = exp_terms.astype(BF16)
        chance_ref[head, start:stop, :] = low_terms
        summed = dot_nn(low_terms, values)
        inv = 1.0 / summed[:, PAIR:]
        outs.append(summed[:, :PAIR] * inv)
        invs.append(inv)
        if head == 1:
            ctx_ref[start:stop, :] = jnp.where(first, outs[0], outs[1]).astype(BF16)
            inv_ref[start:stop, :] = jnp.where(first, invs[0], invs[1])
            outs, invs = [], []


def attend(lengths, arrived, qkv_text, qkv_region):
    text_count, slots = qkv_text.shape[0], qkv_region.shape[0]
    count = text_count + slots
    return pl.pallas_call(
        attend_body,
        grid_spec=pltpu.PrefetchScalarGridSpec(
            num_scalar_prefetch=1,
            grid=(PAIRS,),
            in_specs=[pl.BlockSpec((slots, TAGS), lambda p, *_: (0, D // TAGS))] + thirds(text_count) + thirds(slots),
            out_specs=[
                pl.BlockSpec((count, PAIR), lambda p, *_: (0, p)),
                pl.BlockSpec((2, count, count), lambda p, *_: (p, 0, 0)),
                pl.BlockSpec((count, PAIR), lambda p, *_: (0, p)),
            ],
            scratch_shapes=[pltpu.VMEM((count, count), F32)],
        ),
        out_shape=(
            struct((count, D), BF16),
            struct((HEADS, count, count), BF16),
            struct((count, D), F32),
        ),
        cost_estimate=cost(4 * count * count * D * 4, HEADS * count * count * 2, HEADS * count * count),
        name="attend",
    )(lengths, arrived, *(qkv_text,) * 3, *(qkv_region,) * 3)


def attend_back_body(
    text_q_ref,
    text_k_ref,
    text_v_ref,
    region_q_ref,
    region_k_ref,
    region_v_ref,
    w_q_ref,
    w_k_ref,
    w_v_ref,
    chance_ref,
    inv_ref,
    ctx_ref,
    dctx_ref,
    d_mid_ref,
    rows_turned_ref,
    keep_ref,
    send_ref,
    sum_ref,
    text_grad_ref,
    region_grad_ref,
    total_ref,
    grad_ref,
):
    count = ctx_ref.shape[0]
    text_count = text_q_ref.shape[0]
    queries = join(text_q_ref, region_q_ref) * jnp.asarray(SCALE, BF16)
    key_rows = join(text_k_ref, region_k_ref)
    values = join(text_v_ref, region_v_ref)
    scaled = dctx_ref[...].astype(F32) * inv_ref[...]
    product = scaled * ctx_ref[...].astype(F32)
    scaled_low = scaled.astype(BF16)
    scaled_turned = scaled.T.astype(BF16)
    q_turned = queries.astype(F32).T.astype(BF16)
    step = 256
    first = head_mask(0)
    keys_turned, values_turned = [None, None], [None, None]
    tasks = [(start, head) for start in range(0, count, step) for head in range(2)]

    def d_chance_of(start, head):
        d_part = jnp.where(head_mask(head), scaled_low[start : start + step], jnp.zeros((), BF16))
        return dot_nt(d_part, values)

    following, ques = d_chance_of(*tasks[0]), []
    for index, (start, head) in enumerate(tasks):
        stop, low, high = start + step, head * HDIM, (head + 1) * HDIM
        d_chance = following
        if index + 1 < len(tasks):
            following = d_chance_of(*tasks[index + 1])
        low_terms = chance_ref[head, start:stop, :]
        delta = jnp.sum(jnp.where(head_mask(head), product[start:stop], 0.0), axis=1, keepdims=True)
        d_scores = (low_terms.astype(F32) * (d_chance - delta)).astype(BF16)
        ques.append(dot_nn(d_scores, key_rows))
        v_add = dot_nn(scaled_turned[low:high, start:stop], low_terms)
        k_add = dot_nn(q_turned[low:high, start:stop], d_scores)
        values_turned[head] = v_add if start == 0 else values_turned[head] + v_add
        keys_turned[head] = k_add if start == 0 else keys_turned[head] + k_add
        if head == 1:
            d_ques = (jnp.where(first, ques[0], ques[1]) * SCALE).astype(BF16)
            grad_ref[start:stop, :PAIR] = d_ques
            ques = []
    grad_ref[:, PAIR : 2 * PAIR] = jnp.concatenate(keys_turned, axis=0).T.astype(BF16)
    d_values = jnp.concatenate(values_turned, axis=0).T.astype(BF16)
    grad_ref[:, 2 * PAIR :] = d_values
    sum_ref[...] = column_sum(grad_ref[...].astype(F32))

    @pl.when(pl.program_id(0) == 0)
    def _():
        total_ref[...] = d_mid_ref[...]

    w_part = jnp.concatenate([w_q_ref[...], w_k_ref[...], w_v_ref[...]], axis=1)
    total_ref[...] += dot_nt(grad_ref[...], w_part)
    half = keep_ref.shape[0]
    keep_ref[...] = dot_nn(rows_turned_ref[:half, :], grad_ref[...]).astype(BF16)
    send_ref[...] = dot_nn(rows_turned_ref[half:, :], grad_ref[...]).astype(BF16)

    @pl.when(pl.program_id(0) == pl.num_programs(0) - 1)
    def _():
        text_grad_ref[...] = total_ref[:text_count, :].astype(BF16)
        region_grad_ref[...] = total_ref[text_count:, :].astype(BF16)


def attend_back(qkv_text, qkv_region, w_qkv, chance, inv, ctx, d_ctx, d_mid, rows_turned):
    text_count, slots = qkv_text.shape[0], qkv_region.shape[0]
    count = text_count + slots
    return pl.pallas_call(
        attend_back_body,
        grid=(PAIRS,),
        in_specs=thirds(text_count)
        + thirds(slots)
        + thirds(D)
        + [
            pl.BlockSpec((2, count, count), lambda p: (p, 0, 0)),
            pl.BlockSpec((count, PAIR), lambda p: (0, p)),
            pl.BlockSpec((count, PAIR), lambda p: (0, p)),
            pl.BlockSpec((count, PAIR), lambda p: (0, p)),
            whole((count, D)),
            whole((D, count)),
        ],
        out_specs=[
            pl.BlockSpec((D // 2, 3 * PAIR), lambda p: (0, p)),
            pl.BlockSpec((D // 2, 3 * PAIR), lambda p: (0, p)),
            pl.BlockSpec((1, 3 * PAIR), lambda p: (0, p)),
            whole((text_count, D)),
            whole((slots, D)),
        ],
        out_shape=(
            struct((D // 2, 3 * D), BF16),
            struct((D // 2, 3 * D), BF16),
            struct((1, 3 * D), F32),
            struct((text_count, D), BF16),
            struct((slots, D), BF16),
        ),
        scratch_shapes=[pltpu.VMEM((count, D), F32), pltpu.VMEM((count, 3 * PAIR), BF16)],
        cost_estimate=cost(8 * count * count * D * 4 + 12 * count * D * D, HEADS * count * count * 2),
        name="attend_back",
    )(*(qkv_text,) * 3, *(qkv_region,) * 3, *(w_qkv,) * 3, chance, inv, ctx, d_ctx, d_mid, rows_turned)


def gelu_parts(inputs):
    weight = jnp.exp2(inputs * inputs * (-0.5 * 1.4426950408889634))
    place = 1.0 / (1.0 + jnp.abs(inputs) * TAIL_RATE)
    poly = 0.5 * TAIL[4]
    for factor in TAIL[3::-1]:
        poly = poly * place + 0.5 * factor
    tail = weight * (poly * place)
    phi_sum = jnp.where(inputs >= 0.0, 1.0 - tail, tail)
    return inputs * phi_sum, phi_sum + inputs * weight * 0.3989422804014327


def feed_body(
    ctx_ref,
    w_out_ref,
    text_ref,
    region_ref,
    perm_ref,
    out_bias_ref,
    attn_gain_ref,
    attn_shift_ref,
    down_bias_ref,
    ffn_gain_ref,
    ffn_shift_ref,
    w_up_ref,
    up_bias_ref,
    w_down_ref,
    cot_text_ref,
    cot_region_ref,
    hidden_ref,
    slope_ref,
    norm_ref,
    inv_ref,
    rows_turned_ref,
    ctx_turned_ref,
    low_turned_ref,
    text_out_ref,
    region_out_ref,
    d_second_ref,
    d_down_ref,
    stats_ref,
    normed_ref,
    low_ref,
    total_ref,
):
    step = pl.program_id(0)
    text_count = text_ref.shape[0]
    count = ctx_ref.shape[0]
    parts = [(start, start + 256) for start in range(0, count, 256)]

    def each(body):
        @pl.loop(0, text_count // 256)
        def _(part):
            rows = pl.ds(pl.multiple_of(part * 256, 256), 256)
            body(rows, 0, rows)

        for start in range(text_count, count, 256):
            body(pl.ds(start, 256), 1, pl.ds(start - text_count, 256))

    @pl.when(step == 0)
    def _():
        def first(rows, side, own):
            inputs = (text_ref, region_ref)[side][own, :]
            ctx = ctx_ref[rows, :]
            attn_out = dot_nn(ctx, w_out_ref[...]) + row_of(out_bias_ref)
            norm, inv = standardize(inputs.astype(F32) + attn_out)
            normed = norm * row_of(attn_gain_ref) + row_of(attn_shift_ref)
            low = normed.astype(BF16)
            norm_ref[rows, :] = norm
            inv_ref[rows, :] = inv
            normed_ref[rows, :] = normed
            low_ref[rows, :] = low
            total_ref[rows, :] = normed + row_of(down_bias_ref)
            rows_turned_ref[:, rows] = dot_nt(perm_ref[...], inputs).astype(BF16)
            ctx_turned_ref[:, rows] = dot_nt(perm_ref[...], ctx).astype(BF16)
            low_turned_ref[:, rows] = dot_nt(perm_ref[...], low).astype(BF16)

        each(first)

    def up_of(start, stop):
        return dot_nn(low_ref[start:stop, :], w_up_ref[...]) + up_bias_ref[...]

    following = up_of(*parts[0])
    for index, (start, stop) in enumerate(parts):
        up_sum = following
        if index + 1 < len(parts):
            following = up_of(*parts[index + 1])
        value, slope = gelu_parts(up_sum)
        hidden = value.astype(BF16)
        hidden_ref[start:stop, :] = hidden
        slope_ref[start:stop, :] = slope.astype(BF16)
        total_ref[start:stop, :] += dot_nn(hidden, w_down_ref[...])

    @pl.when(step == pl.num_programs(0) - 1)
    def _():
        stats_ref[...] = jnp.zeros(stats_ref.shape, F32)

        def last(rows, side, own):
            norm, inv = standardize(total_ref[rows, :])
            out_ref = (text_out_ref, region_out_ref)[side]
            out_ref[own, :] = (norm * row_of(ffn_gain_ref) + row_of(ffn_shift_ref)).astype(BF16)
            upstream = (cot_text_ref, cot_region_ref)[side][own, :].astype(F32)
            d_second = standardize_back(upstream * row_of(ffn_gain_ref), norm, inv)
            d_down = d_second.astype(BF16)
            d_second_ref[rows, :] = d_second
            d_down_ref[rows, :] = d_down
            stats_ref[0:1, :] += column_sum(upstream * norm)
            stats_ref[1:2, :] += column_sum(upstream)
            stats_ref[2:3, :] += column_sum(d_down.astype(F32))

        each(last)


def feed_forward(ctx, w_out, text, arrived, perm, vecs, w_up, up_bias, w_down, cot_text, cot_region):
    count, text_count = ctx.shape[0], text.shape[0]
    slots = count - text_count
    units = w_up.shape[1]
    chunk = 512
    half = D // 2
    return pl.pallas_call(
        feed_body,
        grid=(units // chunk,),
        in_specs=[
            whole((count, D)),
            whole((D, D)),
            whole((text_count, D)),
            whole((slots, D)),
            whole((D, D)),
        ]
        + [whole((D,))] * len(vecs)
        + [
            pl.BlockSpec((D, chunk), lambda j: (0, j)),
            pl.BlockSpec((1, chunk), lambda j: (0, j)),
            pl.BlockSpec((chunk, D), lambda j: (j, 0)),
            whole((text_count, D)),
            whole((slots, D)),
        ],
        out_specs=[
            pl.BlockSpec((count, chunk), lambda j: (0, j)),
            pl.BlockSpec((count, chunk), lambda j: (0, j)),
            whole((count, D)),
            whole((count, 1)),
            whole((D, count)),
            whole((D, count)),
            whole((D, count)),
            whole((text_count, D)),
            whole((slots, D)),
            whole((count, D)),
            whole((count, D)),
            whole((8, D)),
        ],
        out_shape=(
            struct((count, units), BF16),
            struct((count, units), BF16),
            struct((count, D), F32),
            struct((count, 1), F32),
            struct((D, count), BF16),
            struct((D, count), BF16),
            struct((D, count), BF16),
            struct((text_count, D), BF16),
            struct((slots, D), BF16),
            struct((count, D), F32),
            struct((count, D), BF16),
            struct((8, D), F32),
        ),
        scratch_shapes=[
            pltpu.VMEM((count, D), F32),
            pltpu.VMEM((count, D), BF16),
            pltpu.VMEM((count, D), F32),
        ],
        cost_estimate=cost(4 * count * D * units + 8 * count * D * D, 4 * D * units + 4 * count * units, count * units),
        name="feed_forward",
    )(ctx, w_out, text, arrived, perm, *vecs, w_up, up_bias, w_down, cot_text, cot_region)


def feed_back_body(
    d_down_ref,
    slope_ref,
    w_down_ref,
    w_up_ref,
    d_second_ref,
    norm_ref,
    inv_ref,
    gain_ref,
    w_out_ref,
    low_turned_ref,
    ctx_turned_ref,
    up_keep_ref,
    up_send_ref,
    out_keep_ref,
    out_send_ref,
    up_sum_ref,
    d_mid_ref,
    d_ctx_ref,
    stats_ref,
    total_ref,
    d_up_ref,
    d_attn_ref,
):
    step = pl.program_id(0)
    count = d_down_ref.shape[0]
    parts = [(start, start + 256) for start in range(0, count, 256)]

    @pl.when(step == 0)
    def _():
        total_ref[...] = d_second_ref[...]

    up_total = jnp.zeros(up_sum_ref.shape, F32)
    def hidden_of(start, stop):
        return dot_nt(d_down_ref[start:stop, :], w_down_ref[...])

    following = hidden_of(*parts[0])
    for index, (start, stop) in enumerate(parts):
        d_hidden = following
        if index + 1 < len(parts):
            following = hidden_of(*parts[index + 1])
        d_up = (d_hidden * slope_ref[start:stop, :].astype(F32)).astype(BF16)
        d_up_ref[start:stop, :] = d_up
        up_total = up_total + column_sum(d_up.astype(F32))
        total_ref[start:stop, :] += dot_nt(d_up, w_up_ref[...])
    up_sum_ref[...] = up_total
    half = up_keep_ref.shape[0]
    up_keep_ref[...] = dot_nn(low_turned_ref[:half, :], d_up_ref[...]).astype(BF16)
    up_send_ref[...] = dot_nn(low_turned_ref[half:, :], d_up_ref[...]).astype(BF16)

    @pl.when(step == pl.num_programs(0) - 1)
    def _():
        stats_ref[...] = jnp.zeros(stats_ref.shape, F32)

        @pl.loop(0, len(parts))
        def _(part):
            rows = pl.ds(pl.multiple_of(part * 256, 256), 256)
            d_first = total_ref[rows, :]
            norm = norm_ref[rows, :]
            d_mid = standardize_back(d_first * row_of(gain_ref), norm, inv_ref[rows, :])
            d_attn = d_mid.astype(BF16)
            d_mid_ref[rows, :] = d_mid
            d_attn_ref[rows, :] = d_attn
            d_ctx_ref[rows, :] = dot_nt(d_attn, w_out_ref[...]).astype(BF16)
            stats_ref[0:1, :] += column_sum(d_first * norm)
            stats_ref[1:2, :] += column_sum(d_first)
            stats_ref[2:3, :] += column_sum(d_attn.astype(F32))

        out_keep_ref[...] = dot_nn(ctx_turned_ref[:half, :], d_attn_ref[...]).astype(BF16)
        out_send_ref[...] = dot_nn(ctx_turned_ref[half:, :], d_attn_ref[...]).astype(BF16)


def feed_back(d_down, slope, w_down, w_up, d_second, norm, inv, gain, w_out, low_turned, ctx_turned):
    count, units = slope.shape
    chunk = 512
    return pl.pallas_call(
        feed_back_body,
        grid=(units // chunk,),
        in_specs=[
            whole((count, D)),
            pl.BlockSpec((count, chunk), lambda j: (0, j)),
            pl.BlockSpec((chunk, D), lambda j: (j, 0)),
            pl.BlockSpec((D, chunk), lambda j: (0, j)),
            whole((count, D)),
            whole((count, D)),
            whole((count, 1)),
            whole((D,)),
            whole((D, D)),
            whole((D, count)),
            whole((D, count)),
        ],
        out_specs=[
            pl.BlockSpec((D // 2, chunk), lambda j: (0, j)),
            pl.BlockSpec((D // 2, chunk), lambda j: (0, j)),
            whole((D // 2, D)),
            whole((D // 2, D)),
            pl.BlockSpec((1, chunk), lambda j: (0, j)),
            whole((count, D)),
            whole((count, D)),
            whole((8, D)),
        ],
        out_shape=(
            struct((D // 2, units), BF16),
            struct((D // 2, units), BF16),
            struct((D // 2, D), BF16),
            struct((D // 2, D), BF16),
            struct((1, units), F32),
            struct((count, D), F32),
            struct((count, D), BF16),
            struct((8, D), F32),
        ),
        scratch_shapes=[
            pltpu.VMEM((count, D), F32),
            pltpu.VMEM((count, chunk), BF16),
            pltpu.VMEM((count, D), BF16),
        ],
        cost_estimate=cost(6 * count * D * units + 4 * count * D * D, 4 * D * units + 4 * count * units),
        name="feed_back",
    )(d_down, slope, w_down, w_up, d_second, norm, inv, gain, w_out, low_turned, ctx_turned)


def region_back_body(
    back_ref,
    hot_ref,
    norm_ref,
    inv_ref,
    gain_ref,
    boxes_ref,
    qkv_ref,
    attn_ref,
    ffn_ref,
    up_ref,
    perm_ref,
    d_proj_ref,
    *piece_refs,
):
    rows = norm_ref.shape[0]
    d_region = dot_tn(hot_ref[...], back_ref[...])
    norm = norm_ref[...]
    d_pre = standardize_back(d_region * row_of(gain_ref), norm, inv_ref[...])
    d_proj = d_pre.astype(BF16)
    d_proj_ref[...] = d_proj
    boxes = jnp.concatenate([boxes_ref[...], jnp.zeros((4, rows), F32)], axis=0).T
    vectors = [column_sum(d_pre), column_sum(d_region * norm), column_sum(d_region)]
    vectors += [column_sum(boxes[:, side : side + 1] * d_pre) for side in range(4)]
    for part in (0, 2):
        starts = [(3 * pair + part) * PAIR for pair in range(PAIRS)]
        vectors.append(jnp.concatenate([qkv_ref[:, start : start + PAIR] for start in starts], axis=1))
    for ref in (attn_ref, ffn_ref):
        vectors += [ref[2:3, :], ref[0:2, :]]
    vectors.append(up_ref[...])
    filled = sum(vector.shape[0] for vector in vectors)
    vectors.append(jnp.zeros((VECS - filled, D), F32))
    low_vectors = jnp.concatenate(vectors, axis=0).astype(BF16)
    turned = dot_nt(perm_ref[...], jnp.concatenate([d_proj, low_vectors], axis=0)).astype(BF16)
    size = D // len(piece_refs)
    for index, piece_ref in enumerate(piece_refs):
        piece_ref[...] = turned[index * size : (index + 1) * size]


def region_back(back, hot, norm, *others):
    rows = norm.shape[0]
    return pl.pallas_call(
        region_back_body,
        out_shape=(struct((rows, D), BF16),) + (struct((D // 4, rows + VECS), BF16),) * 4,
        cost_estimate=cost(0, 0),
        name="region_back",
    )(back, hot, norm, *others)


def swap_cores(sent):
    return lax.ppermute(sent, "enc", [(0, 1), (1, 0)])


def swap_chips(sent, offset, peers):
    return lax.ppermute(sent, "dp", [(peer, peer ^ offset) for peer in range(peers)])


MASKS = (0, 1, 3, 2)


def reverse(value, width):
    result = value & 0
    for bit in range(width):
        result = result | (((value >> bit) & 1) << (width - 1 - bit))
    return result


def after(first, *others):
    if not others:
        return first
    return lax.optimization_barrier((first,) + others)[0]


def swap_cores(sent):
    return [lax.ppermute(array, "enc", [(0, 1), (1, 0)]) for array in sent]


def swap_chips(sent, mask, peers):
    return lax.ppermute(sent, "dp", [(peer, peer ^ mask) for peer in range(peers)])


def combine_body(plans, counts, *refs):
    refs, out_refs = refs[:counts], refs[counts:]
    for out_ref, (unit, segments) in zip(out_refs, plans):

        def add(start, size, segments=segments, out_ref=out_ref):
            for place, at, terms in segments:
                sums = [refs[index][pl.ds(start, size), left:right].astype(F32) for index, left, right in terms]
                value = functools.reduce(jnp.add, sums).astype(out_ref.dtype)
                out_ref[pl.ds(place + start, size), at : at + value.shape[1]] = value

        if unit % 32 or unit < 64:
            add(0, unit)
        else:

            @pl.loop(0, unit // 32)
            def _(step, add=add):
                add(pl.multiple_of(step * 32, 32), 32)


def segments_of(terms, columns):
    edges = set()
    for array, _, first in terms:
        edges |= {first, first + array.shape[1]}
    for left, right in columns:
        inside = sorted({left, right} | {edge for edge in edges if left < edge < right})
        yield from zip(inside, inside[1:])


def combine_plain(terms, start, stop, columns, dtype):
    sums = []
    for left, right in segments_of(terms, columns):
        blocks = [
            array[row + start : row + stop, left - first : right - first].astype(F32)
            for array, row, first in terms
            if first <= left and right <= first + array.shape[1]
        ]
        sums.append(functools.reduce(jnp.add, blocks))
    return jnp.concatenate(sums, axis=1).astype(dtype)


def combine(wanted, name):
    plans, operands, specs, shapes, known = [], [], [], [], {}
    for terms, start, stop, columns, dtype in wanted:
        unit = functools.reduce(math.gcd, [value for _, row, _ in terms for value in (row + start, row + stop)])
        if unit % 8:
            return [combine_plain(*each) for each in wanted]
        segments = []
        for place in range(0, stop - start, unit):
            at = 0
            for left, right in segments_of(terms, columns):
                sources = []
                for array, row, first in terms:
                    if first <= left and right <= first + array.shape[1]:
                        block = (row + start + place) // unit
                        key = (id(array), unit, block)
                        if key not in known:
                            known[key] = len(operands)
                            operands.append(array)
                            specs.append(pl.BlockSpec((unit, array.shape[1]), lambda j, block=block: (block, 0)))
                        sources.append((known[key], left - first, right - first))
                segments.append((place, at, sources))
                at += right - left
        plans.append((unit, segments))
        shapes.append(struct((stop - start, at), dtype))
    return pl.pallas_call(
        functools.partial(combine_body, plans, len(operands)),
        grid=(1,),
        in_specs=specs,
        out_specs=[pl.BlockSpec(shape.shape, lambda j: (0, 0)) for shape in shapes],
        out_shape=tuple(shapes),
        cost_estimate=cost(0, 0),
        name=name,
    )(*operands)


def side_by_side(*arrays):
    terms, first = [], 0
    for array in arrays:
        terms.append((array, 0, first))
        first += array.shape[1]
    return terms


class Pair:
    def __init__(self, terms, rows, middle, width, peers):
        self.terms, self.size, self.middle, self.width, self.peers = terms, rows // 4, middle, width, peers
        self.sides = [(0, middle)], [(middle, width)]

    def start(self):
        size, (first, second) = self.size, self.sides
        wanted = [(self.terms, size, 3 * size, first, BF16), (self.terms, 2 * size, 4 * size, second, BF16)]
        self.sent = list(combine(wanted, "pair_start"))
        return self.sent

    def ship(self):
        self.got = [swap_chips(sent, bit, self.peers) for sent, bit in zip(self.sent, (1, 2))]
        return self.got

    def hold(self, *behind):
        self.got = [after(array, *behind) for array in self.got]

    def turn(self):
        size, (first, second), (one, two) = self.size, self.sides, self.got
        wanted = [
            (self.terms + [(one, -2 * size, 0)], 3 * size, 4 * size, first, BF16),
            (self.terms + [(two, -size, self.middle)], size, 2 * size, second, BF16),
        ]
        self.sent = list(combine(wanted, "pair_turn"))
        return self.sent

    def finish(self):
        last = [swap_chips(sent, bit, self.peers) for sent, bit in zip(self.sent, (2, 1))]
        (one, two), middle = self.got, self.middle
        arrived = [(one, 0, 0), (two, self.size, middle), (last[0], 0, 0), (last[1], 0, middle)]
        return Scatter(self.terms + arrived, self.size, self.width, self.peers, 2, 2)


class Scatter:
    def __init__(self, terms, rows, width, peers, bit, fresh):
        self.terms, self.rows, self.width, self.peers, self.bit, self.fresh = terms, rows, width, peers, bit, fresh

    def cut(self, bits, *behind):
        self.bits = min(bits, self.peers.bit_length() - 1 - self.bit)
        self.rows >>= self.bits
        wanted = [
            (self.terms, offset * self.rows, (offset + 1) * self.rows, [(0, self.width)], BF16)
            for offset in range(1, 1 << self.bits)
        ]
        self.sent = [after(array, *behind) for array in combine(wanted, "cut")]
        return self.sent

    def ship(self):
        masks = [reverse(offset, self.bits) << self.bit for offset in range(1, 1 << self.bits)]
        got = [swap_chips(sent, mask, self.peers) for sent, mask in zip(self.sent, masks)]
        self.terms = self.terms + side_by_side_rows(got)
        self.bit += self.bits
        self.fresh = len(got)
        return got

    def hold(self, *behind):
        late = [(after(array, *behind), row, first) for array, row, first in self.terms[-self.fresh :]]
        self.terms = self.terms[: -self.fresh] + late

    def finish(self, bits):
        while 1 << self.bit < self.peers:
            self.cut(bits)
            self.ship()
        return self

    def shares(self, *ranges):
        return [(self.terms, 0, self.rows, columns, F32) for columns in ranges]


def side_by_side_rows(arrays):
    return [(array, 0, 0) for array in arrays]


def direct(terms, rows, width, peers, bit):
    size = rows // 4
    wanted = [(terms, place * size, (place + 1) * size, [(0, width)], BF16) for place in range(1, 4)]
    sent = combine(wanted, "direct")
    got = [swap_chips(array, mask, peers) for array, mask in zip(sent, MASKS[1:])]
    return sent, Scatter(terms + side_by_side_rows(got), size, width, peers, bit, 3)


def swap_near(pieces, peers):
    return [swap_chips(piece, offset << 2, peers) for offset, piece in enumerate(pieces[1:], 1)]


def place_of(block, peers):
    rest = peers // 4
    top = block // rest
    return (top ^ (top >> 1)) + (reverse(block % rest, rest.bit_length() - 1) << 2)


def units_body(order_ref, *refs):
    kept, got = refs[:-3:2], refs[1:-3:2]
    near_ref, far_ref, keep_ref = refs[-3:]
    step, half = pl.program_id(0), near_ref.shape[1]
    rows = [(one[...].astype(F32) + two[...].astype(F32)).astype(BF16) for one, two in zip(kept, got)]
    rows = jnp.concatenate(rows, axis=0)
    keep_ref[...] = rows

    @pl.when((step == 1) | (step == 2))
    def _():
        near_ref[...] = rows[:, :half]

    @pl.when(step >= 2)
    def _():
        far_ref[...] = rows[:, half:]


def cut_units(kept, got, order, peers):
    count, width = kept.shape
    size, half, rest = count // peers, width // 2, peers // 4
    if size % 16:
        rows = (kept.astype(F32) + got.astype(F32)).reshape(peers, size, width)
        rows = jnp.take(rows, order, axis=0).reshape(count, width).astype(BF16)
        return rows[count // 4 : 3 * count // 4, :half], rows[count // 2 :, half:], rows
    specs = []
    for index in range(rest):
        specs += [pl.BlockSpec((size, width), lambda j, order, index=index: (order[j * rest + index], 0))] * 2
    return pl.pallas_call(
        units_body,
        grid_spec=pltpu.PrefetchScalarGridSpec(
            num_scalar_prefetch=1,
            grid=(4,),
            in_specs=specs,
            out_specs=[
                pl.BlockSpec((count // 4, half), lambda j, order: (jnp.clip(j - 1, 0, 1), 0)),
                pl.BlockSpec((count // 4, half), lambda j, order: (jnp.clip(j - 2, 0, 1), 0)),
                pl.BlockSpec((count // 4, width), lambda j, order: (j, 0)),
            ],
        ),
        out_shape=(struct((count // 2, half), BF16), struct((count // 2, half), BF16), struct((count, width), BF16)),
        cost_estimate=cost(count * width, 8 * count * width),
        name="cut_units",
    )(order, *(kept, got) * rest)


def region_product_body(*refs):
    *refs, keep_ref, send_ref = refs
    pieces, feats = refs[: len(refs) // 2], refs[len(refs) // 2 :]
    rows, width = feats[0].shape
    half = keep_ref.shape[0]
    turned = jnp.concatenate([piece[:, :rows] for piece in pieces], axis=1)
    vectors = functools.reduce(jnp.add, [piece[:, rows:].astype(F32) for piece in pieces])
    product = dot_nn(turned, jnp.concatenate([ref[...] for ref in feats], axis=0)).astype(BF16)
    for ref, start in ((keep_ref, 0), (send_ref, half)):
        ref[:, :width] = product[start : start + half]
        ref[:, width:] = vectors[start : start + half].astype(BF16)


def region_product(pieces, feats):
    half, width = pieces[0].shape[0] // 2, feats[0].shape[1] + VECS
    return pl.pallas_call(
        region_product_body,
        out_shape=(struct((half, width), BF16), struct((half, width), BF16)),
        cost_estimate=cost(0, 0),
        name="region_product",
    )(*pieces, *feats)


def one_hot_rows(core, place, inner, peers):
    share = D // (2 * peers)
    core, place = core ^ lax.axis_index("enc"), place ^ lax.axis_index("dp")
    row = (core * peers + place) * share + inner
    return (lax.broadcasted_iota(jnp.int32, (D, D), 1) == row).astype(BF16)


def share_order(peers):
    share = D // (2 * peers)
    row = lax.broadcasted_iota(jnp.int32, (D, 1), 0)
    block = row // share
    return one_hot_rows(block // peers, place_of(block % peers, peers), row % share, peers)


def region_order(peers):
    share, rest = D // (2 * peers), peers // 16
    row = lax.broadcasted_iota(jnp.int32, (D, 1), 0)
    block = row // share
    top = (block // rest) % 4
    place = (top ^ (top >> 1)) + ((block // (8 * rest)) << 2) + (reverse(block % rest, rest.bit_length() - 1) << 4)
    return one_hot_rows((block // (4 * rest)) % 2, place, row % share, peers)


def exchange(array):
    return lax.all_to_all(array, "dp", split_axis=0, concat_axis=0, tiled=True)


def per_device(
    text_in,
    text_lengths,
    region_feats,
    region_boxes,
    region_dest,
    region_seq,
    w_region,
    w_box,
    type_embed,
    region_gain,
    region_shift,
    w_qkv,
    q_bias,
    v_bias,
    w_out,
    out_bias,
    attn_gain,
    attn_shift,
    w_up,
    up_bias,
    w_down,
    down_bias,
    ffn_gain,
    ffn_shift,
    cot_text,
    cot_region,
):
    peers = lax.axis_size("dp")
    source_rows = region_feats.shape[0]
    capacity = max(2, 2 * source_rows // peers)
    slots = peers * capacity
    text_count = text_in.shape[0]
    units = w_up.shape[1]

    def row(vector):
        return vector.reshape(1, -1)

    outgoing, cot_sent, hot, region_norm, region_inv = region_forward(
        capacity,
        slots,
        region_feats,
        w_region,
        region_boxes,
        row(region_dest),
        row(region_seq),
        w_box,
        type_embed,
        region_gain,
        region_shift,
        cot_region,
    )
    arrived = exchange(outgoing)
    arrived_cot = exchange(cot_sent)


    bias = jnp.concatenate([q_bias, jnp.zeros_like(q_bias), v_bias])[None]
    perm, region_perm = lax.optimization_barrier((share_order(peers), region_order(peers)))
    order = place_of(jnp.arange(peers, dtype=jnp.int32), peers) ^ lax.axis_index("dp")
    qkv_text = (dot_nn(text_in, w_qkv) + bias).astype(BF16)
    far_feats = swap_near([region_feats] + [after(region_feats, qkv_text)] * 3, peers)
    qkv_region = (dot_nn(arrived[:, :D], w_qkv) + bias).astype(BF16)
    context, chance, chance_inv = attend(text_lengths, arrived, qkv_text, qkv_region)
    vecs = (out_bias, attn_gain, attn_shift, down_bias, ffn_gain, ffn_shift)
    (
        hidden,
        slope,
        norm,
        inv,
        rows_turned,
        ctx_turned,
        low_turned,
        text_out,
        region_sent,
        d_second,
        d_down,
        ffn_stats,
    ) = feed_forward(context, w_out, text_in, arrived, perm, vecs, w_up, row(up_bias), w_down, cot_text, arrived_cot)

    d_down = after(d_down, *far_feats)
    core = lax.axis_index("enc")
    half = units // 2

    def unit_product(which):
        side = lax.dynamic_slice_in_dim(hidden, which * half, half, axis=1)
        return dot_tn(side, d_down).astype(BF16)

    (got,) = swap_cores([unit_product(1 - core)])
    *sent, kept = cut_units(unit_product(core), got, order, peers)
    down = Pair([(kept, 0, 0)], half, D // 2, D, peers)
    down.sent = sent
    covered = after(d_down, *sent)
    near = down.ship()
    up_keep, up_send, out_keep, out_send, up_grad, d_mid, d_ctx, attn_stats = feed_back(
        covered, slope, w_down, w_up, d_second, norm, inv, attn_gain, w_out, low_turned, ctx_turned
    )
    up_send, out_send = lax.optimization_barrier((up_send, out_send, *near))[:2]
    got = swap_cores([up_send, out_send])
    down.turn()
    down = down.finish()
    up_out = Pair(
        side_by_side(up_keep, out_keep) + side_by_side(*got), D // 2, (units + D) // 2, units + D, peers
    )
    sent = up_out.start()
    near = up_out.ship()
    returned = exchange(after(region_sent, *sent))
    down.hold(*sent)
    covered = after(d_ctx, *sent, *down.cut(2))
    far = down.ship()
    qkv_keep, qkv_send, qkv_sums, text_grad, d_rows_region = attend_back(
        qkv_text, qkv_region, w_qkv, chance, chance_inv, context, covered, d_mid, rows_turned
    )
    qkv_send = after(qkv_send, returned, *near, *far)
    (got,) = swap_cores([qkv_send])
    sent_back = exchange(after(d_rows_region, qkv_send))
    qkv = Pair([(qkv_keep, 0, 0), (got, 0, 0)], D // 2, 3 * D // 2, 3 * D, peers)
    sent = qkv.start()
    qkv_got = qkv.ship()
    up_out.hold(*sent)
    sent = up_out.turn()
    up_out = up_out.finish()
    sent_back = after(sent_back, *qkv_got)

    share = D // (2 * peers)
    quarter = units // D
    up_rows = after(up_grad, *sent).reshape(2 * peers, quarter, share).transpose(1, 0, 2).reshape(quarter, D)
    d_proj, *pieces = region_back(
        sent_back,
        hot,
        region_norm,
        region_inv,
        region_gain,
        region_boxes,
        qkv_sums,
        attn_stats,
        ffn_stats,
        up_rows,
        region_perm,
    )
    feats_width = region_feats.shape[1]
    up_out.hold(*pieces)
    qkv.hold(*pieces)
    region_got = swap_near(pieces, peers)
    qkv.turn()
    qkv = qkv.finish()
    qkv_got = [array for array, _, _ in qkv.terms[-qkv.fresh :]]
    sent = up_out.cut(1)
    up_out.ship()
    region_got = [after(array, *qkv_got, *sent) for array in region_got]
    last_keep, last_send = region_product(pieces[:1] + region_got, [region_feats] + far_feats)
    (got,) = swap_cores([last_send])
    qkv.hold(last_send)
    qkv.cut(1)
    qkv.ship()
    last_sent, last = direct(
        [(last_keep, 0, 0), (got, 0, 0)], last_keep.shape[0], feats_width + VECS, peers, 4
    )
    qkv.hold(*last_sent)
    up_out.hold(*last_sent)
    down.hold(*last_sent)
    sent = up_out.cut(1)
    up_out.ship()
    d_proj, returned = lax.optimization_barrier((d_proj, returned, *sent))[:2]
    region_out = dot_tn(hot, returned).astype(BF16)
    feats_grad = dot_nt(d_proj, w_region).astype(BF16)
    starts = [(3 * pair + part) * PAIR for part in range(3) for pair in range(PAIRS)]
    heads = [(start, start + PAIR) for start in starts]
    w_qkv_share, w_up_share, w_out_share, w_down_share = combine(
        qkv.finish(1).shares(heads)
        + up_out.finish(1).shares([(0, units)], [(units, units + D)])
        + down.finish(2).shares([(0, D)]),
        "shares",
    )
    w_region_share, vectors = combine(
        last.finish(2).shares([(0, feats_width)], [(feats_width, feats_width + VECS)]), "last_shares"
    )
    vectors = vectors.T
    return (
        text_out,
        region_out,
        text_grad,
        feats_grad,
        w_region_share.T,
        vectors[3:7],
        vectors[0],
        vectors[1],
        vectors[2],
        w_qkv_share,
        vectors[7],
        vectors[8],
        w_out_share,
        vectors[9],
        vectors[10],
        vectors[11],
        w_up_share,
        vectors[15 : 15 + quarter].reshape(-1),
        w_down_share,
        vectors[12],
        vectors[13],
        vectors[14],
    )


def solution(mesh):
    both = ("enc", "dp")
    rows, flat, none = P(both, None), P(both), P()
    in_specs = (rows, rows, rows, P(None, both), rows, flat) + (none,) * 18 + (rows, rows)
    out_specs = (
        (rows,) * 4
        + (P(None, both), P(None, both), flat, flat, flat, rows, flat, flat, rows)
        + (flat, flat, flat, rows, flat, rows, flat, flat, flat)
    )
    return jax.shard_map(per_device, mesh=mesh, in_specs=in_specs, out_specs=out_specs, check_vma=False)
```
